32 devices in a mesh: groups: 2 (over y), seq: 4 (over x, core), role: 4 (over z).
Axes of the slice: x: 2, y: 2, z: 4, core: 2. Of those that a mesh axis runs over, the one named last changes fastest.
Arguments:
- query_rows: bfloat16 [8, 256, 4096], P('groups', 'seq', 'role'), parts along dimension 0, may hold values from -6 to 6
- encoded_key_rows: bfloat16 [8, 256, 512], P('groups', ('seq', 'role')), parts along dimension 0, may hold values from -6 to 6
- value_matrix_rows: bfloat16 [8, 256, 512], P('groups', ('seq', 'role')), parts along dimension 0, may hold values from -6 to 6
- output_weight: bfloat16 [4096, 2048], P('role', 'seq'), may hold values from -0.09375 to 0.09375
- residual: bfloat16 [8, 256, 2048], P(('groups', 'role'), 'seq'), parts along dimension 0, may hold values from -7.5 to 7.5
- norm_gain: float32 [2048], replicated, may hold values from 0.5 to 1.5
- route_experts: int32 [8, 256, 8], P(('groups', 'role'), 'seq'), parts along dimension 0, may hold values from 0 to 15, all different within a row; in each aligned block of 64 rows (0 to 63, 64 to 127, ..., all dimensions but the last counted through in order) at most 33 rows name the same one
- route_gates: float32 [8, 256, 8], P(('groups', 'role'), 'seq'), parts along dimension 0, may hold values from 0.05 to 0.3
- gate_weight: bfloat16 [16, 2048, 768], P(('seq', 'role')), may hold values from -0.125 to 0.125
- up_weight: bfloat16 [16, 2048, 768], P(('seq', 'role')), may hold values from -0.125 to 0.125
- down_weight: bfloat16 [16, 768, 2048], P(('seq', 'role')), may hold values from -0.21875 to 0.21875
Outputs:
- layer_output: bfloat16 [8, 256, 2048], P(('groups', 'role'), 'seq'), parts along dimension 0
The draws below stay inside these ranges and needn't reach their ends.
There are 2 independent parts, one for each index of `groups`. The reference program is written for one: setup_inputs(seed, part) draws one part's arguments, and reference() takes and returns one part's arrays. A program takes and returns all parts, laid end to end along the dimension named above; an argument that names none is the same for every part. Nothing has to cross between parts.
Inputs may be any that keep to these rules, and one draw needn't show every extreme that they name: `route_experts`: each token names 8 different experts. Within the 64 positions of one sequence that one index of seq holds, no expert is named by more than 33 routes, and in every draw some expert is named by exactly 33 routes in some such block.
All inputs are finite; a program needn't handle non-finite values.
Results may differ from the reference program's by a relative error of at most 0.014.
Values may be sent and summed in bfloat16 or wider, within the bound.
A program may use at most 128 MiB of HBM per device.

```python
import math
import jax
import jax.numpy as jnp
import numpy as np
from jax import lax

D = 2048
FF = 768
QUERY_HEADS = 32
KEY_VALUE_HEADS = 4
HEAD_WIDTH = 128
TOPK = 8
SEQ_TOK = 64
EXPERTS = 16
SEQUENCE_LENGTH = 256
BATCH_SEQUENCES = 4
HPD = 8
CAP = 33
N_SEQ = 4
N_ROLE = 4


def draw_query_rows(key, part):
    value_entries = jnp.clip(1.5 * jax.random.normal(jax.random.fold_in(key, 11), (BATCH_SEQUENCES, SEQUENCE_LENGTH, QUERY_HEADS * HEAD_WIDTH), jnp.float32), -6.0, 6.0)
    return value_entries.astype(jnp.bfloat16)


def draw_encoded_key_rows(key, part):
    value_entries = jnp.clip(1.5 * jax.random.normal(jax.random.fold_in(key, 12), (BATCH_SEQUENCES, SEQUENCE_LENGTH, KEY_VALUE_HEADS * HEAD_WIDTH), jnp.float32), -6.0, 6.0)
    return value_entries.astype(jnp.bfloat16)


def draw_residual(key, part):
    random_splits = jax.random.split(jax.random.fold_in(key, 13), 3)
    row_scale = jnp.exp(jax.random.uniform(random_splits[1], (BATCH_SEQUENCES, SEQUENCE_LENGTH, 1), jnp.float32, math.log(0.25), math.log(2.5)))
    column_scale = jnp.exp(jax.random.uniform(random_splits[0], (D,), jnp.float32, math.log(0.1), 0.0))
    noise_rows = jnp.clip(jax.random.normal(random_splits[2], (BATCH_SEQUENCES, SEQUENCE_LENGTH, D), jnp.float32), -3.0, 3.0)
    return (noise_rows * column_scale * row_scale).astype(jnp.bfloat16)


def block_scale(stream_key, dims, pieces, least, largest):
    gain, own = 1.0, jax.random.fold_in(stream_key, 6)
    for axis_at, shards_of in pieces:
        draws = jnp.exp(jax.random.uniform(jax.random.fold_in(own, axis_at), (shards_of,), jnp.float32, least / len(pieces), largest / len(pieces)))
        gain = gain * jnp.repeat(draws, dims[axis_at] // shards_of).reshape([-1 if axis == axis_at else 1 for axis in range(len(dims))])
    return gain


def shared_out(key, own, number, rows, amount, top, most, skew):
    sequence = jax.random.permutation(key, amount)
    packed, usual = load_shares(amount, rows * top, most, skew, True), load_shares(amount, rows * top, most, skew, False)
    places = jnp.arange(amount)

    def named(sizes, turn):
        used = int((sizes > 0).sum())
        fixed = max(1, used // 4)
        shifted = fixed + (places - fixed + turn * (used - fixed)) % max(1, amount - fixed)
        return jnp.zeros((amount,), jnp.int32).at[sequence[jnp.where(places < fixed, places, shifted)]].set(jnp.asarray(sizes, jnp.int32))

    sizes = jnp.where(number % 4 == 0, named(packed, number // 4), named(usual, number - number // 4 - 1))
    mixed = jax.random.permutation(jax.random.fold_in(own, 3), amount)
    source_of, receiver = mixed[0:amount // 2 * 2:2], mixed[1:amount // 2 * 2:2]
    room = jnp.minimum(sizes[source_of] - 1, most - sizes[receiver]) // 2
    room = jnp.where((source_of == sequence[0]) | (receiver == sequence[0]) | (sizes[receiver] == 0), 0, jnp.maximum(room, 0))
    shifted = jax.random.randint(jax.random.fold_in(own, 4), (amount // 2,), 0, 1 << 20) % (room + 1)
    sizes = sizes.at[source_of].add(-shifted).at[receiver].add(shifted)
    members = jnp.searchsorted(jnp.cumsum(sizes), jnp.arange(rows * top), side="right").astype(jnp.int32)
    grid = members.reshape(top, rows).T
    grid = grid[jax.random.permutation(jax.random.fold_in(own, 1), rows)]
    turn = jax.random.randint(jax.random.fold_in(own, 2), (rows, 1), 0, top)
    return jnp.take_along_axis(grid, (jnp.arange(top)[None, :] + turn) % top, axis=1)


def load_shares(amount, total, bound, slope, full):
    weights = [(1 << 20) // math.isqrt(grade ** slope) + 1 for grade in range(1, amount + 1)]
    largest = bound if full else min(bound, max(-(-total // amount), total * weights[0] // sum(weights)))
    least = 1 if total - largest >= amount - 1 else 0
    holding, surplus = [largest] + [least] * (amount - 1), total - largest - least * (amount - 1)
    while surplus > 0:
        movable = [i for i in range(1, amount) if holding[i] < largest] or [i for i in range(1, amount) if holding[i] < bound]
        whole, left = sum([weights[i] for i in movable]), surplus
        for i in movable:
            addition = min(bound - holding[i], max(1, left * weights[i] // whole), surplus)
            holding[i] = holding[i] + addition
            surplus = surplus - addition
    return np.array(holding)


def normal_values(rng, dims, deviation, bound, cuts=(), kind=jnp.bfloat16):
    loudness = block_scale(rng, dims, cuts, -0.22, 0.18) if cuts else 1.0
    drawn = jax.random.normal(rng, dims, jnp.float32) * deviation * loudness
    return jnp.minimum(jnp.maximum(drawn, -bound), bound).astype(kind)


def setup_inputs(seed: int = 0, part: int = 0) -> dict:
    key_of = jax.random.split(jax.random.key(seed), 12)
    part_keys = jax.random.split(jax.random.fold_in(key_of[11], part), 12)
    query_rows = draw_query_rows(jax.random.fold_in(jax.random.fold_in(key_of[11], part), 71), part)
    encoded_key_rows = draw_encoded_key_rows(jax.random.fold_in(jax.random.fold_in(key_of[11], part), 71), part)
    value_matrix_rows = normal_values(part_keys[2], (BATCH_SEQUENCES, SEQUENCE_LENGTH, KEY_VALUE_HEADS * HEAD_WIDTH), 1.0, 6.0, ((1, 16),))
    output_weight = normal_values(key_of[3], (QUERY_HEADS * HEAD_WIDTH, D), (QUERY_HEADS * HEAD_WIDTH) ** -0.5, 0.09375, ((0, 4), (1, 4)))
    residual = draw_residual(jax.random.fold_in(jax.random.fold_in(key_of[11], part), 71), part)
    norm_gain = jnp.clip(1.0 + 0.1 * jax.random.normal(key_of[5], (D,), jnp.float32), 0.5, 1.5)
    route_experts_keys = jax.random.split(jax.random.fold_in(part_keys[6], 1), BATCH_SEQUENCES * SEQUENCE_LENGTH // SEQ_TOK)
    route_experts_turns = jax.random.permutation(jax.random.fold_in(part_keys[6], 3), BATCH_SEQUENCES * SEQUENCE_LENGTH // SEQ_TOK)
    route_experts = jax.vmap(lambda own, number: shared_out(jax.random.fold_in(part_keys[6], 2), own, number, SEQ_TOK, EXPERTS, TOPK, CAP, 1))(route_experts_keys, route_experts_turns).reshape((BATCH_SEQUENCES, SEQUENCE_LENGTH, TOPK))
    route_gates = jnp.clip(0.05 + 0.25 * jax.random.uniform(part_keys[7], (BATCH_SEQUENCES, SEQUENCE_LENGTH, TOPK), jnp.float32) ** block_scale(part_keys[7], (BATCH_SEQUENCES, SEQUENCE_LENGTH, TOPK), ((0, 4), (1, 4)), -0.2, 0.2), 0.05, 0.3)
    gate_weight = normal_values(key_of[8], (EXPERTS, D, FF), D ** -0.5, 0.125, ((0, 16),))
    up_weight = normal_values(key_of[9], (EXPERTS, D, FF), D ** -0.5, 0.125, ((0, 16),))
    down_weight = normal_values(key_of[10], (EXPERTS, FF, D), FF ** -0.5, 0.21875, ((0, 16),))
    return dict(query_rows=query_rows, encoded_key_rows=encoded_key_rows, value_matrix_rows=value_matrix_rows, output_weight=output_weight, residual=residual, norm_gain=norm_gain, route_experts=route_experts, route_gates=route_gates, gate_weight=gate_weight, up_weight=up_weight, down_weight=down_weight)


epsilon = 1e-06
masked_score = -1e+30

def attend_head(query_head, key_head, value_head):
    length = query_head.shape[0]
    scores = jnp.dot(query_head.astype(jnp.float32), key_head.astype(jnp.float32).T, precision=lax.Precision.HIGHEST) * HEAD_WIDTH ** (-0.5)
    positions = jnp.arange(length, dtype=jnp.int32)
    causal = positions[None, :] <= positions[:, None]
    scores = jnp.where(causal, scores, masked_score)
    row_peak = lax.optimization_barrier(jnp.max(scores, axis=1, keepdims=True))
    weights = jnp.exp(scores - row_peak)
    totals = lax.optimization_barrier(jnp.sum(weights, axis=1, keepdims=True))
    rounded = weights.astype(jnp.bfloat16)
    mixed_rows = jnp.dot(rounded.astype(jnp.float32), value_head.astype(jnp.float32), precision=lax.Precision.HIGHEST) / totals
    return mixed_rows.astype(jnp.bfloat16)

def reference(query_rows, encoded_key_rows, value_matrix_rows, output_weight, residual, norm_gain, route_experts, route_gates, gate_weight, up_weight, down_weight):
    query_group_width = QUERY_HEADS // KEY_VALUE_HEADS
    heads_query = query_rows.reshape(BATCH_SEQUENCES, SEQUENCE_LENGTH, QUERY_HEADS, HEAD_WIDTH)
    key_per_head = encoded_key_rows.reshape(BATCH_SEQUENCES, SEQUENCE_LENGTH, KEY_VALUE_HEADS, HEAD_WIDTH)
    value_per_head = value_matrix_rows.reshape(BATCH_SEQUENCES, SEQUENCE_LENGTH, KEY_VALUE_HEADS, HEAD_WIDTH)

    def one_pair(pair_index):
        batch_index = pair_index // QUERY_HEADS
        head_index = pair_index % QUERY_HEADS
        kv_index = head_index // query_group_width
        return attend_head(heads_query[batch_index, :, head_index], key_per_head[batch_index, :, kv_index], value_per_head[batch_index, :, kv_index])
    attended = lax.map(one_pair, jnp.arange(BATCH_SEQUENCES * QUERY_HEADS, dtype=jnp.int32))
    attended = attended.reshape(BATCH_SEQUENCES, QUERY_HEADS, SEQUENCE_LENGTH, HEAD_WIDTH).transpose(0, 2, 1, 3).reshape(BATCH_SEQUENCES, SEQUENCE_LENGTH, QUERY_HEADS * HEAD_WIDTH)
    grouped_weight = output_weight.astype(jnp.float32).reshape(N_ROLE, HPD * HEAD_WIDTH, D)

    def project(sequence_rows):
        split_rows = sequence_rows.astype(jnp.float32).reshape(SEQUENCE_LENGTH, N_ROLE, HPD * HEAD_WIDTH)
        partials = jnp.einsum('lgk,gkd->lgd', split_rows, grouped_weight, precision=lax.Precision.HIGHEST)
        partials = lax.optimization_barrier(partials.astype(jnp.bfloat16))
        return lax.optimization_barrier(jnp.sum(partials.astype(jnp.float32), axis=1))
    projected = lax.map(project, attended)
    hidden = residual.astype(jnp.float32) + projected
    variance = lax.optimization_barrier(jnp.mean(hidden * hidden, axis=-1, keepdims=True))
    normed = (hidden * lax.rsqrt(variance + epsilon) * norm_gain).astype(jnp.bfloat16)
    tokens = BATCH_SEQUENCES * SEQUENCE_LENGTH
    flat_inputs = normed.reshape(tokens, D)
    flat_ids = route_experts.reshape(tokens * TOPK)
    flat_gates = route_gates.reshape(tokens * TOPK)
    most_rows = CAP * N_SEQ * N_ROLE

    def one_expert(running, inputs):
        gate_matrix, up_matrix, down_matrix, expert = inputs
        chosen = flat_ids == expert
        picked = jnp.nonzero(chosen, size=most_rows, fill_value=0)[0]
        listed = jnp.sum(chosen.astype(jnp.int32))
        valid = jnp.arange(most_rows, dtype=jnp.int32) < listed
        token_index = picked // TOPK
        row_block = flat_inputs[token_index].astype(jnp.float32)
        gate_hidden = jnp.dot(row_block, gate_matrix.astype(jnp.float32), precision=lax.Precision.HIGHEST)
        up_hidden = jnp.dot(row_block, up_matrix.astype(jnp.float32), precision=lax.Precision.HIGHEST)
        activated = (jax.nn.silu(gate_hidden) * up_hidden).astype(jnp.bfloat16)
        expert_out = jnp.dot(activated.astype(jnp.float32), down_matrix.astype(jnp.float32), precision=lax.Precision.HIGHEST)
        expert_out = lax.optimization_barrier(expert_out.astype(jnp.bfloat16))
        weight = jnp.where(valid, flat_gates[picked], 0.0)
        running = running.at[token_index].add(weight[:, None] * expert_out.astype(jnp.float32))
        return (running, None)
    start_sum = jnp.zeros((tokens, D), jnp.float32)
    expert_sum, unused = lax.scan(one_expert, start_sum, (gate_weight, up_weight, down_weight, jnp.arange(EXPERTS, dtype=jnp.int32)))
    return (hidden + expert_sum.reshape(BATCH_SEQUENCES, SEQUENCE_LENGTH, D)).astype(jnp.bfloat16)
```

```python
from functools import partial

import jax
import jax.numpy as jnp
from jax import lax
from jax.experimental import pallas as pl
from jax.experimental.pallas import tpu as pltpu
from jax.sharding import PartitionSpec as P

D = 2048
QUERY_HEADS = 32
KEY_VALUE_HEADS = 4
HEAD_WIDTH = 128
TOPK = 8


epsilon = 1e-06
masked_score = -1e30


def score_block(queries, every_key, query_position, block_start, block_width, score_scale):
    keys_part = lax.slice_in_dim(every_key, block_start, block_start + block_width, axis=0)
    raw_scores = (
        jnp.einsum("qhd,kd->hqk", queries, keys_part, preferred_element_type=jnp.float32)
        * score_scale
    )
    key_position = block_start + jnp.arange(block_width, dtype=jnp.int32)
    return jnp.where(
        key_position[None, None, :] <= query_position[None, :, None], raw_scores, masked_score
    )


def value_block(rounded, every_value, block_start, block_width):
    prob_block = lax.slice_in_dim(rounded, block_start, block_start + block_width, axis=2)
    values_part = lax.slice_in_dim(every_value, block_start, block_start + block_width, axis=0)
    return jnp.einsum("hqk,kd->qhd", prob_block, values_part, preferred_element_type=jnp.float32)


def shards(
    query_rows,
    encoded_key_rows,
    value_matrix_rows,
    output_weight,
    residual,
    norm_gain,
    route_experts,
    route_gates,
    gate_weight,
    up_weight,
    down_weight,
):
    seq_count = lax.axis_size("seq")
    role_count = lax.axis_size("role")
    seq_index = lax.axis_index("seq")
    role_index = lax.axis_index("role")
    batch_count = query_rows.shape[0]
    local_length = query_rows.shape[1]
    local_heads = query_rows.shape[2] // HEAD_WIDTH
    full_length = local_length * seq_count
    query_group_width = QUERY_HEADS // KEY_VALUE_HEADS
    head_pick = role_index * local_heads // query_group_width
    role_keys, role_values = (
        lax.all_gather(encoded_key_rows, "role", axis=1, tiled=True),
        lax.all_gather(value_matrix_rows, "role", axis=1, tiled=True),
    )
    head_keys = lax.dynamic_slice_in_dim(role_keys, head_pick * HEAD_WIDTH, HEAD_WIDTH, 2)
    head_values = lax.dynamic_slice_in_dim(role_values, head_pick * HEAD_WIDTH, HEAD_WIDTH, 2)
    whole_keys, whole_values, whole_proj = (
        lax.all_gather(head_keys, "seq", axis=1, tiled=True),
        lax.all_gather(head_values, "seq", axis=1, tiled=True),
        lax.all_gather(output_weight, "seq", axis=1, tiled=True),
    )
    key_width = full_length // 8
    score_scale = HEAD_WIDTH ** (-0.5)
    query_position = seq_index * local_length + jnp.arange(local_length, dtype=jnp.int32)
    last_needed = (seq_index + 1) * local_length

    def one_sequence(operands):
        own_queries, every_key, every_value = operands
        queries = own_queries.reshape(local_length, local_heads, HEAD_WIDTH)
        pieces = []
        for number in range(8):
            block_start = number * key_width
            compute = partial(
                score_block, queries, every_key, query_position, block_start, key_width, score_scale
            )
            skipped = partial(
                jnp.full, (local_heads, local_length, key_width), masked_score, jnp.float32
            )
            pieces.append(lax.cond(block_start < last_needed, compute, skipped))
        scores = jnp.concatenate(pieces, axis=2)
        row_peak = jnp.max(scores, axis=2, keepdims=True)
        weights = jnp.exp(scores - row_peak)
        totals = jnp.sum(weights, axis=2, keepdims=True)
        rounded = weights.astype(jnp.bfloat16)
        mixed_rows = jnp.zeros((local_length, local_heads, HEAD_WIDTH), jnp.float32)
        for number in range(8):
            block_start = number * key_width
            product = partial(value_block, rounded, every_value, block_start, key_width)
            nothing = partial(jnp.zeros, (local_length, local_heads, HEAD_WIDTH), jnp.float32)
            mixed_rows = mixed_rows + lax.cond(block_start < last_needed, product, nothing)
        attended = (mixed_rows / totals.transpose(1, 0, 2)).astype(jnp.bfloat16)
        return attended.reshape(local_length, local_heads * HEAD_WIDTH)

    attended = lax.map(one_sequence, (query_rows, whole_keys, whole_values))
    flat_attended = attended.reshape(batch_count * local_length, local_heads * HEAD_WIDTH)
    projected = lax.psum_scatter(
        jnp.dot(flat_attended, whole_proj, preferred_element_type=jnp.float32).astype(jnp.bfloat16),
        "role",
        scatter_dimension=0,
        tiled=True,
    ).astype(jnp.float32)
    hidden = residual[0].astype(jnp.float32) + projected
    variance = jnp.mean(hidden * hidden, axis=-1, keepdims=True)
    normed = (hidden * lax.rsqrt(variance + epsilon) * norm_gain).astype(jnp.bfloat16)
    expert_ids = route_experts.reshape(-1)
    gate_values = route_gates.reshape(-1)
    experts_local = gate_weight.shape[0]
    device_count = seq_count * role_count
    expert_count = experts_local * device_count
    assign = expert_ids.shape[0]
    capacity = assign // expert_count + 1
    onehot = (expert_ids[:, None] == jnp.arange(expert_count, dtype=jnp.int32)[None, :]).astype(
        jnp.int32
    )
    before = jnp.tri(assign, k=-1, dtype=jnp.bfloat16)
    earlier = jnp.dot(
        before, onehot.astype(jnp.bfloat16), preferred_element_type=jnp.float32
    ).astype(jnp.int32)
    slot_rank = jnp.sum(earlier * onehot, axis=1)
    slot_index = expert_ids * capacity + slot_rank
    source_token = jnp.arange(assign, dtype=jnp.int32) // TOPK
    slot_token = jnp.zeros((expert_count * capacity,), jnp.int32).at[slot_index].set(source_token)
    slot_used = jnp.zeros((expert_count * capacity,), jnp.bfloat16).at[slot_index].set(1.0)
    outgoing = (normed[slot_token] * slot_used[:, None]).reshape(
        device_count, experts_local, capacity, D
    )
    incoming = lax.all_to_all(outgoing, ("seq", "role"), split_axis=0, concat_axis=0, tiled=True)
    gate_hidden = jnp.einsum(
        "sjcd,jdf->sjcf", incoming, gate_weight, preferred_element_type=jnp.float32
    )
    up_hidden = jnp.einsum(
        "sjcd,jdf->sjcf", incoming, up_weight, preferred_element_type=jnp.float32
    )
    activated = (jax.nn.silu(gate_hidden) * up_hidden).astype(jnp.bfloat16)
    returned = lax.all_to_all(
        jnp.einsum(
            "sjcf,jfd->sjcd", activated, down_weight, preferred_element_type=jnp.float32
        ).astype(jnp.bfloat16),
        ("seq", "role"),
        split_axis=0,
        concat_axis=0,
        tiled=True,
    )
    gathered = returned.reshape(expert_count * capacity, D)[slot_index]
    weighted = gathered.astype(jnp.float32) * gate_values[:, None]
    expert_sum = jnp.sum(weighted.reshape(-1, TOPK, D), axis=1)
    return (hidden + expert_sum).astype(jnp.bfloat16).reshape(residual.shape)


MESH = pl.DeviceIdType.MESH
LANES = 128
LAGS = (3, 3)


def aligned(index, size):
    return pl.ds(pl.multiple_of(index * size, size), size)


SCALE_LANE = 32


def layer_kernel(
    roles,
    seqs,
    q_hbm,
    k_hbm,
    v_hbm,
    wo_hbm,
    res_hbm,
    gain_hbm,
    ids_hbm,
    gates_hbm,
    gw_hbm,
    uw_hbm,
    dw_hbm,
    out_ref,
    q,
    kv,
    wo,
    res,
    gain,
    ids,
    gates,
    gw,
    uw,
    dw,
    att,
    gains,
    base,
    part,
    from_end,
    from_mid,
    tok,
    tab,
    act,
    y,
    y_core,
    y_x,
    y_line,
    final,
    load_sem,
    own_sem,
    kv1_s,
    kv1_r,
    kv2_s,
    kv2_r,
    wm_s,
    wm_r,
    wx_s,
    wx_r,
    wy_s,
    wy_r,
    tb_s,
    tb_r,
    em_s,
    em_r,
    mm_s,
    mm_r,
    me_s,
    me_r,
    tx_s,
    tx_r,
    tc_s,
    tc_r,
    yc_s,
    yc_r,
    yx_s,
    yx_r,
    yz_s,
    yz_r,
):
    s = lax.axis_index("seq")
    r = lax.axis_index("role")
    g = lax.axis_index("groups")
    mate = s + 1 - 2 * (s % 2)
    side = (s + 2) % 4
    far = mate + 2 - 4 * (mate // 2)
    batch, rows, width = q.shape
    heads = width // HEAD_WIDTH
    own_keys = k_hbm.shape[1]
    full = rows * seqs
    cols = wo.shape[2]
    depth = cols * seqs
    offs = (1, 2, 3)
    chunks = 4
    chunk_rows = width // (2 * chunks)
    middle = (r + 1) // 2 % 2
    inner = r + 1 - 2 * (r // 2)
    outer = r - 1 + 2 * (r // 2)
    other = 3 - r

    def role_of(i):
        return (r // 2 + i // 2) % 2 * 2 + (r + i) % 2

    def turn(i):
        return (1 - i // 2) * 3 * i + i // 2 * (i - 1)

    def column(n):
        return (s // 2 + n // 2) % 2 * 2 + (s + n) % 2

    def remote(src, dst, ssem, rsem, device):
        return pltpu.make_async_remote_copy(
            src_ref=src,
            dst_ref=dst,
            send_sem=ssem,
            recv_sem=rsem,
            device_id=device,
            device_id_type=MESH,
        )

    def to_role(off):
        return {"role": role_of(off)}

    barrier = pltpu.get_barrier_semaphore()
    for off in offs:
        pl.semaphore_signal(barrier, inc=1, device_id=to_role(off), device_id_type=MESH)
    for peer in ({"seq": mate}, {"seq": side}, {"groups": 1 - g}):
        pl.semaphore_signal(barrier, inc=1, device_id=peer, device_id_type=MESH)

    loads = [
        pltpu.make_async_copy(a, b, load_sem.at[i])
        for i, (a, b) in enumerate(
            (
                (q_hbm, q),
                (res_hbm, res),
                (gain_hbm, gain),
                (ids_hbm, ids),
                (gates_hbm, gates),
                (wo_hbm, wo.at[s]),
                (gw_hbm, gw),
                (uw_hbm, uw),
                (dw_hbm, dw),
            )
        )
    ]
    pair = (k_hbm, v_hbm)

    def kv_spot(t, seq, role):
        return kv.at[t, :, aligned(seq * roles + role, own_keys), :]

    owns = [
        pltpu.make_async_copy(
            pair[t].at[:, :, aligned(r, HEAD_WIDTH)], kv_spot(t, s, r), own_sem.at[t]
        )
        for t in range(2)
    ]
    for copy in owns + loads[:6]:
        copy.start()

    for copy in loads[1:5]:
        copy.wait()
    half_lanes = LANES // 2
    place = lax.broadcasted_iota(jnp.int32, (LANES, rows), 0)
    table = jnp.zeros((LANES, rows), jnp.float32)
    for k in range(ids.shape[1]):
        chosen = place % half_lanes == ids[0, k : k + 1, :]
        table = table + jnp.where(chosen, gates[0, k : k + 1, :], 0.0)
    high = table.astype(jnp.bfloat16).astype(jnp.float32)
    parts = jnp.where(place < half_lanes, high, table - high).astype(jnp.bfloat16)
    unit = (
        lax.broadcasted_iota(jnp.int32, (rows, rows), 0)
        == lax.broadcasted_iota(jnp.int32, (rows, rows), 1)
    )
    tab[r, aligned(s, rows), :] = lax.dot_general(
        jnp.where(unit, 1.0, 0.0).astype(jnp.bfloat16),
        parts,
        (((1,), (1,)), ((), ())),
        preferred_element_type=jnp.float32,
    ).astype(jnp.bfloat16)
    base[...] = jnp.zeros_like(base)
    for j in range(seqs):
        block = pl.ds(j * cols, cols)
        gains[0, j] = gain[:, block]
        gains[1, j] = 1.0 / gain[:, block]
        base[j, aligned(r, rows), :] = res[0, :, block]

    pl.semaphore_wait(barrier, roles - 1 + 3)

    def kv1(t, off):
        return remote(
            pair[t].at[:, :, aligned(role_of(off), HEAD_WIDTH)],
            kv_spot(t, s, r),
            kv1_s.at[t, off],
            kv1_r.at[t, off],
            to_role(off),
        )

    def kv1_in(t, off):
        source = role_of(off)
        return remote(
            pair[t].at[:, :, aligned(r, HEAD_WIDTH)],
            kv_spot(t, s, source),
            kv1_s.at[t, off],
            kv1_r.at[t, off],
            to_role(off),
        )

    def tb(off):
        spot = tab.at[r, aligned(s, rows), :]
        return remote(spot, spot, tb_s.at[off], tb_r.at[off], to_role(off))

    def tb_in(off):
        spot = tab.at[role_of(off), aligned(s, rows), :]
        return remote(spot, spot, tb_s.at[off], tb_r.at[off], to_role(off))

    for off in offs:
        for t in range(2):
            kv1(t, off).start()

    def kv2(t, path, seq, target):
        spot = kv.at[t, :, aligned(seq, rows), :]
        return remote(spot, spot, kv2_s.at[t, path], kv2_r.at[t, path], {"seq": target})

    def wo_part(seq, n):
        return wo.at[seq, aligned(n, chunk_rows), :]

    def wo_own(seq):
        return remote(wo.at[seq], wo.at[seq], wm_s.at[0], wm_r.at[0], {"seq": mate})

    def wo_x(seq, c):
        spot = wo_part(seq, g * chunks + c)
        return remote(spot, spot, wx_s.at[c], wx_r.at[c], {"seq": side})

    def wo_y(half, c):
        spot = wo_part(side, half * chunks + c)
        return remote(spot, spot, wy_s.at[c], wy_r.at[c], {"groups": 1 - g})

    def wo_mate(seq, half, c, path):
        spot = wo_part(seq, half * chunks + c)
        sem = 1 + path * chunks + c
        return remote(spot, spot, wm_s.at[sem], wm_r.at[sem], {"seq": mate})

    def wo_pass(c):
        wo_x(side, c).wait_recv()
        wo_y(g, c).start()
        wo_mate(side, g, c, 0).start()

    def wo_turn(c):
        wo_y(1 - g, c).wait_recv()
        wo_mate(side, 1 - g, c, 1).start()

    loads[5].wait()
    wo_x(s, 0).start()
    wo_own(s).start()
    for off in offs:
        tb(off).start()
    for copy in loads[6:]:
        copy.start()
    for copy in owns:
        copy.wait()
    for off in offs:
        for t in range(2):
            kv1_in(t, off).wait_recv()
    for t in range(2):
        kv2(t, 1, s, side).start()
        kv2(t, 0, s, mate).start()
    for c in range(1, chunks):
        wo_x(s, c).start()
    loads[0].wait()
    wo_pass(0)
    for t in range(2):
        kv2(t, 1, side, side).wait_recv()
        kv2(t, 2, side, mate).start()
    for t in range(2):
        kv2(t, 0, mate, mate).wait_recv()
        kv2(t, 2, far, mate).wait_recv()

    half_steps = 2 * roles
    steps = 2 * half_steps

    def spot_of(k):
        late = k // half_steps
        m = k % half_steps
        early_col, early_turn = m // roles, m % roles
        late_col, late_turn = 2 + m % 2, m // 2
        n = (1 - late) * early_col + late * late_col
        return column(n), turn((1 - late) * early_turn + late * late_turn)

    def part_of(k):
        j, b = spot_of(k)
        return part.at[j, aligned(b, rows), :]

    def em(k):
        j, b = spot_of(k)
        return remote(part_of(k), from_end.at[j, b], em_s.at[k], em_r.at[k], {"role": inner})

    def em_in(k):
        j, b = spot_of(k)
        return remote(part_of(k), from_end.at[j, b], em_s.at[k], em_r.at[k], {"role": outer})

    def mm(k):
        j, b = spot_of(k)
        return remote(part_of(k), from_mid.at[j, b], mm_s.at[k], mm_r.at[k], {"role": other})

    def piece(j, b, seq):
        return tok.at[b, j, aligned(seq, rows), :]

    def me(k):
        j, b = spot_of(k)
        return remote(piece(j, b, s), piece(j, b, s), me_s.at[k], me_r.at[k], {"role": outer})

    def me_in(k):
        j, b = spot_of(k)
        return remote(piece(j, b, s), piece(j, b, s), me_s.at[k], me_r.at[k], {"role": inner})

    def table_of(b, seq):
        return tab.at[b, aligned(seq, rows), :]

    def tx(j, b, seq):
        return remote(
            piece(j, b, seq), piece(j, b, seq), tx_s.at[j, b], tx_r.at[j, b], {"seq": side}
        )

    def tx_table(b, seq):
        spot = table_of(b, seq)
        return remote(spot, spot, tx_s.at[seqs, b], tx_r.at[seqs, b], {"seq": side})

    def tc(j, b, path, seq):
        spot = piece(j, b, seq)
        return remote(spot, spot, tc_s.at[path, j, b], tc_r.at[path, j, b], {"seq": mate})

    def tc_table(b, path, seq):
        spot = table_of(b, seq)
        return remote(
            spot, spot, tc_s.at[path, seqs, b], tc_r.at[path, seqs, b], {"seq": mate}
        )

    def when(condition, body):
        if isinstance(condition, bool):
            if condition:
                body()
        else:
            pl.when(condition)(body)

    def is_last(k):
        if isinstance(k, int):
            return k >= half_steps and k % 2 == 1
        return jnp.logical_and(k >= half_steps, k % 2 == 1)

    lane = lax.broadcasted_iota(jnp.int32, (rows, LANES), 1)

    def spread(k):
        j, b = spot_of(k)
        tx(j, b, s).start()
        tc(j, b, 0, s).start()

        def with_table():
            square = jnp.zeros((rows, 1), jnp.float32)
            for c in range(seqs):
                value = tok[b, c, aligned(s, rows), :].astype(jnp.float32) * gains[1, c]
                square = square + jnp.sum(value * value, axis=1, keepdims=True)
            scale = lax.rsqrt(square / depth + epsilon)
            top = scale.astype(jnp.bfloat16).astype(jnp.float32)
            old = tab[b, aligned(s, rows), :].astype(jnp.float32)
            fresh = jnp.where(
                lane == SCALE_LANE,
                top,
                jnp.where(lane == SCALE_LANE + half_lanes, scale - top, old),
            )
            tab[b, aligned(s, rows), :] = fresh.astype(jnp.bfloat16)
            tx_table(b, s).start()
            tc_table(b, 0, s).start()

        when(is_last(k), with_table)

    def relay(k):
        j, b = spot_of(k)
        jj, bb = column_from(side, k), b
        tx(jj, bb, side).wait_recv()
        tc(jj, bb, 1, side).start()

        def with_table():
            tx_table(b, side).wait_recv()
            tc_table(b, 1, side).start()

        when(is_last(k), with_table)

    def column_from(seq, k):
        late = k // half_steps
        m = k % half_steps
        n = (1 - late) * (m // roles) + late * (2 + m % 2)
        return (seq // 2 + n // 2) % 2 * 2 + (seq + n) % 2

    def pair_up(k):
        em_in(k).wait_recv()
        j, b = spot_of(k)
        spot = aligned(b, rows)
        part[j, spot, :] = (
            part[j, spot, :].astype(jnp.float32) + from_end[j, b].astype(jnp.float32)
        ).astype(jnp.bfloat16)
        mm(k).start()

    def complete(k):
        mm(k).wait_recv()
        j, b = spot_of(k)
        total = part[j, aligned(b, rows), :].astype(jnp.float32) + from_mid[j, b].astype(
            jnp.float32
        )
        tok[b, j, aligned(s, rows), :] = (total * gains[0, j]).astype(jnp.bfloat16)
        me(k).start()
        spread(k)

    query_row = s * rows + lax.broadcasted_iota(jnp.int32, (rows, full), 0)
    allowed = lax.broadcasted_iota(jnp.int32, (rows, full), 1) <= query_row
    allowed = jnp.concatenate([allowed] * heads, axis=0)

    def attend(i, carry):
        b = turn(i)
        stacked = jnp.concatenate(
            [q[b, :, h * HEAD_WIDTH : (h + 1) * HEAD_WIDTH] for h in range(heads)], axis=0
        )
        scores = lax.dot_general(
            stacked, kv[0, b], (((1,), (1,)), ((), ())), preferred_element_type=jnp.float32
        ) * (HEAD_WIDTH**-0.5)
        scores = jnp.where(allowed, scores, masked_score)
        weights = jnp.exp(scores - jnp.max(scores, axis=1, keepdims=True))
        totals = jnp.sum(weights, axis=1, keepdims=True)
        mixed = jnp.dot(
            weights.astype(jnp.bfloat16), kv[1, b], preferred_element_type=jnp.float32
        )
        mixed = (mixed / totals).astype(jnp.bfloat16)
        spot = aligned(b, rows)
        for h in range(heads):
            att[spot, h * HEAD_WIDTH : (h + 1) * HEAD_WIDTH] = mixed[h * rows : (h + 1) * rows]
        product = jnp.dot(att[spot, :], wo[s], preferred_element_type=jnp.float32)
        part[s, spot, :] = (product + base[s, spot, :].astype(jnp.float32)).astype(jnp.bfloat16)

        @pl.when(middle == 0)
        def _():
            em(i).start()

        return carry

    def project(j):
        product = jnp.dot(att[...], wo[j], preferred_element_type=jnp.float32)
        part[j] = (product + base[j].astype(jnp.float32)).astype(jnp.bfloat16)

    lax.fori_loop(0, batch, attend, 0)
    wo_own(mate).wait_recv()
    project(mate)
    for off in offs:
        tb_in(off).wait_recv()
        tb(off).wait_send()

    lag, relay_lag = LAGS

    def wo_finish():
        for c in range(chunks):
            wo_mate(far, g, c, 0).wait_recv()
            wo_mate(far, 1 - g, c, 1).wait_recv()
        project(side)
        project(far)

    spread_end = steps + lag

    @pl.when(middle == 0)
    def _():
        for k in range(roles, half_steps):
            em(k).start()
        for c in range(chunks):
            if c + 1 < chunks:
                wo_pass(c + 1)
            wo_turn(c)
        wo_finish()
        for k in range(half_steps, steps):
            em(k).start()

        def step(k, carry):
            me_in(k).wait_recv()
            spread(k)

            @pl.when(k >= relay_lag)
            def _():
                relay(k - relay_lag)

            return carry

        lax.fori_loop(0, steps, step, 0)

    @pl.when(middle == 1)
    def _():
        passes = {
            0: [(wo_pass, 1), (wo_turn, 0)],
            1: [(wo_pass, 2)],
            2: [(wo_turn, 1)],
            3: [(wo_pass, 3)],
            4: [(wo_turn, 2)],
            6: [(wo_turn, 3)],
        }

        def step(k):
            if isinstance(k, int):
                pair_up(k)
            else:
                when(k < steps, lambda: pair_up(k))
            when(k >= lag, lambda: complete(k - lag))
            when(k >= lag + relay_lag, lambda: relay(k - lag - relay_lag))

        for k in range(half_steps):
            for relay_wo, c in passes.get(k, ()):
                relay_wo(c)
            step(k)
        wo_finish()

        def late_step(k, carry):
            step(k)
            return carry

        lax.fori_loop(half_steps, steps + lag, late_step, 0)

    for copy in loads[6:]:
        copy.wait()

    expert = s * roles + r
    hidden_width = act.shape[1]
    step_f = hidden_width // 3 if hidden_width % 3 == 0 else hidden_width
    table_lane = lax.broadcasted_iota(jnp.int32, (full, LANES), 1) % half_lanes

    def yc(b, j, path):
        seq = far if path else mate
        return remote(
            y.at[b, j, aligned(seq, rows), :],
            y_core.at[b, j, path],
            yc_s.at[b, j, path],
            yc_r.at[b, j, path],
            {"seq": mate},
        )

    def yx(b, j):
        return remote(
            y.at[b, j, aligned(side, rows), :],
            y_x.at[b, j],
            yx_s.at[b, j],
            yx_r.at[b, j],
            {"seq": side},
        )

    def yz(way, b, j, to):
        return remote(
            y.at[b, j, aligned(s, rows), :],
            y_line.at[way, b, j],
            yz_s.at[b, j],
            yz_r.at[way, b, j],
            {"role": to},
        )

    def pass_core(b, j):
        yc(b, j, 1).wait_recv()
        spot = aligned(side, rows)
        y[b, j, spot, :] = (
            y[b, j, spot, :].astype(jnp.float32) + y_core[b, j, 1].astype(jnp.float32)
        ).astype(jnp.bfloat16)
        yx(b, j).start()

    def summed(b, j):
        yc(b, j, 0).wait_recv()
        yx(b, j).wait_recv()
        return (
            y[b, j, aligned(s, rows), :].astype(jnp.float32)
            + y_core[b, j, 0].astype(jnp.float32)
            + y_x[b, j].astype(jnp.float32)
        )

    relayed = steps - relay_lag

    def one_block(i, carry):
        b = turn(i)

        for k in range(relayed, steps):
            due = max(0, (k - half_steps) // 2 - 1)

            @pl.when(i == due)
            def _():
                relay(k)

        for j in range(seqs):
            tc(j, b, 0, mate).wait_recv()
            tc(j, b, 1, far).wait_recv()
        tc_table(b, 0, mate).wait_recv()
        tc_table(b, 1, far).wait_recv()
        shares = tab[b].astype(jnp.float32)
        share = jnp.sum(jnp.where(table_lane == expert, shares, 0.0), axis=1, keepdims=True)
        scale = jnp.sum(jnp.where(table_lane == SCALE_LANE, shares, 0.0), axis=1, keepdims=True)
        inputs = jnp.concatenate([tok[b, j] for j in range(seqs)], axis=1)
        for start in range(0, hidden_width, step_f):
            block = pl.ds(start, step_f)
            gate = jnp.dot(inputs, gw[0, :, block], preferred_element_type=jnp.float32) * scale
            up = jnp.dot(inputs, uw[0, :, block], preferred_element_type=jnp.float32) * scale
            act[:, block] = (gate / (1.0 + jnp.exp(-gate)) * up).astype(jnp.bfloat16)
            if start == 0:

                @pl.when(i > 0)
                def _():
                    for j in range(seqs):
                        pass_core(turn(i - 1), j)

        for j in range(seqs):
            block = pl.ds(j * cols, cols)
            product = jnp.dot(act[...], dw[0, :, block], preferred_element_type=jnp.float32)
            y[b, j] = (product * share).astype(jnp.bfloat16)
            yc(b, j, 1).start()
            yc(b, j, 0).start()

        return carry

    lax.fori_loop(0, roles, one_block, 0)
    for j in range(seqs):
        pass_core(turn(roles - 1), j)

    def line(i, carry):
        b = turn(i)
        for j in range(seqs):
            for way in range(2):

                @pl.when(b > r if way == 0 else b < r)
                def _():
                    total = summed(b, j)
                    spot = aligned(s, rows)
                    final[...] = total

                    @pl.when(r > 0 if way == 0 else r < roles - 1)
                    def _():
                        yz(way, b, j, r + 1 - 2 * way).wait_recv()
                        final[...] = final[...] + y_line[way, b, j].astype(jnp.float32)

                    y[b, j, spot, :] = final[...].astype(jnp.bfloat16)
                    yz(way, b, j, r + 1 - 2 * way).start()

        return carry

    lax.fori_loop(0, roles, line, 0)
    for j in range(seqs):
        final[...] = summed(r, j) + tok[r, j, aligned(s, rows), :].astype(jnp.float32) * gains[1, j]
        for way in range(2):

            @pl.when(r > 0 if way == 0 else r < roles - 1)
            def _():
                yz(way, r, j, r + 1 - 2 * way).wait_recv()
                final[...] = final[...] + y_line[way, r, j].astype(jnp.float32)

        out_ref[0, :, j * cols : (j + 1) * cols] = final[...].astype(out_ref.dtype)

    for off in offs:
        for t in range(2):
            kv1(t, off).wait_send()
    for path in range(3):
        for t in range(2):
            kv2(t, path, s, mate).wait_send()
    wo_own(s).wait_send()
    for c in range(chunks):
        wo_x(s, c).wait_send()
        wo_y(g, c).wait_send()
        for path in range(2):
            wo_mate(s, g, c, path).wait_send()

    def drain_steps(k, carry):
        @pl.when(middle == 0)
        def _():
            em(k).wait_send()

        @pl.when(middle == 1)
        def _():
            mm(k).wait_send()
            me(k).wait_send()

        return carry

    lax.fori_loop(0, steps, drain_steps, 0)

    def drain_blocks(b, carry):
        for j in range(seqs):
            tx(j, b, s).wait_send()
            yx(b, j).wait_send()
            for path in range(2):
                tc(j, b, path, s).wait_send()
                yc(b, j, path).wait_send()
        tx_table(b, s).wait_send()
        for path in range(2):
            tc_table(b, path, s).wait_send()

        for way in range(2):

            @pl.when(b > r if way == 0 else b < r)
            def _():
                for j in range(seqs):
                    yz(way, b, j, r + 1 - 2 * way).wait_send()

        return carry

    lax.fori_loop(0, roles, drain_blocks, 0)


def fused(
    query_rows,
    encoded_key_rows,
    value_matrix_rows,
    output_weight,
    residual,
    norm_gain,
    route_experts,
    route_gates,
    gate_weight,
    up_weight,
    down_weight,
):
    seqs, roles = lax.axis_size("seq"), lax.axis_size("role")
    batch, rows, width = query_rows.shape
    depth, cols = residual.shape[2], output_weight.shape[1]
    hidden_width = gate_weight.shape[2]
    full = rows * seqs
    bf16, f32 = jnp.bfloat16, jnp.float32
    gain = norm_gain.reshape(1, depth)
    route_experts = route_experts.transpose(0, 2, 1)
    route_gates = route_gates.transpose(0, 2, 1)
    vmem = [
        pltpu.VMEM(query_rows.shape, bf16),
        pltpu.VMEM((2, batch, full, HEAD_WIDTH), bf16),
        pltpu.VMEM((seqs, width, cols), bf16),
        pltpu.VMEM(residual.shape, bf16),
        pltpu.VMEM(gain.shape, f32),
        pltpu.VMEM(route_experts.shape, jnp.int32),
        pltpu.VMEM(route_gates.shape, f32),
        pltpu.VMEM(gate_weight.shape, bf16),
        pltpu.VMEM(up_weight.shape, bf16),
        pltpu.VMEM(down_weight.shape, bf16),
        pltpu.VMEM((batch * rows, width), bf16),
        pltpu.VMEM((2, seqs, 1, cols), f32),
        pltpu.VMEM((seqs, batch * rows, cols), bf16),
        pltpu.VMEM((seqs, batch * rows, cols), bf16),
        pltpu.VMEM((seqs, batch, rows, cols), bf16),
        pltpu.VMEM((seqs, batch, rows, cols), bf16),
        pltpu.VMEM((roles, seqs, full, cols), bf16),
        pltpu.VMEM((roles, full, LANES), bf16),
        pltpu.VMEM((full, hidden_width), bf16),
        pltpu.VMEM((roles, seqs, full, cols), bf16),
        pltpu.VMEM((roles, seqs, 2, rows, cols), bf16),
        pltpu.VMEM((roles, seqs, rows, cols), bf16),
        pltpu.VMEM((2, roles, seqs, rows, cols), bf16),
        pltpu.VMEM((rows, cols), f32),
    ]
    dma = pltpu.SemaphoreType.DMA
    steps = seqs * roles
    counts = [(2, roles)] * 2 + [(2, 3)] * 2 + [(9,)] * 2 + [(4,)] * 4 + [(4,)] * 2
    counts += [(steps,)] * 6 + [(seqs + 1, roles)] * 2 + [(2, seqs + 1, roles)] * 2
    counts += [(roles, seqs, 2)] * 2 + [(roles, seqs)] * 2
    counts += [(roles, seqs), (2, roles, seqs)]
    return pl.pallas_call(
        partial(layer_kernel, roles, seqs),
        out_shape=jax.ShapeDtypeStruct(residual.shape, bf16),
        in_specs=[pl.BlockSpec(memory_space=pl.ANY)] * 11,
        out_specs=pl.BlockSpec(memory_space=pltpu.VMEM),
        scratch_shapes=vmem + [dma((9,)), dma((2,))] + [dma(count) for count in counts],
        compiler_params=pltpu.CompilerParams(
            collective_id=0, has_side_effects=True, vmem_limit_bytes=60 * 1024 * 1024
        ),
    )(
        query_rows,
        encoded_key_rows,
        value_matrix_rows,
        output_weight,
        residual,
        gain,
        route_experts,
        route_gates,
        gate_weight,
        up_weight,
        down_weight,
    )


def solution(mesh):
    square = mesh.shape["seq"] == 4 and mesh.shape["role"] == 4 and mesh.shape["groups"] == 2
    body = fused if square else shards
    placed = (
        P("groups", "seq", "role"),
        P("groups", ("seq", "role"), None),
        P("groups", ("seq", "role"), None),
        P("role", "seq"),
        P(("groups", "role"), "seq", None),
        P(),
        P(("groups", "role"), "seq", None),
        P(("groups", "role"), "seq", None),
        P(("seq", "role"), None, None),
        P(("seq", "role"), None, None),
        P(("seq", "role"), None, None),
    )
    return jax.shard_map(
        body,
        mesh=mesh,
        in_specs=placed,
        out_specs=P(("groups", "role"), "seq", None),
        check_vma=False,
    )
```

```python
from functools import partial

import jax
import jax.numpy as jnp
from jax import lax
from jax.experimental import pallas as pl
from jax.experimental.pallas import tpu as pltpu
from jax.sharding import PartitionSpec as P

D = 2048
QUERY_HEADS = 32
KEY_VALUE_HEADS = 4
HEAD_WIDTH = 128
TOPK = 8


epsilon = 1e-06
masked_score = -1e30


def score_block(queries, every_key, query_position, block_start, block_width, score_scale):
    keys_part = lax.slice_in_dim(every_key, block_start, block_start + block_width, axis=0)
    raw_scores = (
        jnp.einsum("qhd,kd->hqk", queries, keys_part, preferred_element_type=jnp.float32)
        * score_scale
    )
    key_position = block_start + jnp.arange(block_width, dtype=jnp.int32)
    return jnp.where(
        key_position[None, None, :] <= query_position[None, :, None], raw_scores, masked_score
    )


def value_block(rounded, every_value, block_start, block_width):
    prob_block = lax.slice_in_dim(rounded, block_start, block_start + block_width, axis=2)
    values_part = lax.slice_in_dim(every_value, block_start, block_start + block_width, axis=0)
    return jnp.einsum("hqk,kd->qhd", prob_block, values_part, preferred_element_type=jnp.float32)


def shards(
    query_rows,
    encoded_key_rows,
    value_matrix_rows,
    output_weight,
    residual,
    norm_gain,
    route_experts,
    route_gates,
    gate_weight,
    up_weight,
    down_weight,
):
    seq_count = lax.axis_size("seq")
    role_count = lax.axis_size("role")
    seq_index = lax.axis_index("seq")
    role_index = lax.axis_index("role")
    batch_count = query_rows.shape[0]
    local_length = query_rows.shape[1]
    local_heads = query_rows.shape[2] // HEAD_WIDTH
    full_length = local_length * seq_count
    query_group_width = QUERY_HEADS // KEY_VALUE_HEADS
    head_pick = role_index * local_heads // query_group_width
    role_keys, role_values = (
        lax.all_gather(encoded_key_rows, "role", axis=1, tiled=True),
        lax.all_gather(value_matrix_rows, "role", axis=1, tiled=True),
    )
    head_keys = lax.dynamic_slice_in_dim(role_keys, head_pick * HEAD_WIDTH, HEAD_WIDTH, 2)
    head_values = lax.dynamic_slice_in_dim(role_values, head_pick * HEAD_WIDTH, HEAD_WIDTH, 2)
    whole_keys, whole_values, whole_proj = (
        lax.all_gather(head_keys, "seq", axis=1, tiled=True),
        lax.all_gather(head_values, "seq", axis=1, tiled=True),
        lax.all_gather(output_weight, "seq", axis=1, tiled=True),
    )
    key_width = full_length // 8
    score_scale = HEAD_WIDTH ** (-0.5)
    query_position = seq_index * local_length + jnp.arange(local_length, dtype=jnp.int32)
    last_needed = (seq_index + 1) * local_length

    def one_sequence(operands):
        own_queries, every_key, every_value = operands
        queries = own_queries.reshape(local_length, local_heads, HEAD_WIDTH)
        pieces = []
        for number in range(8):
            block_start = number * key_width
            compute = partial(
                score_block, queries, every_key, query_position, block_start, key_width, score_scale
            )
            skipped = partial(
                jnp.full, (local_heads, local_length, key_width), masked_score, jnp.float32
            )
            pieces.append(lax.cond(block_start < last_needed, compute, skipped))
        scores = jnp.concatenate(pieces, axis=2)
        row_peak = jnp.max(scores, axis=2, keepdims=True)
        weights = jnp.exp(scores - row_peak)
        totals = jnp.sum(weights, axis=2, keepdims=True)
        rounded = weights.astype(jnp.bfloat16)
        mixed_rows = jnp.zeros((local_length, local_heads, HEAD_WIDTH), jnp.float32)
        for number in range(8):
            block_start = number * key_width
            product = partial(value_block, rounded, every_value, block_start, key_width)
            nothing = partial(jnp.zeros, (local_length, local_heads, HEAD_WIDTH), jnp.float32)
            mixed_rows = mixed_rows + lax.cond(block_start < last_needed, product, nothing)
        attended = (mixed_rows / totals.transpose(1, 0, 2)).astype(jnp.bfloat16)
        return attended.reshape(local_length, local_heads * HEAD_WIDTH)

    attended = lax.map(one_sequence, (query_rows, whole_keys, whole_values))
    flat_attended = attended.reshape(batch_count * local_length, local_heads * HEAD_WIDTH)
    projected = lax.psum_scatter(
        jnp.dot(flat_attended, whole_proj, preferred_element_type=jnp.float32).astype(jnp.bfloat16),
        "role",
        scatter_dimension=0,
        tiled=True,
    ).astype(jnp.float32)
    hidden = residual[0].astype(jnp.float32) + projected
    variance = jnp.mean(hidden * hidden, axis=-1, keepdims=True)
    normed = (hidden * lax.rsqrt(variance + epsilon) * norm_gain).astype(jnp.bfloat16)
    expert_ids = route_experts.reshape(-1)
    gate_values = route_gates.reshape(-1)
    experts_local = gate_weight.shape[0]
    device_count = seq_count * role_count
    expert_count = experts_local * device_count
    assign = expert_ids.shape[0]
    capacity = assign // expert_count + 1
    onehot = (expert_ids[:, None] == jnp.arange(expert_count, dtype=jnp.int32)[None, :]).astype(
        jnp.int32
    )
    before = jnp.tri(assign, k=-1, dtype=jnp.bfloat16)
    earlier = jnp.dot(
        before, onehot.astype(jnp.bfloat16), preferred_element_type=jnp.float32
    ).astype(jnp.int32)
    slot_rank = jnp.sum(earlier * onehot, axis=1)
    slot_index = expert_ids * capacity + slot_rank
    source_token = jnp.arange(assign, dtype=jnp.int32) // TOPK
    slot_token = jnp.zeros((expert_count * capacity,), jnp.int32).at[slot_index].set(source_token)
    slot_used = jnp.zeros((expert_count * capacity,), jnp.bfloat16).at[slot_index].set(1.0)
    outgoing = (normed[slot_token] * slot_used[:, None]).reshape(
        device_count, experts_local, capacity, D
    )
    incoming = lax.all_to_all(outgoing, ("seq", "role"), split_axis=0, concat_axis=0, tiled=True)
    gate_hidden = jnp.einsum(
        "sjcd,jdf->sjcf", incoming, gate_weight, preferred_element_type=jnp.float32
    )
    up_hidden = jnp.einsum(
        "sjcd,jdf->sjcf", incoming, up_weight, preferred_element_type=jnp.float32
    )
    activated = (jax.nn.silu(gate_hidden) * up_hidden).astype(jnp.bfloat16)
    returned = lax.all_to_all(
        jnp.einsum(
            "sjcf,jfd->sjcd", activated, down_weight, preferred_element_type=jnp.float32
        ).astype(jnp.bfloat16),
        ("seq", "role"),
        split_axis=0,
        concat_axis=0,
        tiled=True,
    )
    gathered = returned.reshape(expert_count * capacity, D)[slot_index]
    weighted = gathered.astype(jnp.float32) * gate_values[:, None]
    expert_sum = jnp.sum(weighted.reshape(-1, TOPK, D), axis=1)
    return (hidden + expert_sum).astype(jnp.bfloat16).reshape(residual.shape)


MESH = pl.DeviceIdType.MESH
LANES = 128
LAGS = (3, 3)
WO_CHUNKS = 8
WO_FIRST = 3
WO_ATTEND = ((3, 3),)
WO_END = ((0, 4), (1, 0), (1, 1), (1, 2), (0, 5), (0, 6), (1, 3), (0, 7), (1, 4), (1, 5), (1, 6), (1, 7))
WO_MIDDLE = {
    0: ((0, 4), (1, 0), (1, 1), (1, 2), (0, 5)),
    1: ((0, 6), (1, 3)),
    2: ((0, 7), (1, 4)),
    3: ((1, 5),),
    4: ((1, 6),),
    5: ((1, 7),),
}


def aligned(index, size):
    return pl.ds(pl.multiple_of(index * size, size), size)


SCALE_LANE = 32


def layer_kernel(
    roles,
    seqs,
    q_hbm,
    k_hbm,
    v_hbm,
    wo_hbm,
    res_hbm,
    gain_hbm,
    ids_hbm,
    gates_hbm,
    gw_hbm,
    uw_hbm,
    dw_hbm,
    out_hbm,
    q,
    kv,
    wo,
    res,
    gain,
    ids,
    gates,
    gw,
    uw,
    dw,
    att,
    gains,
    base,
    part,
    from_end,
    from_mid,
    tok,
    tab,
    act,
    y,
    y_core,
    y_x,
    y_line,
    final,
    result,
    load_sem,
    own_sem,
    kv1_s,
    kv1_r,
    kv2_s,
    kv2_r,
    wm_s,
    wm_r,
    wx_s,
    wx_r,
    wy_s,
    wy_r,
    tb_s,
    tb_r,
    em_s,
    em_r,
    mm_s,
    mm_r,
    me_s,
    me_r,
    tx_s,
    tx_r,
    tc_s,
    tc_r,
    yc_s,
    yc_r,
    yx_s,
    yx_r,
    yz_s,
    yz_r,
):
    s = lax.axis_index("seq")
    r = lax.axis_index("role")
    g = lax.axis_index("groups")
    mate = s + 1 - 2 * (s % 2)
    side = (s + 2) % 4
    far = mate + 2 - 4 * (mate // 2)
    batch, rows, width = q.shape
    heads = width // HEAD_WIDTH
    own_keys = k_hbm.shape[1]
    full = rows * seqs
    cols = wo.shape[2]
    depth = cols * seqs
    offs = (1, 2, 3)
    chunks = WO_CHUNKS
    chunk_rows = width // (2 * chunks)
    middle = (r + 1) // 2 % 2
    inner = r + 1 - 2 * (r // 2)
    outer = r - 1 + 2 * (r // 2)
    other = 3 - r

    def role_of(i):
        return (r // 2 + i // 2) % 2 * 2 + (r + i) % 2

    def turn(i):
        return (1 - i // 2) * 3 * i + i // 2 * (i - 1)

    def order(i):
        swap = (1 - r // (roles - 1)) * (1 - (i % 3 + 1) // 2)
        return middle * turn(i) + (1 - middle) * (i + swap * (3 - 2 * i))

    def column(n):
        return (s // 2 + n // 2) % 2 * 2 + (s + n) % 2

    def remote(src, dst, ssem, rsem, device):
        return pltpu.make_async_remote_copy(
            src_ref=src,
            dst_ref=dst,
            send_sem=ssem,
            recv_sem=rsem,
            device_id=device,
            device_id_type=MESH,
        )

    def to_role(off):
        return {"role": role_of(off)}

    barrier = pltpu.get_barrier_semaphore()
    for off in offs:
        pl.semaphore_signal(barrier, inc=1, device_id=to_role(off), device_id_type=MESH)
    for peer in ({"seq": mate}, {"seq": side}, {"groups": 1 - g}):
        pl.semaphore_signal(barrier, inc=1, device_id=peer, device_id_type=MESH)

    loads = [
        pltpu.make_async_copy(a, b, load_sem.at[i])
        for i, (a, b) in enumerate(
            (
                (q_hbm, q),
                (res_hbm, res),
                (gain_hbm, gain),
                (ids_hbm, ids),
                (gates_hbm, gates),
                (wo_hbm, wo.at[s]),
                (gw_hbm, gw),
                (uw_hbm, uw),
                (dw_hbm, dw),
            )
        )
    ]
    pair = (k_hbm, v_hbm)

    def kv_spot(t, seq, role):
        return kv.at[t, :, aligned(seq * roles + role, own_keys), :]

    owns = [
        pltpu.make_async_copy(
            pair[t].at[:, :, aligned(r, HEAD_WIDTH)], kv_spot(t, s, r), own_sem.at[t]
        )
        for t in range(2)
    ]
    for copy in owns + loads[:6]:
        copy.start()

    for copy in loads[1:5]:
        copy.wait()
    half_lanes = LANES // 2
    place = lax.broadcasted_iota(jnp.int32, (LANES, rows), 0)
    table = jnp.zeros((LANES, rows), jnp.float32)
    for k in range(ids.shape[1]):
        chosen = place % half_lanes == ids[0, k : k + 1, :]
        table = table + jnp.where(chosen, gates[0, k : k + 1, :], 0.0)
    high = table.astype(jnp.bfloat16).astype(jnp.float32)
    parts = jnp.where(place < half_lanes, high, table - high).astype(jnp.bfloat16)
    unit = (
        lax.broadcasted_iota(jnp.int32, (rows, rows), 0)
        == lax.broadcasted_iota(jnp.int32, (rows, rows), 1)
    )
    tab[r, aligned(s, rows), :] = lax.dot_general(
        jnp.where(unit, 1.0, 0.0).astype(jnp.bfloat16),
        parts,
        (((1,), (1,)), ((), ())),
        preferred_element_type=jnp.float32,
    ).astype(jnp.bfloat16)
    base[...] = jnp.zeros_like(base)
    for j in range(seqs):
        block = pl.ds(j * cols, cols)
        gains[0, j] = gain[:, block]
        gains[1, j] = 1.0 / gain[:, block]
        base[j, aligned(r, rows), :] = res[0, :, block]

    pl.semaphore_wait(barrier, roles - 1 + 3)

    def kv1(t, off):
        return remote(
            pair[t].at[:, :, aligned(role_of(off), HEAD_WIDTH)],
            kv_spot(t, s, r),
            kv1_s.at[t, off],
            kv1_r.at[t, off],
            to_role(off),
        )

    def kv1_in(t, off):
        source = role_of(off)
        return remote(
            pair[t].at[:, :, aligned(r, HEAD_WIDTH)],
            kv_spot(t, s, source),
            kv1_s.at[t, off],
            kv1_r.at[t, off],
            to_role(off),
        )

    def tb(off):
        spot = tab.at[r, aligned(s, rows), :]
        return remote(spot, spot, tb_s.at[off], tb_r.at[off], to_role(off))

    def tb_in(off):
        spot = tab.at[role_of(off), aligned(s, rows), :]
        return remote(spot, spot, tb_s.at[off], tb_r.at[off], to_role(off))

    for off in offs:
        for t in range(2):
            kv1(t, off).start()

    def kv2(t, path, seq, target, b):
        spot = kv.at[t, b, aligned(seq, rows), :]
        return remote(spot, spot, kv2_s.at[t, path], kv2_r.at[t, path, b], {"seq": target})

    def wo_part(seq, n):
        return wo.at[seq, aligned(n, chunk_rows), :]

    def wo_own(seq):
        return remote(wo.at[seq], wo.at[seq], wm_s.at[0], wm_r.at[0], {"seq": mate})

    def wo_x(seq, c):
        spot = wo_part(seq, g * chunks + c)
        return remote(spot, spot, wx_s.at[0], wx_r.at[c], {"seq": side})

    def wo_y(half, c):
        spot = wo_part(side, half * chunks + c)
        return remote(spot, spot, wy_s.at[0], wy_r.at[c], {"groups": 1 - g})

    def wo_mate(seq, half, c, path):
        spot = wo_part(seq, half * chunks + c)
        return remote(
            spot, spot, wm_s.at[1], wm_r.at[1 + path * chunks + c], {"seq": mate}
        )

    def wo_pass(c):
        wo_x(side, c).wait_recv()
        wo_y(g, c).start()
        wo_mate(side, g, c, 0).start()

    def wo_turn(c):
        wo_y(1 - g, c).wait_recv()
        wo_mate(side, 1 - g, c, 1).start()

    loads[5].wait()
    for c in range(WO_FIRST):
        wo_x(s, c).start()
    wo_own(s).start()
    for off in offs:
        tb(off).start()
    for copy in loads[6:]:
        copy.start()
    for copy in owns:
        copy.wait()
    for off in offs:
        for t in range(2):
            kv1_in(t, off).wait_recv()
    for i in range(batch):
        for t in range(2):
            kv2(t, 1, s, side, turn(i)).start()
    for i in range(batch):
        for t in range(2):
            kv2(t, 0, s, mate, turn(i)).start()
    for c in range(WO_FIRST, chunks):
        wo_x(s, c).start()
    loads[0].wait()
    for c in range(WO_FIRST):
        wo_pass(c)

    def kv_relay(i):
        for t in range(2):
            kv2(t, 1, side, side, turn(i)).wait_recv()
            kv2(t, 2, side, mate, turn(i)).start()

    kv_relay(0)

    half_steps = 2 * roles
    steps = 2 * half_steps

    def spot_of(k):
        late = k // half_steps
        m = k % half_steps
        early_col, early_turn = m // roles, m % roles
        late_col, late_turn = 2 + m % 2, m // 2
        n = (1 - late) * early_col + late * late_col
        return column(n), turn((1 - late) * early_turn + late * late_turn)

    def part_of(k):
        j, b = spot_of(k)
        return part.at[j, aligned(b, rows), :]

    def em(k):
        j, b = spot_of(k)
        return remote(part_of(k), from_end.at[j, b], em_s.at[0], em_r.at[k], {"role": inner})

    def em_in(k):
        j, b = spot_of(k)
        return remote(part_of(k), from_end.at[j, b], em_s.at[0], em_r.at[k], {"role": outer})

    def mm(k):
        j, b = spot_of(k)
        return remote(part_of(k), from_mid.at[j, b], mm_s.at[0], mm_r.at[k], {"role": other})

    def piece(j, b, seq):
        return tok.at[b, j, aligned(seq, rows), :]

    def me(k):
        j, b = spot_of(k)
        return remote(piece(j, b, s), piece(j, b, s), me_s.at[0], me_r.at[k], {"role": outer})

    def me_in(k):
        j, b = spot_of(k)
        return remote(piece(j, b, s), piece(j, b, s), me_s.at[0], me_r.at[k], {"role": inner})

    def table_of(b, seq):
        return tab.at[b, aligned(seq, rows), :]

    def tx(j, b, seq):
        return remote(
            piece(j, b, seq), piece(j, b, seq), tx_s.at[0], tx_r.at[j, b], {"seq": side}
        )

    def tx_table(b, seq):
        spot = table_of(b, seq)
        return remote(spot, spot, tx_s.at[1], tx_r.at[seqs, b], {"seq": side})

    def tc(j, b, path, seq):
        spot = piece(j, b, seq)
        return remote(spot, spot, tc_s.at[0], tc_r.at[path, j, b], {"seq": mate})

    def tc_table(b, path, seq):
        spot = table_of(b, seq)
        return remote(
            spot, spot, tc_s.at[1], tc_r.at[path, seqs, b], {"seq": mate}
        )

    def when(condition, body):
        if isinstance(condition, bool):
            if condition:
                body()
        else:
            pl.when(condition)(body)

    def is_last(k):
        if isinstance(k, int):
            return k >= half_steps and k % 2 == 1
        return jnp.logical_and(k >= half_steps, k % 2 == 1)

    lane = lax.broadcasted_iota(jnp.int32, (rows, LANES), 1)

    def spread(k):
        j, b = spot_of(k)
        tx(j, b, s).start()
        tc(j, b, 0, s).start()

        def with_table():
            square = jnp.zeros((rows, 1), jnp.float32)
            for c in range(seqs):
                value = tok[b, c, aligned(s, rows), :].astype(jnp.float32) * gains[1, c]
                square = square + jnp.sum(value * value, axis=1, keepdims=True)
            scale = lax.rsqrt(square / depth + epsilon)
            top = scale.astype(jnp.bfloat16).astype(jnp.float32)
            old = tab[b, aligned(s, rows), :].astype(jnp.float32)
            fresh = jnp.where(
                lane == SCALE_LANE,
                top,
                jnp.where(lane == SCALE_LANE + half_lanes, scale - top, old),
            )
            tab[b, aligned(s, rows), :] = fresh.astype(jnp.bfloat16)
            tx_table(b, s).start()
            tc_table(b, 0, s).start()

        when(is_last(k), with_table)

    def relay(k):
        j, b = spot_of(k)
        jj, bb = column_from(side, k), b
        tx(jj, bb, side).wait_recv()
        tc(jj, bb, 1, side).start()

        def with_table():
            tx_table(b, side).wait_recv()
            tc_table(b, 1, side).start()

        when(is_last(k), with_table)

    def column_from(seq, k):
        late = k // half_steps
        m = k % half_steps
        n = (1 - late) * (m // roles) + late * (2 + m % 2)
        return (seq // 2 + n // 2) % 2 * 2 + (seq + n) % 2

    def pair_up(k):
        em_in(k).wait_recv()
        j, b = spot_of(k)
        spot = aligned(b, rows)
        part[j, spot, :] = (
            part[j, spot, :].astype(jnp.float32) + from_end[j, b].astype(jnp.float32)
        ).astype(jnp.bfloat16)
        mm(k).start()

    def complete(k):
        mm(k).wait_recv()
        j, b = spot_of(k)
        total = part[j, aligned(b, rows), :].astype(jnp.float32) + from_mid[j, b].astype(
            jnp.float32
        )
        tok[b, j, aligned(s, rows), :] = (total * gains[0, j]).astype(jnp.bfloat16)
        me(k).start()
        spread(k)

    query_row = s * rows + lax.broadcasted_iota(jnp.int32, (rows, full), 0)
    allowed = lax.broadcasted_iota(jnp.int32, (rows, full), 1) <= query_row
    allowed = jnp.concatenate([allowed] * heads, axis=0)

    def attend(i, carry):
        b = turn(i)

        @pl.when(i < batch - 1)
        def _():
            kv_relay(i + 1)

        for t in range(2):
            kv2(t, 0, mate, mate, b).wait_recv()
            kv2(t, 2, far, mate, b).wait_recv()
        stacked = jnp.concatenate(
            [q[b, :, h * HEAD_WIDTH : (h + 1) * HEAD_WIDTH] for h in range(heads)], axis=0
        )
        scores = lax.dot_general(
            stacked, kv[0, b], (((1,), (1,)), ((), ())), preferred_element_type=jnp.float32
        ) * (HEAD_WIDTH**-0.5)
        scores = jnp.where(allowed, scores, masked_score)
        weights = jnp.exp(scores - jnp.max(scores, axis=1, keepdims=True))
        totals = jnp.sum(weights, axis=1, keepdims=True)
        mixed = jnp.dot(
            weights.astype(jnp.bfloat16), kv[1, b], preferred_element_type=jnp.float32
        )
        mixed = (mixed / totals).astype(jnp.bfloat16)
        spot = aligned(b, rows)
        for h in range(heads):
            att[spot, h * HEAD_WIDTH : (h + 1) * HEAD_WIDTH] = mixed[h * rows : (h + 1) * rows]
        product = jnp.dot(att[spot, :], wo[s], preferred_element_type=jnp.float32)
        part[s, spot, :] = (product + base[s, spot, :].astype(jnp.float32)).astype(jnp.bfloat16)

        @pl.when(middle == 0)
        def _():
            em(i).start()

        for at, c in WO_ATTEND:

            @pl.when(i == at)
            def _():
                wo_pass(c)

        return carry

    def project(j):
        product = jnp.dot(att[...], wo[j], preferred_element_type=jnp.float32)
        part[j] = (product + base[j].astype(jnp.float32)).astype(jnp.bfloat16)

    lax.fori_loop(0, batch, attend, 0)
    wo_own(mate).wait_recv()
    project(mate)
    for off in offs:
        tb_in(off).wait_recv()
        tb(off).wait_send()

    lag, relay_lag = LAGS

    def wo_finish():
        for c in range(chunks):
            wo_mate(far, g, c, 0).wait_recv()
            wo_mate(far, 1 - g, c, 1).wait_recv()
        project(side)
        project(far)

    held = steps - lag
    @pl.when(middle == 0)
    def _():
        for k in range(roles, half_steps):
            em(k).start()
        for relay_wo, c in WO_END:
            (wo_turn if relay_wo else wo_pass)(c)
        wo_finish()
        for k in range(half_steps, steps):
            em(k).start()

        def step(k, carry):
            me_in(k).wait_recv()
            spread(k)

            @pl.when(k >= relay_lag)
            def _():
                relay(k - relay_lag)

            return carry

        lax.fori_loop(0, steps - 1, step, 0)

    @pl.when(middle == 1)
    def _():
        def step(k):
            if isinstance(k, int):
                pair_up(k)
            else:
                when(k < steps, lambda: pair_up(k))
            when(k >= lag, lambda: complete(k - lag))
            when(k >= lag + relay_lag, lambda: relay(k - lag - relay_lag))

        for k in range(half_steps):
            for relay_wo, c in WO_MIDDLE.get(k, ()):
                (wo_turn if relay_wo else wo_pass)(c)
            step(k)
        wo_finish()

        def late_step(k, carry):
            step(k)
            return carry

        lax.fori_loop(half_steps, steps, late_step, 0)

    for copy in loads[6:]:
        copy.wait()

    expert = s * roles + r
    hidden_width = act.shape[1]
    step_f = hidden_width // 3 if hidden_width % 3 == 0 else hidden_width
    table_lane = lax.broadcasted_iota(jnp.int32, (full, LANES), 1) % half_lanes

    def yc(b, j, path):
        seq = far if path else mate
        return remote(
            y.at[b, j, aligned(seq, rows), :],
            y_core.at[b, j, path],
            yc_s.at[0],
            yc_r.at[b, j, path],
            {"seq": mate},
        )

    def yx(b, j):
        return remote(
            y.at[b, j, aligned(side, rows), :],
            y_x.at[b, j],
            yx_s.at[0],
            yx_r.at[b, j],
            {"seq": side},
        )

    def yz(way, b, j, to):
        return remote(
            y.at[b, j, aligned(s, rows), :],
            y_line.at[way, b, j],
            yz_s.at[0],
            yz_r.at[way, b, j],
            {"role": to},
        )

    def pass_core(b, j):
        yc(b, j, 1).wait_recv()
        spot = aligned(side, rows)
        y[b, j, spot, :] = (
            y[b, j, spot, :].astype(jnp.float32) + y_core[b, j, 1].astype(jnp.float32)
        ).astype(jnp.bfloat16)
        yx(b, j).start()

    def summed(b, j):
        yc(b, j, 0).wait_recv()
        yx(b, j).wait_recv()
        return (
            y[b, j, aligned(s, rows), :].astype(jnp.float32)
            + y_core[b, j, 0].astype(jnp.float32)
            + y_x[b, j].astype(jnp.float32)
        )

    def hop(b, j):
        for way in range(2):

            @pl.when(b > r if way == 0 else b < r)
            def _():
                final[...] = summed(b, j)

                @pl.when(r > 0 if way == 0 else r < roles - 1)
                def _():
                    yz(way, b, j, r + 1 - 2 * way).wait_recv()
                    final[...] = final[...] + y_line[way, b, j].astype(jnp.float32)

                y[b, j, aligned(s, rows), :] = final[...].astype(jnp.bfloat16)
                yz(way, b, j, r + 1 - 2 * way).start()

    def late_middle(k):
        if k < steps:
            complete(k)
        relay(k - relay_lag)

    def late_end(k):
        if k < steps:
            me_in(k).wait_recv()
            spread(k)
        relay(k - relay_lag)

    def one_block(i, carry):
        b = order(i)
        for j in range(seqs):
            tc(j, b, 0, mate).wait_recv()
            tc(j, b, 1, far).wait_recv()
        tc_table(b, 0, mate).wait_recv()
        tc_table(b, 1, far).wait_recv()
        shares = tab[b].astype(jnp.float32)
        share = jnp.sum(jnp.where(table_lane == expert, shares, 0.0), axis=1, keepdims=True)
        scale = jnp.sum(jnp.where(table_lane == SCALE_LANE, shares, 0.0), axis=1, keepdims=True)
        inputs = jnp.concatenate([tok[b, j] for j in range(seqs)], axis=1)
        for start in range(0, hidden_width, step_f):
            block = pl.ds(start, step_f)
            gate = jnp.dot(inputs, gw[0, :, block], preferred_element_type=jnp.float32) * scale
            up = jnp.dot(inputs, uw[0, :, block], preferred_element_type=jnp.float32) * scale
            act[:, block] = (gate / (1.0 + jnp.exp(-gate)) * up).astype(jnp.bfloat16)
            if start == 0:

                @pl.when(i > 0)
                def _():
                    for j in range(seqs):
                        pass_core(order(i - 1), j)

                @pl.when(jnp.logical_and(i == roles - 1, middle == 0))
                def _():
                    for j in range(seqs):
                        hop(order(0), j)

        for at in range(roles - 1):

            @pl.when(jnp.logical_and(i == at, middle == 1))
            def _():
                for k in range(held + 2 * at, held + 2 * at + 2):
                    late_middle(k)

            if at < roles - 2:

                @pl.when(jnp.logical_and(i == at, middle == 0))
                def _():
                    for k in range(steps - 1 + 2 * at, steps + 1 + 2 * at):
                        late_end(k)

        for j in range(seqs):
            block = pl.ds(j * cols, cols)
            product = jnp.dot(act[...], dw[0, :, block], preferred_element_type=jnp.float32)
            y[b, j] = (product * share).astype(jnp.bfloat16)
            yc(b, j, 1).start()
            yc(b, j, 0).start()

        return carry

    lax.fori_loop(0, roles, one_block, 0)
    for j in range(seqs):
        pass_core(order(roles - 1), j)

    def sent(ref, sem):
        remote(ref, ref, sem, sem, {"seq": mate}).wait_send()

    sent(tok.at[0], wm_s.at[1])
    sent(wo.at[0], wm_s.at[0])
    half_wo = wo.at[0, 0 : width // 2]
    sent(half_wo, wx_s.at[0])
    sent(half_wo, wy_s.at[0])
    sent(from_end, tx_s.at[0])
    sent(y_core, tc_s.at[0])
    sent(tab.at[:, 0:rows], tx_s.at[1])
    sent(tab.at[:, 0 : 2 * rows], tc_s.at[1])
    for off in offs:
        for t in range(2):
            kv1(t, off).wait_send()
    for path in range(3):
        for t in range(2):
            sent(kv.at[t, :, 0:rows], kv2_s.at[t, path])

    @pl.when(middle == 0)
    def _():
        sent(from_end, em_s.at[0])

        for i in range(1, roles - 1):
            for j in range(seqs):
                hop(order(i), j)

    @pl.when(middle == 1)
    def _():
        sent(from_end, mm_s.at[0])
        sent(from_end, me_s.at[0])
        for b in ((2 - r) * (roles - 1), (r - 1) * (roles - 1), other):
            for j in range(seqs):
                hop(b, j)

    sent(y_core, yc_s.at[0])
    sent(y_x, yx_s.at[0])
    stores = [
        pltpu.make_async_copy(
            result.at[:, j * cols : (j + 1) * cols],
            out_hbm.at[0, :, j * cols : (j + 1) * cols],
            own_sem.at[j],
        )
        for j in range(seqs)
    ]
    for j in range(seqs):
        final[...] = summed(r, j) + tok[r, j, aligned(s, rows), :].astype(jnp.float32) * gains[1, j]
        for way in range(2):

            @pl.when(r > 0 if way == 0 else r < roles - 1)
            def _():
                yz(way, r, j, r + 1 - 2 * way).wait_recv()
                final[...] = final[...] + y_line[way, r, j].astype(jnp.float32)

        result[:, j * cols : (j + 1) * cols] = final[...].astype(result.dtype)
        stores[j].start()
    for store in stores:
        store.wait()
    sent(y_x.at[0 : roles - 1], yz_s.at[0])


def fused(
    query_rows,
    encoded_key_rows,
    value_matrix_rows,
    output_weight,
    residual,
    norm_gain,
    route_experts,
    route_gates,
    gate_weight,
    up_weight,
    down_weight,
):
    seqs, roles = lax.axis_size("seq"), lax.axis_size("role")
    batch, rows, width = query_rows.shape
    depth, cols = residual.shape[2], output_weight.shape[1]
    hidden_width = gate_weight.shape[2]
    full = rows * seqs
    bf16, f32 = jnp.bfloat16, jnp.float32
    gain = norm_gain.reshape(1, depth)
    route_experts = route_experts.transpose(0, 2, 1)
    route_gates = route_gates.transpose(0, 2, 1)
    vmem = [
        pltpu.VMEM(query_rows.shape, bf16),
        pltpu.VMEM((2, batch, full, HEAD_WIDTH), bf16),
        pltpu.VMEM((seqs, width, cols), bf16),
        pltpu.VMEM(residual.shape, bf16),
        pltpu.VMEM(gain.shape, f32),
        pltpu.VMEM(route_experts.shape, jnp.int32),
        pltpu.VMEM(route_gates.shape, f32),
        pltpu.VMEM(gate_weight.shape, bf16),
        pltpu.VMEM(up_weight.shape, bf16),
        pltpu.VMEM(down_weight.shape, bf16),
        pltpu.VMEM((batch * rows, width), bf16),
        pltpu.VMEM((2, seqs, 1, cols), f32),
        pltpu.VMEM((seqs, batch * rows, cols), bf16),
        pltpu.VMEM((seqs, batch * rows, cols), bf16),
        pltpu.VMEM((seqs, batch, rows, cols), bf16),
        pltpu.VMEM((seqs, batch, rows, cols), bf16),
        pltpu.VMEM((roles, seqs, full, cols), bf16),
        pltpu.VMEM((roles, full, LANES), bf16),
        pltpu.VMEM((full, hidden_width), bf16),
        pltpu.VMEM((roles, seqs, full, cols), bf16),
        pltpu.VMEM((roles, seqs, 2, rows, cols), bf16),
        pltpu.VMEM((roles, seqs, rows, cols), bf16),
        pltpu.VMEM((2, roles, seqs, rows, cols), bf16),
        pltpu.VMEM((rows, cols), f32),
        pltpu.VMEM((rows, depth), bf16),
    ]
    dma = pltpu.SemaphoreType.DMA
    steps = seqs * roles
    chunks = WO_CHUNKS
    counts = [(2, roles)] * 2 + [(2, 3), (2, 3, batch)] + [(2,), (1 + 2 * chunks,)]
    counts += [(1,), (chunks,)] * 2 + [(4,)] * 2 + [(1,), (steps,)] * 3
    counts += [(2,), (seqs + 1, roles), (2,), (2, seqs + 1, roles)]
    counts += [(1,), (roles, seqs, 2), (1,), (roles, seqs), (1,), (2, roles, seqs)]
    return pl.pallas_call(
        partial(layer_kernel, roles, seqs),
        out_shape=jax.ShapeDtypeStruct(residual.shape, bf16),
        in_specs=[pl.BlockSpec(memory_space=pl.ANY)] * 11,
        out_specs=pl.BlockSpec(memory_space=pl.ANY),
        scratch_shapes=vmem + [dma((9,)), dma((seqs,))] + [dma(count) for count in counts],
        compiler_params=pltpu.CompilerParams(
            collective_id=0, has_side_effects=True, vmem_limit_bytes=60 * 1024 * 1024
        ),
    )(
        query_rows,
        encoded_key_rows,
        value_matrix_rows,
        output_weight,
        residual,
        gain,
        route_experts,
        route_gates,
        gate_weight,
        up_weight,
        down_weight,
    )


def solution(mesh):
    square = mesh.shape["seq"] == 4 and mesh.shape["role"] == 4 and mesh.shape["groups"] == 2
    body = fused if square else shards
    placed = (
        P("groups", "seq", "role"),
        P("groups", ("seq", "role"), None),
        P("groups", ("seq", "role"), None),
        P("role", "seq"),
        P(("groups", "role"), "seq", None),
        P(),
        P(("groups", "role"), "seq", None),
        P(("groups", "role"), "seq", None),
        P(("seq", "role"), None, None),
        P(("seq", "role"), None, None),
        P(("seq", "role"), None, None),
    )
    return jax.shard_map(
        body,
        mesh=mesh,
        in_specs=placed,
        out_specs=P(("groups", "role"), "seq", None),
        check_vma=False,
    )
```

```python
from functools import partial

import jax
import jax.numpy as jnp
from jax import lax
from jax.experimental import pallas as pl
from jax.experimental.pallas import tpu as pltpu
from jax.sharding import PartitionSpec as P

D = 2048
QUERY_HEADS = 32
KEY_VALUE_HEADS = 4
HEAD_WIDTH = 128
TOPK = 8


epsilon = 1e-06
masked_score = -1e30


def score_block(queries, every_key, query_position, block_start, block_width, score_scale):
    keys_part = lax.slice_in_dim(every_key, block_start, block_start + block_width, axis=0)
    raw_scores = (
        jnp.einsum("qhd,kd->hqk", queries, keys_part, preferred_element_type=jnp.float32)
        * score_scale
    )
    key_position = block_start + jnp.arange(block_width, dtype=jnp.int32)
    return jnp.where(
        key_position[None, None, :] <= query_position[None, :, None], raw_scores, masked_score
    )


def value_block(rounded, every_value, block_start, block_width):
    prob_block = lax.slice_in_dim(rounded, block_start, block_start + block_width, axis=2)
    values_part = lax.slice_in_dim(every_value, block_start, block_start + block_width, axis=0)
    return jnp.einsum("hqk,kd->qhd", prob_block, values_part, preferred_element_type=jnp.float32)


def shards(
    query_rows,
    encoded_key_rows,
    value_matrix_rows,
    output_weight,
    residual,
    norm_gain,
    route_experts,
    route_gates,
    gate_weight,
    up_weight,
    down_weight,
):
    seq_count = lax.axis_size("seq")
    role_count = lax.axis_size("role")
    seq_index = lax.axis_index("seq")
    role_index = lax.axis_index("role")
    batch_count = query_rows.shape[0]
    local_length = query_rows.shape[1]
    local_heads = query_rows.shape[2] // HEAD_WIDTH
    full_length = local_length * seq_count
    query_group_width = QUERY_HEADS // KEY_VALUE_HEADS
    head_pick = role_index * local_heads // query_group_width
    role_keys, role_values = (
        lax.all_gather(encoded_key_rows, "role", axis=1, tiled=True),
        lax.all_gather(value_matrix_rows, "role", axis=1, tiled=True),
    )
    head_keys = lax.dynamic_slice_in_dim(role_keys, head_pick * HEAD_WIDTH, HEAD_WIDTH, 2)
    head_values = lax.dynamic_slice_in_dim(role_values, head_pick * HEAD_WIDTH, HEAD_WIDTH, 2)
    whole_keys, whole_values, whole_proj = (
        lax.all_gather(head_keys, "seq", axis=1, tiled=True),
        lax.all_gather(head_values, "seq", axis=1, tiled=True),
        lax.all_gather(output_weight, "seq", axis=1, tiled=True),
    )
    key_width = full_length // 8
    score_scale = HEAD_WIDTH ** (-0.5)
    query_position = seq_index * local_length + jnp.arange(local_length, dtype=jnp.int32)
    last_needed = (seq_index + 1) * local_length

    def one_sequence(operands):
        own_queries, every_key, every_value = operands
        queries = own_queries.reshape(local_length, local_heads, HEAD_WIDTH)
        pieces = []
        for number in range(8):
            block_start = number * key_width
            compute = partial(
                score_block, queries, every_key, query_position, block_start, key_width, score_scale
            )
            skipped = partial(
                jnp.full, (local_heads, local_length, key_width), masked_score, jnp.float32
            )
            pieces.append(lax.cond(block_start < last_needed, compute, skipped))
        scores = jnp.concatenate(pieces, axis=2)
        row_peak = jnp.max(scores, axis=2, keepdims=True)
        weights = jnp.exp(scores - row_peak)
        totals = jnp.sum(weights, axis=2, keepdims=True)
        rounded = weights.astype(jnp.bfloat16)
        mixed_rows = jnp.zeros((local_length, local_heads, HEAD_WIDTH), jnp.float32)
        for number in range(8):
            block_start = number * key_width
            product = partial(value_block, rounded, every_value, block_start, key_width)
            nothing = partial(jnp.zeros, (local_length, local_heads, HEAD_WIDTH), jnp.float32)
            mixed_rows = mixed_rows + lax.cond(block_start < last_needed, product, nothing)
        attended = (mixed_rows / totals.transpose(1, 0, 2)).astype(jnp.bfloat16)
        return attended.reshape(local_length, local_heads * HEAD_WIDTH)

    attended = lax.map(one_sequence, (query_rows, whole_keys, whole_values))
    flat_attended = attended.reshape(batch_count * local_length, local_heads * HEAD_WIDTH)
    projected = lax.psum_scatter(
        jnp.dot(flat_attended, whole_proj, preferred_element_type=jnp.float32).astype(jnp.bfloat16),
        "role",
        scatter_dimension=0,
        tiled=True,
    ).astype(jnp.float32)
    hidden = residual[0].astype(jnp.float32) + projected
    variance = jnp.mean(hidden * hidden, axis=-1, keepdims=True)
    normed = (hidden * lax.rsqrt(variance + epsilon) * norm_gain).astype(jnp.bfloat16)
    expert_ids = route_experts.reshape(-1)
    gate_values = route_gates.reshape(-1)
    experts_local = gate_weight.shape[0]
    device_count = seq_count * role_count
    expert_count = experts_local * device_count
    assign = expert_ids.shape[0]
    capacity = assign // expert_count + 1
    onehot = (expert_ids[:, None] == jnp.arange(expert_count, dtype=jnp.int32)[None, :]).astype(
        jnp.int32
    )
    before = jnp.tri(assign, k=-1, dtype=jnp.bfloat16)
    earlier = jnp.dot(
        before, onehot.astype(jnp.bfloat16), preferred_element_type=jnp.float32
    ).astype(jnp.int32)
    slot_rank = jnp.sum(earlier * onehot, axis=1)
    slot_index = expert_ids * capacity + slot_rank
    source_token = jnp.arange(assign, dtype=jnp.int32) // TOPK
    slot_token = jnp.zeros((expert_count * capacity,), jnp.int32).at[slot_index].set(source_token)
    slot_used = jnp.zeros((expert_count * capacity,), jnp.bfloat16).at[slot_index].set(1.0)
    outgoing = (normed[slot_token] * slot_used[:, None]).reshape(
        device_count, experts_local, capacity, D
    )
    incoming = lax.all_to_all(outgoing, ("seq", "role"), split_axis=0, concat_axis=0, tiled=True)
    gate_hidden = jnp.einsum(
        "sjcd,jdf->sjcf", incoming, gate_weight, preferred_element_type=jnp.float32
    )
    up_hidden = jnp.einsum(
        "sjcd,jdf->sjcf", incoming, up_weight, preferred_element_type=jnp.float32
    )
    activated = (jax.nn.silu(gate_hidden) * up_hidden).astype(jnp.bfloat16)
    returned = lax.all_to_all(
        jnp.einsum(
            "sjcf,jfd->sjcd", activated, down_weight, preferred_element_type=jnp.float32
        ).astype(jnp.bfloat16),
        ("seq", "role"),
        split_axis=0,
        concat_axis=0,
        tiled=True,
    )
    gathered = returned.reshape(expert_count * capacity, D)[slot_index]
    weighted = gathered.astype(jnp.float32) * gate_values[:, None]
    expert_sum = jnp.sum(weighted.reshape(-1, TOPK, D), axis=1)
    return (hidden + expert_sum).astype(jnp.bfloat16).reshape(residual.shape)


MESH = pl.DeviceIdType.MESH
LANES = 128
LAGS = (3, 3)
WO_CHUNKS = 8
WO_FIRST = 3
WO_ATTEND = ((3, 3),)
WO_END = ((0, 4), (1, 0), (1, 1), (1, 2), (0, 5), (0, 6), (1, 3), (0, 7), (1, 4), (1, 5), (1, 6), (1, 7))
WO_MIDDLE = {
    0: ((0, 4), (1, 0), (1, 1), (1, 2), (0, 5)),
    1: ((0, 6), (1, 3)),
    2: ((0, 7), (1, 4)),
    3: ((1, 5),),
    4: ((1, 6),),
    5: ((1, 7),),
}


def aligned(index, size):
    return pl.ds(pl.multiple_of(index * size, size), size)


SCALE_LANE = 32


def layer_kernel(
    roles,
    seqs,
    q_hbm,
    k_hbm,
    v_hbm,
    wo_hbm,
    res_hbm,
    gain_hbm,
    ids_hbm,
    gates_hbm,
    gw_hbm,
    uw_hbm,
    dw_hbm,
    out_hbm,
    q,
    kv,
    wo,
    res,
    gain,
    ids,
    gates,
    gw,
    uw,
    dw,
    att,
    gains,
    base,
    part,
    from_end,
    from_mid,
    from_mate,
    tok,
    tab,
    act,
    y,
    y_core,
    y_x,
    y_line,
    final,
    result,
    load_sem,
    own_sem,
    kv1_s,
    kv1_r,
    kv2_s,
    kv2_r,
    wm_s,
    wm_r,
    wx_s,
    wx_r,
    wy_s,
    wy_r,
    tb_s,
    tb_r,
    ln_s,
    ln_r,
    mm_s,
    mm_r,
    tx_s,
    tx_r,
    tc_s,
    tc_r,
    yc_s,
    yc_r,
    yx_s,
    yx_r,
    yz_s,
    yz_r,
):
    s = lax.axis_index("seq")
    r = lax.axis_index("role")
    g = lax.axis_index("groups")
    mate = s + 1 - 2 * (s % 2)
    side = (s + 2) % 4
    far = mate + 2 - 4 * (mate // 2)
    batch, rows, width = q.shape
    heads = width // HEAD_WIDTH
    own_keys = k_hbm.shape[1]
    full = rows * seqs
    cols = wo.shape[2]
    depth = cols * seqs
    offs = (1, 2, 3)
    chunks = WO_CHUNKS
    chunk_rows = width // (2 * chunks)
    middle = (r + 1) // 2 % 2
    inner = r + 1 - 2 * (r // 2)
    outer = r - 1 + 2 * (r // 2)
    other = 3 - r

    def role_of(i):
        return (r // 2 + i // 2) % 2 * 2 + (r + i) % 2

    def turn(i):
        return (1 - i // 2) * 3 * i + i // 2 * (i - 1)

    def order(i):
        swap = (1 - r // (roles - 1)) * (1 - (i % 3 + 1) // 2)
        return middle * turn(i) + (1 - middle) * (i + swap * (3 - 2 * i))

    def column(n):
        return (s // 2 + n // 2) % 2 * 2 + (s + n) % 2

    def remote(src, dst, ssem, rsem, device):
        return pltpu.make_async_remote_copy(
            src_ref=src,
            dst_ref=dst,
            send_sem=ssem,
            recv_sem=rsem,
            device_id=device,
            device_id_type=MESH,
        )

    def to_role(off):
        return {"role": role_of(off)}

    barrier = pltpu.get_barrier_semaphore()
    for off in offs:
        pl.semaphore_signal(barrier, inc=1, device_id=to_role(off), device_id_type=MESH)
    for peer in ({"seq": mate}, {"seq": side}, {"groups": 1 - g}):
        pl.semaphore_signal(barrier, inc=1, device_id=peer, device_id_type=MESH)

    loads = [
        pltpu.make_async_copy(a, b, load_sem.at[i])
        for i, (a, b) in enumerate(
            (
                (q_hbm, q),
                (res_hbm, res),
                (gain_hbm, gain),
                (ids_hbm, ids),
                (gates_hbm, gates),
                (wo_hbm, wo.at[s]),
                (gw_hbm, gw),
                (uw_hbm, uw),
                (dw_hbm, dw),
            )
        )
    ]
    pair = (k_hbm, v_hbm)

    def kv_spot(t, seq, role):
        return kv.at[t, :, aligned(seq * roles + role, own_keys), :]

    owns = [
        pltpu.make_async_copy(
            pair[t].at[:, :, aligned(r, HEAD_WIDTH)], kv_spot(t, s, r), own_sem.at[t]
        )
        for t in range(2)
    ]
    for copy in owns + loads[:6]:
        copy.start()

    for copy in loads[1:5]:
        copy.wait()
    half_lanes = LANES // 2
    place = lax.broadcasted_iota(jnp.int32, (LANES, rows), 0)
    table = jnp.zeros((LANES, rows), jnp.float32)
    for k in range(ids.shape[1]):
        chosen = place % half_lanes == ids[0, k : k + 1, :]
        table = table + jnp.where(chosen, gates[0, k : k + 1, :], 0.0)
    high = table.astype(jnp.bfloat16).astype(jnp.float32)
    parts = jnp.where(place < half_lanes, high, table - high).astype(jnp.bfloat16)
    unit = (
        lax.broadcasted_iota(jnp.int32, (rows, rows), 0)
        == lax.broadcasted_iota(jnp.int32, (rows, rows), 1)
    )
    tab[r, aligned(s, rows), :] = lax.dot_general(
        jnp.where(unit, 1.0, 0.0).astype(jnp.bfloat16),
        parts,
        (((1,), (1,)), ((), ())),
        preferred_element_type=jnp.float32,
    ).astype(jnp.bfloat16)
    base[...] = jnp.zeros_like(base)
    for j in range(seqs):
        block = pl.ds(j * cols, cols)
        gains[0, j] = gain[:, block]
        gains[1, j] = 1.0 / gain[:, block]
        base[j, aligned(r, rows), :] = res[0, :, block]

    pl.semaphore_wait(barrier, roles - 1 + 3)

    def kv1(t, off):
        return remote(
            pair[t].at[:, :, aligned(role_of(off), HEAD_WIDTH)],
            kv_spot(t, s, r),
            kv1_s.at[0],
            kv1_r.at[0],
            to_role(off),
        )

    def tb(off):
        spot = tab.at[r, aligned(s, rows), :]
        return remote(spot, spot, tb_s.at[0], tb_r.at[0], to_role(off))

    def sent(ref, sem):
        remote(ref, ref, sem, sem, {"seq": mate}).wait_send()

    def landed(ref, sem):
        remote(ref, ref, sem, sem, {"seq": mate}).wait_recv()

    for off in offs:
        for t in range(2):
            kv1(t, off).start()

    def kv2(path, seq, target, b):
        spot = kv.at[:, b, aligned(seq, rows), :]
        return remote(spot, spot, kv2_s.at[0], kv2_r.at[path, b], {"seq": target})

    def wo_part(seq, n):
        return wo.at[seq, aligned(n, chunk_rows), :]

    def wo_own(seq):
        return remote(wo.at[seq], wo.at[seq], wm_s.at[0], wm_r.at[0], {"seq": mate})

    def wo_x(seq, c):
        spot = wo_part(seq, g * chunks + c)
        return remote(spot, spot, wx_s.at[0], wx_r.at[c], {"seq": side})

    def wo_y(half, c):
        spot = wo_part(side, half * chunks + c)
        return remote(spot, spot, wy_s.at[0], wy_r.at[c], {"groups": 1 - g})

    def wo_mate(seq, half, c):
        spot = wo_part(seq, half * chunks + c)
        return remote(spot, spot, wm_s.at[1], wm_r.at[1], {"seq": mate})

    def wo_pass(c):
        wo_x(side, c).wait_recv()
        wo_y(g, c).start()
        wo_mate(side, g, c).start()

    def wo_turn(c):
        wo_y(1 - g, c).wait_recv()
        wo_mate(side, 1 - g, c).start()

    loads[5].wait()
    for c in range(WO_FIRST):
        wo_x(s, c).start()
    wo_own(s).start()
    for off in offs:
        tb(off).start()
    for copy in loads[6:]:
        copy.start()
    for copy in owns:
        copy.wait()
    landed(kv.at[:, :, 0 : own_keys * (roles - 1)], kv1_r.at[0])
    for path, target in ((1, side), (0, mate)):
        for i in range(batch):
            kv2(path, s, target, turn(i)).start()
    for c in range(WO_FIRST, chunks):
        wo_x(s, c).start()
    loads[0].wait()
    for c in range(WO_FIRST):
        wo_pass(c)

    def kv_relay(i):
        kv2(1, side, side, turn(i)).wait_recv()
        kv2(2, side, mate, turn(i)).start()

    kv_relay(0)

    half_steps = 2 * roles
    steps = 2 * half_steps

    def spot_of(k):
        late = k // half_steps
        m = k % half_steps
        early_col, early_turn = m // roles, m % roles
        late_col, late_turn = 2 + m % 2, m // 2
        n = (1 - late) * early_col + late * late_col
        return column(n), turn((1 - late) * early_turn + late * late_turn)

    def part_of(k):
        j, b = spot_of(k)
        return part.at[j, aligned(b, rows), :]

    def em(k):
        j, b = spot_of(k)
        return remote(part_of(k), from_end.at[j, b], ln_s.at[0], ln_r.at[k], {"role": inner})

    def em_in(k):
        j, b = spot_of(k)
        return remote(part_of(k), from_end.at[j, b], ln_s.at[0], ln_r.at[k], {"role": outer})

    def mm(k):
        j, b = spot_of(k)
        return remote(part_of(k), from_mid.at[j, b], mm_s.at[0], mm_r.at[k], {"role": other})

    def piece(j, b, seq):
        return tok.at[b, j, aligned(seq, rows), :]

    def me(k):
        j, b = spot_of(k)
        return remote(piece(j, b, s), piece(j, b, s), ln_s.at[0], ln_r.at[k], {"role": outer})

    def me_in(k):
        j, b = spot_of(k)
        return remote(piece(j, b, s), piece(j, b, s), ln_s.at[0], ln_r.at[k], {"role": inner})

    def table_of(b, seq):
        return tab.at[b, aligned(seq, rows), :]

    def tx(j, b, seq):
        return remote(
            piece(j, b, seq), piece(j, b, seq), tx_s.at[0], tx_r.at[j, b], {"seq": side}
        )

    def tx_table(j, b, seq):
        spot = table_of(b, seq)
        return remote(spot, spot, tx_s.at[1], tx_r.at[j, b], {"seq": side})

    def tc(j, b, seq):
        spot = piece(j, b, seq)
        return remote(spot, spot, tc_s.at[0], tc_r.at[b], {"seq": mate})

    def tc_table(b, seq):
        spot = table_of(b, seq)
        return remote(spot, spot, tc_s.at[1], tc_r.at[b], {"seq": mate})

    table_rows = rows * LANES // cols
    with_table_bytes = from_mate.at[0 : rows + table_rows]
    sequence_bytes = from_mate.at[...]

    def when(condition, body):
        if isinstance(condition, bool):
            if condition:
                body()
        else:
            pl.when(condition)(body)

    def is_last(k):
        if isinstance(k, int):
            return k >= half_steps and k % 2 == 1
        return jnp.logical_and(k >= half_steps, k % 2 == 1)

    lane = lax.broadcasted_iota(jnp.int32, (rows, LANES), 1)

    def spread(k):
        j, b = spot_of(k)
        tx(j, b, s).start()
        tc(j, b, s).start()

        def with_table():
            square = jnp.zeros((rows, 1), jnp.float32)
            for c in range(seqs):
                value = tok[b, c, aligned(s, rows), :].astype(jnp.float32) * gains[1, c]
                square = square + jnp.sum(value * value, axis=1, keepdims=True)
            scale = lax.rsqrt(square / depth + epsilon)
            top = scale.astype(jnp.bfloat16).astype(jnp.float32)
            old = tab[b, aligned(s, rows), :].astype(jnp.float32)
            fresh = jnp.where(
                lane == SCALE_LANE,
                top,
                jnp.where(lane == SCALE_LANE + half_lanes, scale - top, old),
            )
            tab[b, aligned(s, rows), :] = fresh.astype(jnp.bfloat16)
            tx_table(j, b, s).start()
            tc_table(b, s).start()

        when(is_last(k), with_table)

    def relay(k):
        j, b = column_from(side, k), spot_of(k)[1]

        def plain():
            tx(j, b, side).wait_recv()
            tc(j, b, side).start()

        def with_table():
            landed(with_table_bytes, tx_r.at[j, b])
            tc(j, b, side).start()
            tc_table(b, side).start()

        if isinstance(k, int):
            (with_table if is_last(k) else plain)()
        else:
            pl.when(is_last(k))(with_table)
            pl.when(jnp.logical_not(is_last(k)))(plain)

    def column_from(seq, k):
        late = k // half_steps
        m = k % half_steps
        n = (1 - late) * (m // roles) + late * (2 + m % 2)
        return (seq // 2 + n // 2) % 2 * 2 + (seq + n) % 2

    def pair_up(k):
        em_in(k).wait_recv()
        j, b = spot_of(k)
        spot = aligned(b, rows)
        part[j, spot, :] = (
            part[j, spot, :].astype(jnp.float32) + from_end[j, b].astype(jnp.float32)
        ).astype(jnp.bfloat16)
        mm(k).start()

    def complete(k):
        mm(k).wait_recv()
        j, b = spot_of(k)
        total = part[j, aligned(b, rows), :].astype(jnp.float32) + from_mid[j, b].astype(
            jnp.float32
        )
        tok[b, j, aligned(s, rows), :] = (total * gains[0, j]).astype(jnp.bfloat16)
        me(k).start()
        spread(k)

    query_row = s * rows + lax.broadcasted_iota(jnp.int32, (rows, full), 0)
    allowed = lax.broadcasted_iota(jnp.int32, (rows, full), 1) <= query_row
    allowed = jnp.concatenate([allowed] * heads, axis=0)

    def attend(i, carry):
        b = turn(i)

        @pl.when(i < batch - 1)
        def _():
            kv_relay(i + 1)

        kv2(0, mate, mate, b).wait_recv()
        kv2(2, far, mate, b).wait_recv()
        stacked = jnp.concatenate(
            [q[b, :, h * HEAD_WIDTH : (h + 1) * HEAD_WIDTH] for h in range(heads)], axis=0
        )
        scores = lax.dot_general(
            stacked, kv[0, b], (((1,), (1,)), ((), ())), preferred_element_type=jnp.float32
        ) * (HEAD_WIDTH**-0.5)
        scores = jnp.where(allowed, scores, masked_score)
        weights = jnp.exp(scores - jnp.max(scores, axis=1, keepdims=True))
        totals = jnp.sum(weights, axis=1, keepdims=True)
        mixed = jnp.dot(
            weights.astype(jnp.bfloat16), kv[1, b], preferred_element_type=jnp.float32
        )
        mixed = (mixed / totals).astype(jnp.bfloat16)
        spot = aligned(b, rows)
        for h in range(heads):
            att[spot, h * HEAD_WIDTH : (h + 1) * HEAD_WIDTH] = mixed[h * rows : (h + 1) * rows]
        product = jnp.dot(att[spot, :], wo[s], preferred_element_type=jnp.float32)
        part[s, spot, :] = (product + base[s, spot, :].astype(jnp.float32)).astype(jnp.bfloat16)

        @pl.when(middle == 0)
        def _():
            em(i).start()

        for at, c in WO_ATTEND:

            @pl.when(i == at)
            def _():
                wo_pass(c)

        return carry

    def project(j):
        product = jnp.dot(att[...], wo[j], preferred_element_type=jnp.float32)
        part[j] = (product + base[j].astype(jnp.float32)).astype(jnp.bfloat16)

    lax.fori_loop(0, batch, attend, 0)
    wo_own(mate).wait_recv()
    project(mate)
    others = tab.at[0 : roles - 1, 0:rows]
    landed(others, tb_r.at[0])
    sent(others, tb_s.at[0])

    lag, relay_lag = LAGS

    def wo_finish():
        landed(wo.at[far], wm_r.at[1])
        project(side)
        project(far)

    held = steps - lag
    @pl.when(middle == 0)
    def _():
        for k in range(roles, half_steps):
            em(k).start()
        for relay_wo, c in WO_END:
            (wo_turn if relay_wo else wo_pass)(c)
        wo_finish()
        for k in range(half_steps, steps):
            em(k).start()

        def step(k, carry):
            me_in(k).wait_recv()
            spread(k)

            @pl.when(k >= relay_lag)
            def _():
                relay(k - relay_lag)

            return carry

        lax.fori_loop(0, steps - lag, step, 0)
        for k in range(steps - lag - relay_lag, steps - lag - relay_lag + 2):
            relay(k)

    @pl.when(middle == 1)
    def _():
        def step(k):
            if isinstance(k, int):
                pair_up(k)
            else:
                when(k < steps, lambda: pair_up(k))
            when(k >= lag, lambda: complete(k - lag))
            when(k >= lag + relay_lag, lambda: relay(k - lag - relay_lag))

        for k in range(half_steps):
            for relay_wo, c in WO_MIDDLE.get(k, ()):
                (wo_turn if relay_wo else wo_pass)(c)
            step(k)
        wo_finish()

        def late_step(k, carry):
            step(k)
            return carry

        lax.fori_loop(half_steps, steps, late_step, 0)

    for copy in loads[6:]:
        copy.wait()

    expert = s * roles + r
    hidden_width = act.shape[1]
    step_f = hidden_width // 3 if hidden_width % 3 == 0 else hidden_width
    table_lane = lax.broadcasted_iota(jnp.int32, (full, LANES), 1) % half_lanes

    def yc(b, j, path):
        seq = far if path else mate
        return remote(
            y.at[b, j, aligned(seq, rows), :],
            y_core.at[b, j, path],
            yc_s.at[0],
            yc_r.at[b, j * path + seqs * (1 - path)],
            {"seq": mate},
        )

    def yx(b, j):
        return remote(
            y.at[b, j, aligned(side, rows), :],
            y_x.at[b, j],
            yx_s.at[0],
            yx_r.at[b, j],
            {"seq": side},
        )

    def slot(way, b, at):
        own = way * (1 - ((at - b) * way + roles - 2) // (roles - 1))
        return b * (1 - own) + roles * own

    def yz(way, b, j, to):
        place_there = slot(way, b, to)
        return remote(
            y.at[b, j, aligned(s, rows), :],
            y_line.at[place_there, j],
            yz_s.at[0],
            yz_r.at[place_there, j],
            {"role": to},
        )

    def yz_in(way, b, j):
        here = slot(way, b, r)
        landed(y_line.at[here, j], yz_r.at[here, j])
        return y_line[here, j].astype(jnp.float32)

    def pass_core(b, j):
        yc(b, j, 1).wait_recv()
        spot = aligned(side, rows)
        y[b, j, spot, :] = (
            y[b, j, spot, :].astype(jnp.float32) + y_core[b, j, 1].astype(jnp.float32)
        ).astype(jnp.bfloat16)
        yx(b, j).start()

    def summed(b, j):
        if j == 0:
            landed(y_core.at[b, :, 0], yc_r.at[b, seqs])
        yx(b, j).wait_recv()
        return (
            y[b, j, aligned(s, rows), :].astype(jnp.float32)
            + y_core[b, j, 0].astype(jnp.float32)
            + y_x[b, j].astype(jnp.float32)
        )

    def hop(b, j):
        for way in range(2):

            @pl.when(b > r if way == 0 else b < r)
            def _():
                final[...] = summed(b, j)

                @pl.when(r > 0 if way == 0 else r < roles - 1)
                def _():
                    final[...] = final[...] + yz_in(way, b, j)

                y[b, j, aligned(s, rows), :] = final[...].astype(jnp.bfloat16)
                yz(way, b, j, r + 1 - 2 * way).start()

    def early_hop(n):
        hop(order(n // seqs), n % seqs)

    def arrive_end(k):
        me_in(k).wait_recv()
        spread(k)

    late_middle = {
        (0, 0): ((complete, 13), (relay, 10)),
        (0, 2): ((complete, 14), (relay, 11)),
        (0, 3): ((complete, 15), (relay, 12)),
        (1, 2): ((relay, 13),),
        (1, 3): ((relay, 14),),
        (2, 0): ((relay, 15),),
    }
    late_end = {
        (0, 0): ((arrive_end, 13),),
        (0, 2): ((arrive_end, 14), (relay, 12)),
        (0, 3): ((arrive_end, 15),),
        (0, 4): ((relay, 13),),
        (1, 2): ((relay, 14), (relay, 15)),
        (1, 3): ((early_hop, 0), (early_hop, 1)),
        (2, 0): ((early_hop, 2),),
        (2, 2): ((early_hop, 3),),
        (2, 3): ((early_hop, 4),),
        (3, 0): ((early_hop, 5),),
        (3, 2): ((early_hop, 6),),
        (3, 3): ((early_hop, 7),),
    }

    def late(i, at):
        for here, plan in ((1, late_middle), (0, late_end)):
            for (block, place_in), jobs in plan.items():
                if place_in == at:

                    @pl.when(jnp.logical_and(i == block, middle == here))
                    def _():
                        for job, k in jobs:
                            job(k)

    def one_block(i, carry):
        b = order(i)
        landed(sequence_bytes, tc_r.at[b])
        shares = tab[b].astype(jnp.float32)
        share = jnp.sum(jnp.where(table_lane == expert, shares, 0.0), axis=1, keepdims=True)
        scale = jnp.sum(jnp.where(table_lane == SCALE_LANE, shares, 0.0), axis=1, keepdims=True)
        inputs = jnp.concatenate([tok[b, j] for j in range(seqs)], axis=1)
        for start in range(0, hidden_width, step_f):
            block = pl.ds(start, step_f)
            gate = jnp.dot(inputs, gw[0, :, block], preferred_element_type=jnp.float32) * scale
            up = jnp.dot(inputs, uw[0, :, block], preferred_element_type=jnp.float32) * scale
            act[:, block] = (gate / (1.0 + jnp.exp(-gate)) * up).astype(jnp.bfloat16)
            if start == 0:

                @pl.when(i > 1)
                def _():
                    for j in range(seqs):
                        pass_core(order(i - 1), j)

                late(i, 0)

        late(i, 2)
        for j in range(seqs):
            block = pl.ds(j * cols, cols)
            product = jnp.dot(act[...], dw[0, :, block], preferred_element_type=jnp.float32)
            y[b, j] = (product * share).astype(jnp.bfloat16)
            yc(b, j, 1).start()
            yc(b, j, 0).start()
        late(i, 3)

        @pl.when(i == 0)
        def _():
            for j in range(seqs):
                pass_core(b, j)

        late(i, 4)
        return carry

    lax.fori_loop(0, roles, one_block, 0)
    for j in range(seqs):
        pass_core(order(roles - 1), j)

    sent(tok.at[0], wm_s.at[1])
    sent(wo.at[0], wm_s.at[0])
    half_wo = wo.at[0, 0 : width // 2]
    sent(half_wo, wx_s.at[0])
    sent(half_wo, wy_s.at[0])
    sent(from_end, tx_s.at[0])
    sent(y_core, tc_s.at[0])
    sent(tab.at[:, 0:rows], tx_s.at[1])
    sent(tab.at[:, 0 : 2 * rows], tc_s.at[1])
    sent(kv.at[:, :, 0 : own_keys * (roles - 1)], kv1_s.at[0])
    sent(kv.at[:, :, 0 : 3 * rows], kv2_s.at[0])

    @pl.when(middle == 0)
    def _():
        sent(from_end, ln_s.at[0])

        for j in range(seqs):
            hop(order(roles - 2), j)

    @pl.when(middle == 1)
    def _():
        sent(from_end, mm_s.at[0])
        sent(from_end, ln_s.at[0])
        for b in ((2 - r) * (roles - 1), (r - 1) * (roles - 1), other):
            for j in range(seqs):
                hop(b, j)

    sent(y_core, yc_s.at[0])
    sent(y_x, yx_s.at[0])
    stores = [
        pltpu.make_async_copy(
            result.at[:, j * cols : (j + 1) * cols],
            out_hbm.at[0, :, j * cols : (j + 1) * cols],
            own_sem.at[j],
        )
        for j in range(seqs)
    ]
    for j in range(seqs):
        final[...] = summed(r, j) + tok[r, j, aligned(s, rows), :].astype(jnp.float32) * gains[1, j]
        for way in range(2):

            @pl.when(r > 0 if way == 0 else r < roles - 1)
            def _():
                final[...] = final[...] + yz_in(way, r, j)

        result[:, j * cols : (j + 1) * cols] = final[...].astype(result.dtype)
        stores[j].start()
    for store in stores:
        store.wait()
    sent(y_x.at[0 : roles - 1], yz_s.at[0])


def fused(
    query_rows,
    encoded_key_rows,
    value_matrix_rows,
    output_weight,
    residual,
    norm_gain,
    route_experts,
    route_gates,
    gate_weight,
    up_weight,
    down_weight,
):
    seqs, roles = lax.axis_size("seq"), lax.axis_size("role")
    batch, rows, width = query_rows.shape
    depth, cols = residual.shape[2], output_weight.shape[1]
    hidden_width = gate_weight.shape[2]
    full = rows * seqs
    bf16, f32 = jnp.bfloat16, jnp.float32
    gain = norm_gain.reshape(1, depth)
    route_experts = route_experts.transpose(0, 2, 1)
    route_gates = route_gates.transpose(0, 2, 1)
    vmem = [
        pltpu.VMEM(query_rows.shape, bf16),
        pltpu.VMEM((2, batch, full, HEAD_WIDTH), bf16),
        pltpu.VMEM((seqs, width, cols), bf16),
        pltpu.VMEM(residual.shape, bf16),
        pltpu.VMEM(gain.shape, f32),
        pltpu.VMEM(route_experts.shape, jnp.int32),
        pltpu.VMEM(route_gates.shape, f32),
        pltpu.VMEM(gate_weight.shape, bf16),
        pltpu.VMEM(up_weight.shape, bf16),
        pltpu.VMEM(down_weight.shape, bf16),
        pltpu.VMEM((batch * rows, width), bf16),
        pltpu.VMEM((2, seqs, 1, cols), f32),
        pltpu.VMEM((seqs, batch * rows, cols), bf16),
        pltpu.VMEM((seqs, batch * rows, cols), bf16),
        pltpu.VMEM((seqs, batch, rows, cols), bf16),
        pltpu.VMEM((seqs, batch, rows, cols), bf16),
        pltpu.VMEM((2 * (full + rows * LANES // cols), cols), bf16),
        pltpu.VMEM((roles, seqs, full, cols), bf16),
        pltpu.VMEM((roles, full, LANES), bf16),
        pltpu.VMEM((full, hidden_width), bf16),
        pltpu.VMEM((roles, seqs, full, cols), bf16),
        pltpu.VMEM((roles, seqs, 2, rows, cols), bf16),
        pltpu.VMEM((roles, seqs, rows, cols), bf16),
        pltpu.VMEM((roles + 1, seqs, rows, cols), bf16),
        pltpu.VMEM((rows, cols), f32),
        pltpu.VMEM((rows, depth), bf16),
    ]
    dma = pltpu.SemaphoreType.DMA
    steps = seqs * roles
    chunks = WO_CHUNKS
    counts = [(1,)] * 3 + [(3, batch)] + [(2,)] * 2 + [(1,), (chunks,)] * 2 + [(1,)] * 2
    counts += [(1,), (steps,)] * 2 + [(2,), (seqs, roles), (2,), (roles,)]
    counts += [(1,), (roles, seqs + 1), (1,), (roles, seqs), (1,), (roles + 1, seqs)]
    return pl.pallas_call(
        partial(layer_kernel, roles, seqs),
        out_shape=jax.ShapeDtypeStruct(residual.shape, bf16),
        in_specs=[pl.BlockSpec(memory_space=pl.ANY)] * 11,
        out_specs=pl.BlockSpec(memory_space=pl.ANY),
        scratch_shapes=vmem + [dma((9,)), dma((seqs,))] + [dma(count) for count in counts],
        compiler_params=pltpu.CompilerParams(
            collective_id=0, has_side_effects=True, vmem_limit_bytes=60 * 1024 * 1024
        ),
    )(
        query_rows,
        encoded_key_rows,
        value_matrix_rows,
        output_weight,
        residual,
        gain,
        route_experts,
        route_gates,
        gate_weight,
        up_weight,
        down_weight,
    )


def solution(mesh):
    square = mesh.shape["seq"] == 4 and mesh.shape["role"] == 4 and mesh.shape["groups"] == 2
    body = fused if square else shards
    placed = (
        P("groups", "seq", "role"),
        P("groups", ("seq", "role"), None),
        P("groups", ("seq", "role"), None),
        P("role", "seq"),
        P(("groups", "role"), "seq", None),
        P(),
        P(("groups", "role"), "seq", None),
        P(("groups", "role"), "seq", None),
        P(("seq", "role"), None, None),
        P(("seq", "role"), None, None),
        P(("seq", "role"), None, None),
    )
    return jax.shard_map(
        body,
        mesh=mesh,
        in_specs=placed,
        out_specs=P(("groups", "role"), "seq", None),
        check_vma=False,
    )
```

```python
from functools import partial

import jax
import jax.numpy as jnp
from jax import lax
from jax.experimental import pallas as pl
from jax.experimental.pallas import tpu as pltpu
from jax.sharding import PartitionSpec as P

D = 2048
QUERY_HEADS = 32
KEY_VALUE_HEADS = 4
HEAD_WIDTH = 128
TOPK = 8


epsilon = 1e-06
masked_score = -1e30


def score_block(queries, every_key, query_position, block_start, block_width, score_scale):
    keys_part = lax.slice_in_dim(every_key, block_start, block_start + block_width, axis=0)
    raw_scores = (
        jnp.einsum("qhd,kd->hqk", queries, keys_part, preferred_element_type=jnp.float32)
        * score_scale
    )
    key_position = block_start + jnp.arange(block_width, dtype=jnp.int32)
    return jnp.where(
        key_position[None, None, :] <= query_position[None, :, None], raw_scores, masked_score
    )


def value_block(rounded, every_value, block_start, block_width):
    prob_block = lax.slice_in_dim(rounded, block_start, block_start + block_width, axis=2)
    values_part = lax.slice_in_dim(every_value, block_start, block_start + block_width, axis=0)
    return jnp.einsum("hqk,kd->qhd", prob_block, values_part, preferred_element_type=jnp.float32)


def shards(
    query_rows,
    encoded_key_rows,
    value_matrix_rows,
    output_weight,
    residual,
    norm_gain,
    route_experts,
    route_gates,
    gate_weight,
    up_weight,
    down_weight,
):
    seq_count = lax.axis_size("seq")
    role_count = lax.axis_size("role")
    seq_index = lax.axis_index("seq")
    role_index = lax.axis_index("role")
    batch_count = query_rows.shape[0]
    local_length = query_rows.shape[1]
    local_heads = query_rows.shape[2] // HEAD_WIDTH
    full_length = local_length * seq_count
    query_group_width = QUERY_HEADS // KEY_VALUE_HEADS
    head_pick = role_index * local_heads // query_group_width
    role_keys, role_values = (
        lax.all_gather(encoded_key_rows, "role", axis=1, tiled=True),
        lax.all_gather(value_matrix_rows, "role", axis=1, tiled=True),
    )
    head_keys = lax.dynamic_slice_in_dim(role_keys, head_pick * HEAD_WIDTH, HEAD_WIDTH, 2)
    head_values = lax.dynamic_slice_in_dim(role_values, head_pick * HEAD_WIDTH, HEAD_WIDTH, 2)
    whole_keys, whole_values, whole_proj = (
        lax.all_gather(head_keys, "seq", axis=1, tiled=True),
        lax.all_gather(head_values, "seq", axis=1, tiled=True),
        lax.all_gather(output_weight, "seq", axis=1, tiled=True),
    )
    key_width = full_length // 8
    score_scale = HEAD_WIDTH ** (-0.5)
    query_position = seq_index * local_length + jnp.arange(local_length, dtype=jnp.int32)
    last_needed = (seq_index + 1) * local_length

    def one_sequence(operands):
        own_queries, every_key, every_value = operands
        queries = own_queries.reshape(local_length, local_heads, HEAD_WIDTH)
        pieces = []
        for number in range(8):
            block_start = number * key_width
            compute = partial(
                score_block, queries, every_key, query_position, block_start, key_width, score_scale
            )
            skipped = partial(
                jnp.full, (local_heads, local_length, key_width), masked_score, jnp.float32
            )
            pieces.append(lax.cond(block_start < last_needed, compute, skipped))
        scores = jnp.concatenate(pieces, axis=2)
        row_peak = jnp.max(scores, axis=2, keepdims=True)
        weights = jnp.exp(scores - row_peak)
        totals = jnp.sum(weights, axis=2, keepdims=True)
        rounded = weights.astype(jnp.bfloat16)
        mixed_rows = jnp.zeros((local_length, local_heads, HEAD_WIDTH), jnp.float32)
        for number in range(8):
            block_start = number * key_width
            product = partial(value_block, rounded, every_value, block_start, key_width)
            nothing = partial(jnp.zeros, (local_length, local_heads, HEAD_WIDTH), jnp.float32)
            mixed_rows = mixed_rows + lax.cond(block_start < last_needed, product, nothing)
        attended = (mixed_rows / totals.transpose(1, 0, 2)).astype(jnp.bfloat16)
        return attended.reshape(local_length, local_heads * HEAD_WIDTH)

    attended = lax.map(one_sequence, (query_rows, whole_keys, whole_values))
    flat_attended = attended.reshape(batch_count * local_length, local_heads * HEAD_WIDTH)
    projected = lax.psum_scatter(
        jnp.dot(flat_attended, whole_proj, preferred_element_type=jnp.float32).astype(jnp.bfloat16),
        "role",
        scatter_dimension=0,
        tiled=True,
    ).astype(jnp.float32)
    hidden = residual[0].astype(jnp.float32) + projected
    variance = jnp.mean(hidden * hidden, axis=-1, keepdims=True)
    normed = (hidden * lax.rsqrt(variance + epsilon) * norm_gain).astype(jnp.bfloat16)
    expert_ids = route_experts.reshape(-1)
    gate_values = route_gates.reshape(-1)
    experts_local = gate_weight.shape[0]
    device_count = seq_count * role_count
    expert_count = experts_local * device_count
    assign = expert_ids.shape[0]
    capacity = assign // expert_count + 1
    onehot = (expert_ids[:, None] == jnp.arange(expert_count, dtype=jnp.int32)[None, :]).astype(
        jnp.int32
    )
    before = jnp.tri(assign, k=-1, dtype=jnp.bfloat16)
    earlier = jnp.dot(
        before, onehot.astype(jnp.bfloat16), preferred_element_type=jnp.float32
    ).astype(jnp.int32)
    slot_rank = jnp.sum(earlier * onehot, axis=1)
    slot_index = expert_ids * capacity + slot_rank
    source_token = jnp.arange(assign, dtype=jnp.int32) // TOPK
    slot_token = jnp.zeros((expert_count * capacity,), jnp.int32).at[slot_index].set(source_token)
    slot_used = jnp.zeros((expert_count * capacity,), jnp.bfloat16).at[slot_index].set(1.0)
    outgoing = (normed[slot_token] * slot_used[:, None]).reshape(
        device_count, experts_local, capacity, D
    )
    incoming = lax.all_to_all(outgoing, ("seq", "role"), split_axis=0, concat_axis=0, tiled=True)
    gate_hidden = jnp.einsum(
        "sjcd,jdf->sjcf", incoming, gate_weight, preferred_element_type=jnp.float32
    )
    up_hidden = jnp.einsum(
        "sjcd,jdf->sjcf", incoming, up_weight, preferred_element_type=jnp.float32
    )
    activated = (jax.nn.silu(gate_hidden) * up_hidden).astype(jnp.bfloat16)
    returned = lax.all_to_all(
        jnp.einsum(
            "sjcf,jfd->sjcd", activated, down_weight, preferred_element_type=jnp.float32
        ).astype(jnp.bfloat16),
        ("seq", "role"),
        split_axis=0,
        concat_axis=0,
        tiled=True,
    )
    gathered = returned.reshape(expert_count * capacity, D)[slot_index]
    weighted = gathered.astype(jnp.float32) * gate_values[:, None]
    expert_sum = jnp.sum(weighted.reshape(-1, TOPK, D), axis=1)
    return (hidden + expert_sum).astype(jnp.bfloat16).reshape(residual.shape)


MESH = pl.DeviceIdType.MESH
LANES = 128
LAGS = (3, 3)
WO_CHUNKS = 8
WO_FIRST = 3
WO_ATTEND = ((3, 3),)
WO_END = ((0, 4), (1, 0), (1, 1), (1, 2), (0, 5), (0, 6), (1, 3), (0, 7), (1, 4), (1, 5), (1, 6), (1, 7))
WO_MIDDLE = {
    0: ((0, 4), (1, 0), (1, 1), (1, 2), (0, 5)),
    1: ((0, 6), (1, 3)),
    2: ((0, 7), (1, 4)),
    3: ((1, 5),),
    4: ((1, 6),),
    5: ((1, 7),),
}


def aligned(index, size):
    return pl.ds(pl.multiple_of(index * size, size), size)


SCALE_LANE = 32


def layer_kernel(
    roles,
    seqs,
    q_hbm,
    k_hbm,
    v_hbm,
    wo_hbm,
    res_hbm,
    gain_hbm,
    ids_hbm,
    gates_hbm,
    gw_hbm,
    uw_hbm,
    dw_hbm,
    out_ref,
    q,
    kv,
    wo,
    res,
    gain,
    ids,
    gates,
    gw,
    uw,
    dw,
    att,
    gains,
    base,
    part,
    from_end,
    from_mid,
    from_mate,
    tok,
    tab,
    act,
    y,
    y_core,
    y_x,
    y_line,
    final,
    load_sem,
    own_sem,
    kv1_s,
    kv1_r,
    kv2_s,
    kv2_r,
    wm_s,
    wm_r,
    wx_s,
    wx_r,
    wy_s,
    wy_r,
    tb_s,
    tb_r,
    ln_s,
    ln_r,
    mm_s,
    mm_r,
    tx_s,
    tx_r,
    tc_s,
    tc_r,
    yc_s,
    yc_r,
    yx_s,
    yx_r,
    yz_s,
    yz_r,
):
    s = lax.axis_index("seq")
    r = lax.axis_index("role")
    g = lax.axis_index("groups")
    mate = s + 1 - 2 * (s % 2)
    side = (s + 2) % 4
    far = mate + 2 - 4 * (mate // 2)
    batch, rows, width = q.shape
    heads = width // HEAD_WIDTH
    own_keys = k_hbm.shape[1]
    full = rows * seqs
    cols = wo.shape[2]
    depth = cols * seqs
    offs = (1, 2, 3)
    chunks = WO_CHUNKS
    chunk_rows = width // (2 * chunks)
    middle = (r + 1) // 2 % 2
    inner = r + 1 - 2 * (r // 2)
    outer = r - 1 + 2 * (r // 2)
    other = 3 - r

    def role_of(i):
        return (r // 2 + i // 2) % 2 * 2 + (r + i) % 2

    def turn(i):
        return (i + roles - 1) % roles

    def order(i):
        swap = (1 - r // (roles - 1)) * (1 - (i % 3 + 1) // 2)
        return middle * turn(i) + (1 - middle) * (i + swap * (3 - 2 * i))

    def column(n):
        return (s // 2 + n // 2) % 2 * 2 + (s + n) % 2

    def remote(src, dst, ssem, rsem, device):
        return pltpu.make_async_remote_copy(
            src_ref=src,
            dst_ref=dst,
            send_sem=ssem,
            recv_sem=rsem,
            device_id=device,
            device_id_type=MESH,
        )

    def to_role(off):
        return {"role": role_of(off)}

    barrier = pltpu.get_barrier_semaphore()
    for off in offs:
        pl.semaphore_signal(barrier, inc=1, device_id=to_role(off), device_id_type=MESH)
    for peer in ({"seq": mate}, {"seq": side}, {"groups": 1 - g}):
        pl.semaphore_signal(barrier, inc=1, device_id=peer, device_id_type=MESH)

    loads = [
        pltpu.make_async_copy(a, b, load_sem.at[i])
        for i, (a, b) in enumerate(
            (
                (q_hbm, q),
                (res_hbm, res),
                (gain_hbm, gain),
                (ids_hbm, ids),
                (gates_hbm, gates),
                (wo_hbm, wo.at[s]),
                (gw_hbm, gw),
                (uw_hbm, uw),
                (dw_hbm, dw),
            )
        )
    ]
    pair = (k_hbm, v_hbm)

    def kv_spot(t, seq, role):
        return kv.at[t, :, aligned(seq * roles + role, own_keys), :]

    owns = [
        pltpu.make_async_copy(
            pair[t].at[:, :, aligned(r, HEAD_WIDTH)], kv_spot(t, s, r), own_sem.at[t]
        )
        for t in range(2)
    ]
    for copy in owns + loads[:6]:
        copy.start()

    for copy in loads[1:5]:
        copy.wait()
    half_lanes = LANES // 2
    place = lax.broadcasted_iota(jnp.int32, (LANES, rows), 0)
    table = jnp.zeros((LANES, rows), jnp.float32)
    for k in range(ids.shape[1]):
        chosen = place % half_lanes == ids[0, k : k + 1, :]
        table = table + jnp.where(chosen, gates[0, k : k + 1, :], 0.0)
    high = table.astype(jnp.bfloat16).astype(jnp.float32)
    parts = jnp.where(place < half_lanes, high, table - high).astype(jnp.bfloat16)
    unit = (
        lax.broadcasted_iota(jnp.int32, (rows, rows), 0)
        == lax.broadcasted_iota(jnp.int32, (rows, rows), 1)
    )
    tab[r, aligned(s, rows), :] = lax.dot_general(
        jnp.where(unit, 1.0, 0.0).astype(jnp.bfloat16),
        parts,
        (((1,), (1,)), ((), ())),
        preferred_element_type=jnp.float32,
    ).astype(jnp.bfloat16)
    base[...] = jnp.zeros_like(base)
    for j in range(seqs):
        block = pl.ds(j * cols, cols)
        gains[0, j] = gain[:, block]
        gains[1, j] = 1.0 / gain[:, block]
        base[j, aligned(r, rows), :] = res[0, :, block]

    pl.semaphore_wait(barrier, roles - 1 + 3)

    def kv1(t, off):
        return remote(
            pair[t].at[:, :, aligned(role_of(off), HEAD_WIDTH)],
            kv_spot(t, s, r),
            kv1_s.at[0],
            kv1_r.at[0],
            to_role(off),
        )

    def tb(off):
        spot = tab.at[r, aligned(s, rows), :]
        return remote(spot, spot, tb_s.at[0], tb_r.at[0], to_role(off))

    def sent(ref, sem):
        remote(ref, ref, sem, sem, {"seq": mate}).wait_send()

    def landed(ref, sem):
        remote(ref, ref, sem, sem, {"seq": mate}).wait_recv()

    for off in offs:
        for t in range(2):
            kv1(t, off).start()

    def kv2(path, seq, target, b):
        spot = kv.at[:, b, aligned(seq, rows), :]
        return remote(spot, spot, kv2_s.at[0], kv2_r.at[path, b], {"seq": target})

    def wo_part(seq, n):
        return wo.at[seq, aligned(n, chunk_rows), :]

    def wo_own(seq):
        return remote(wo.at[seq], wo.at[seq], wm_s.at[0], wm_r.at[0], {"seq": mate})

    def wo_x(seq, c):
        spot = wo_part(seq, g * chunks + c)
        return remote(spot, spot, wx_s.at[0], wx_r.at[c], {"seq": side})

    def wo_y(half, c):
        spot = wo_part(side, half * chunks + c)
        return remote(spot, spot, wy_s.at[0], wy_r.at[c], {"groups": 1 - g})

    def wo_mate(seq, half, c):
        spot = wo_part(seq, half * chunks + c)
        return remote(spot, spot, wm_s.at[1], wm_r.at[1], {"seq": mate})

    def wo_pass(c):
        wo_x(side, c).wait_recv()
        wo_y(g, c).start()
        wo_mate(side, g, c).start()

    def wo_turn(c):
        wo_y(1 - g, c).wait_recv()
        wo_mate(side, 1 - g, c).start()

    loads[5].wait()
    for c in range(WO_FIRST):
        wo_x(s, c).start()
    wo_own(s).start()
    for off in offs:
        tb(off).start()
    for copy in loads[6:]:
        copy.start()
    for copy in owns:
        copy.wait()
    landed(kv.at[:, :, 0 : own_keys * (roles - 1)], kv1_r.at[0])
    for path, target in ((1, side), (0, mate)):
        for i in range(batch):
            kv2(path, s, target, turn(i)).start()
    for c in range(WO_FIRST, chunks):
        wo_x(s, c).start()
    loads[0].wait()
    for c in range(WO_FIRST):
        wo_pass(c)

    def kv_relay(i):
        kv2(1, side, side, turn(i)).wait_recv()
        kv2(2, side, mate, turn(i)).start()

    kv_relay(0)

    half_steps = 2 * roles
    steps = 2 * half_steps

    def spot_of(k):
        late = k // half_steps
        m = k % half_steps
        early_col, early_turn = m // roles, m % roles
        late_col, late_turn = 2 + m % 2, m // 2
        n = (1 - late) * early_col + late * late_col
        return column(n), turn((1 - late) * early_turn + late * late_turn)

    def part_of(k):
        j, b = spot_of(k)
        return part.at[j, aligned(b, rows), :]

    def em(k):
        j, b = spot_of(k)
        return remote(part_of(k), from_end.at[j, b], ln_s.at[0], ln_r.at[k], {"role": inner})

    def em_in(k):
        j, b = spot_of(k)
        return remote(part_of(k), from_end.at[j, b], ln_s.at[0], ln_r.at[k], {"role": outer})

    def mm(k):
        j, b = spot_of(k)
        return remote(part_of(k), from_mid.at[j, b], mm_s.at[0], mm_r.at[k], {"role": other})

    def piece(j, b, seq):
        return tok.at[b, j, aligned(seq, rows), :]

    def me(k):
        j, b = spot_of(k)
        return remote(piece(j, b, s), piece(j, b, s), ln_s.at[0], ln_r.at[k], {"role": outer})

    def me_in(k):
        j, b = spot_of(k)
        return remote(piece(j, b, s), piece(j, b, s), ln_s.at[0], ln_r.at[k], {"role": inner})

    def table_of(b, seq):
        return tab.at[b, aligned(seq, rows), :]

    def tx(j, b, seq):
        return remote(
            piece(j, b, seq), piece(j, b, seq), tx_s.at[0], tx_r.at[j, b], {"seq": side}
        )

    def tx_table(j, b, seq):
        spot = table_of(b, seq)
        return remote(spot, spot, tx_s.at[1], tx_r.at[j, b], {"seq": side})

    def tc(j, b, seq):
        spot = piece(j, b, seq)
        return remote(spot, spot, tc_s.at[0], tc_r.at[b], {"seq": mate})

    def tc_table(b, seq):
        spot = table_of(b, seq)
        return remote(spot, spot, tc_s.at[1], tc_r.at[b], {"seq": mate})

    table_rows = rows * LANES // cols
    with_table_bytes = from_mate.at[0 : rows + table_rows]
    sequence_bytes = from_mate.at[...]

    def when(condition, body):
        if isinstance(condition, bool):
            if condition:
                body()
        else:
            pl.when(condition)(body)

    def is_last(k):
        if isinstance(k, int):
            return k >= half_steps and k % 2 == 1
        return jnp.logical_and(k >= half_steps, k % 2 == 1)

    lane = lax.broadcasted_iota(jnp.int32, (rows, LANES), 1)

    def spread(k):
        j, b = spot_of(k)
        tx(j, b, s).start()
        tc(j, b, s).start()

        def with_table():
            square = jnp.zeros((rows, 1), jnp.float32)
            for c in range(seqs):
                value = tok[b, c, aligned(s, rows), :].astype(jnp.float32) * gains[1, c]
                square = square + jnp.sum(value * value, axis=1, keepdims=True)
            scale = lax.rsqrt(square / depth + epsilon)
            top = scale.astype(jnp.bfloat16).astype(jnp.float32)
            old = tab[b, aligned(s, rows), :].astype(jnp.float32)
            fresh = jnp.where(
                lane == SCALE_LANE,
                top,
                jnp.where(lane == SCALE_LANE + half_lanes, scale - top, old),
            )
            tab[b, aligned(s, rows), :] = fresh.astype(jnp.bfloat16)
            tx_table(j, b, s).start()
            tc_table(b, s).start()

        when(is_last(k), with_table)

    def relay(k):
        j, b = column_from(side, k), spot_of(k)[1]

        def plain():
            tx(j, b, side).wait_recv()
            tc(j, b, side).start()

        def with_table():
            landed(with_table_bytes, tx_r.at[j, b])
            tc(j, b, side).start()
            tc_table(b, side).start()

        if isinstance(k, int):
            (with_table if is_last(k) else plain)()
        else:
            pl.when(is_last(k))(with_table)
            pl.when(jnp.logical_not(is_last(k)))(plain)

    def column_from(seq, k):
        late = k // half_steps
        m = k % half_steps
        n = (1 - late) * (m // roles) + late * (2 + m % 2)
        return (seq // 2 + n // 2) % 2 * 2 + (seq + n) % 2

    def pair_up(k):
        em_in(k).wait_recv()
        j, b = spot_of(k)
        spot = aligned(b, rows)
        part[j, spot, :] = (
            part[j, spot, :].astype(jnp.float32) + from_end[j, b].astype(jnp.float32)
        ).astype(jnp.bfloat16)
        mm(k).start()

    def complete(k):
        mm(k).wait_recv()
        j, b = spot_of(k)
        total = part[j, aligned(b, rows), :].astype(jnp.float32) + from_mid[j, b].astype(
            jnp.float32
        )
        tok[b, j, aligned(s, rows), :] = (total * gains[0, j]).astype(jnp.bfloat16)
        me(k).start()
        spread(k)

    query_row = s * rows + lax.broadcasted_iota(jnp.int32, (rows, full), 0)
    allowed = lax.broadcasted_iota(jnp.int32, (rows, full), 1) <= query_row
    allowed = jnp.concatenate([allowed] * heads, axis=0)

    def attend(i, carry):
        b = turn(i)

        @pl.when(i < batch - 1)
        def _():
            kv_relay(i + 1)

        kv2(0, mate, mate, b).wait_recv()
        kv2(2, far, mate, b).wait_recv()
        stacked = jnp.concatenate(
            [q[b, :, h * HEAD_WIDTH : (h + 1) * HEAD_WIDTH] for h in range(heads)], axis=0
        )
        scores = lax.dot_general(
            stacked, kv[0, b], (((1,), (1,)), ((), ())), preferred_element_type=jnp.float32
        ) * (HEAD_WIDTH**-0.5)
        scores = jnp.where(allowed, scores, masked_score)
        weights = jnp.exp(scores - jnp.max(scores, axis=1, keepdims=True))
        totals = jnp.sum(weights, axis=1, keepdims=True)
        mixed = jnp.dot(
            weights.astype(jnp.bfloat16), kv[1, b], preferred_element_type=jnp.float32
        )
        mixed = (mixed / totals).astype(jnp.bfloat16)
        spot = aligned(b, rows)
        for h in range(heads):
            att[spot, h * HEAD_WIDTH : (h + 1) * HEAD_WIDTH] = mixed[h * rows : (h + 1) * rows]
        product = jnp.dot(att[spot, :], wo[s], preferred_element_type=jnp.float32)
        part[s, spot, :] = (product + base[s, spot, :].astype(jnp.float32)).astype(jnp.bfloat16)

        @pl.when(middle == 0)
        def _():
            em(i).start()

        for at, c in WO_ATTEND:

            @pl.when(i == at)
            def _():
                wo_pass(c)

        return carry

    def project(j):
        product = jnp.dot(att[...], wo[j], preferred_element_type=jnp.float32)
        part[j] = (product + base[j].astype(jnp.float32)).astype(jnp.bfloat16)

    lax.fori_loop(0, batch, attend, 0)
    wo_own(mate).wait_recv()
    project(mate)
    others = tab.at[0 : roles - 1, 0:rows]
    landed(others, tb_r.at[0])
    sent(others, tb_s.at[0])

    lag, relay_lag = LAGS

    def wo_finish():
        landed(wo.at[far], wm_r.at[1])
        project(side)
        project(far)

    held = steps - lag
    @pl.when(middle == 0)
    def _():
        for k in range(roles, half_steps):
            em(k).start()
        for relay_wo, c in WO_END:
            (wo_turn if relay_wo else wo_pass)(c)
        wo_finish()
        for k in range(half_steps, steps):
            em(k).start()

        def step(k, carry):
            me_in(k).wait_recv()
            spread(k)

            @pl.when(k >= relay_lag)
            def _():
                relay(k - relay_lag)

            return carry

        lax.fori_loop(0, steps - lag, step, 0)

        @pl.when(r > 0)
        def _():
            for k in range(steps - lag - relay_lag, steps - lag - relay_lag + 2):
                relay(k)

    @pl.when(middle == 1)
    def _():
        def step(k):
            if isinstance(k, int):
                pair_up(k)
            else:
                when(k < steps, lambda: pair_up(k))
            when(k >= lag, lambda: complete(k - lag))
            when(k >= lag + relay_lag, lambda: relay(k - lag - relay_lag))

        for k in range(half_steps):
            for relay_wo, c in WO_MIDDLE.get(k, ()):
                (wo_turn if relay_wo else wo_pass)(c)
            step(k)
        wo_finish()

        def late_step(k, carry):
            step(k)
            return carry

        lax.fori_loop(half_steps, steps, late_step, 0)

    for copy in loads[6:]:
        copy.wait()

    expert = s * roles + r
    hidden_width = act.shape[1]
    step_f = hidden_width // 3 if hidden_width % 3 == 0 else hidden_width
    table_lane = lax.broadcasted_iota(jnp.int32, (full, LANES), 1) % half_lanes

    def yc(b, j, path):
        seq = far if path else mate
        return remote(
            y.at[b, j, aligned(seq, rows), :],
            y_core.at[b, j, path],
            yc_s.at[0],
            yc_r.at[b, j * path + seqs * (1 - path)],
            {"seq": mate},
        )

    def yx(b, j):
        return remote(
            y.at[b, j, aligned(side, rows), :],
            y_x.at[b, j],
            yx_s.at[0],
            yx_r.at[b, j],
            {"seq": side},
        )

    def slot(way, b, at):
        own = way * (1 - ((at - b) * way + roles - 2) // (roles - 1))
        return b * (1 - own) + roles * own

    def yz(way, b, j, to):
        place_there = slot(way, b, to)
        return remote(
            y.at[b, j, aligned(s, rows), :],
            y_line.at[place_there, j],
            yz_s.at[0],
            yz_r.at[place_there, j],
            {"role": to},
        )

    def yz_in(way, b, j):
        here = slot(way, b, r)
        landed(y_line.at[here, j], yz_r.at[here, j])
        return y_line[here, j].astype(jnp.float32)

    def pass_core(b, j):
        yc(b, j, 1).wait_recv()
        spot = aligned(side, rows)
        y[b, j, spot, :] = (
            y[b, j, spot, :].astype(jnp.float32) + y_core[b, j, 1].astype(jnp.float32)
        ).astype(jnp.bfloat16)
        yx(b, j).start()

    def summed(b, j):
        if j == 0:
            landed(y_core.at[b, :, 0], yc_r.at[b, seqs])
        yx(b, j).wait_recv()
        return (
            y[b, j, aligned(s, rows), :].astype(jnp.float32)
            + y_core[b, j, 0].astype(jnp.float32)
            + y_x[b, j].astype(jnp.float32)
        )

    def hop(b, j):
        for way in range(2):

            @pl.when(b > r if way == 0 else b < r)
            def _():
                final[...] = summed(b, j)

                @pl.when(r > 0 if way == 0 else r < roles - 1)
                def _():
                    final[...] = final[...] + yz_in(way, b, j)

                y[b, j, aligned(s, rows), :] = final[...].astype(jnp.bfloat16)
                yz(way, b, j, r + 1 - 2 * way).start()

    def relay_first(k):
        @pl.when(r == 0)
        def _():
            relay(k)

    def early_hop(n):
        hop(order(n // seqs), n % seqs)

    def arrive_end(k):
        me_in(k).wait_recv()
        spread(k)

    late_middle = {
        (0, 0): ((complete, 13), (relay, 10)),
        (0, 2): ((complete, 14), (relay, 11)),
        (0, 11): ((complete, 15),),
        (0, 3): ((relay, 12),),
        (1, 2): ((relay, 13),),
        (1, 3): ((relay, 14),),
        (2, 0): ((relay, 15),),
    }
    late_end = {
        (0, 0): ((arrive_end, 13), (relay_first, 10)),
        (0, 2): ((arrive_end, 14), (relay_first, 11)),
        (0, 11): ((arrive_end, 15),),
        (0, 3): ((relay, 12),),
        (0, 4): ((relay, 13),),
        (1, 2): ((relay, 14), (relay, 15)),
        (1, 3): ((early_hop, 0), (early_hop, 1)),
        (2, 0): ((early_hop, 2),),
        (2, 2): ((early_hop, 3),),
        (2, 3): ((early_hop, 4),),
        (3, 0): ((early_hop, 5),),
        (3, 2): ((early_hop, 6),),
        (3, 3): ((early_hop, 7),),
    }

    def late(i, at):
        for here, plan in ((1, late_middle), (0, late_end)):
            for (block, place_in), jobs in plan.items():
                if place_in == at:

                    @pl.when(jnp.logical_and(i == block, middle == here))
                    def _():
                        for job, k in jobs:
                            job(k)

    def one_block(i, carry):
        b = order(i)
        landed(sequence_bytes, tc_r.at[b])
        shares = tab[b].astype(jnp.float32)
        share = jnp.sum(jnp.where(table_lane == expert, shares, 0.0), axis=1, keepdims=True)
        scale = jnp.sum(jnp.where(table_lane == SCALE_LANE, shares, 0.0), axis=1, keepdims=True)
        inputs = jnp.concatenate([tok[b, j] for j in range(seqs)], axis=1)
        for start in range(0, hidden_width, step_f):
            block = pl.ds(start, step_f)
            gate = jnp.dot(inputs, gw[0, :, block], preferred_element_type=jnp.float32) * scale
            up = jnp.dot(inputs, uw[0, :, block], preferred_element_type=jnp.float32) * scale
            act[:, block] = (gate / (1.0 + jnp.exp(-gate)) * up).astype(jnp.bfloat16)
            if start == 0:

                @pl.when(i > 1)
                def _():
                    for j in range(seqs):
                        pass_core(order(i - 1), j)

                late(i, 0)

        late(i, 2)
        for j in range(seqs):
            block = pl.ds(j * cols, cols)
            product = jnp.dot(act[...], dw[0, :, block], preferred_element_type=jnp.float32)
            y[b, j] = (product * share).astype(jnp.bfloat16)
            yc(b, j, 1).start()
            yc(b, j, 0).start()
            if j > 1:

                @pl.when(i == 0)
                def _():
                    pass_core(b, j - 2)

            late(i, 10 + j)
        late(i, 3)

        @pl.when(i == 0)
        def _():
            for j in range(2, seqs):
                pass_core(b, j)

        late(i, 4)
        return carry

    lax.fori_loop(0, roles, one_block, 0)
    for j in range(seqs):
        pass_core(order(roles - 1), j)

    sent(tok.at[0], wm_s.at[1])
    sent(wo.at[0], wm_s.at[0])
    half_wo = wo.at[0, 0 : width // 2]
    sent(half_wo, wx_s.at[0])
    sent(half_wo, wy_s.at[0])
    sent(from_end, tx_s.at[0])
    sent(y_core, tc_s.at[0])
    sent(tab.at[:, 0:rows], tx_s.at[1])
    sent(tab.at[:, 0 : 2 * rows], tc_s.at[1])
    sent(kv.at[:, :, 0 : own_keys * (roles - 1)], kv1_s.at[0])
    sent(kv.at[:, :, 0 : 3 * rows], kv2_s.at[0])

    @pl.when(middle == 0)
    def _():
        sent(from_end, ln_s.at[0])

        for j in range(seqs):
            hop(order(roles - 2), j)

    @pl.when(middle == 1)
    def _():
        sent(from_end, mm_s.at[0])
        sent(from_end, ln_s.at[0])
        for b in ((2 - r) * (roles - 1), (r - 1) * (roles - 1), other):
            for j in range(seqs):
                hop(b, j)

    sent(y_core, yc_s.at[0])
    sent(y_x, yx_s.at[0])
    for j in range(seqs):
        final[...] = summed(r, j) + tok[r, j, aligned(s, rows), :].astype(jnp.float32) * gains[1, j]
        for way in range(2):

            @pl.when(r > 0 if way == 0 else r < roles - 1)
            def _():
                final[...] = final[...] + yz_in(way, r, j)

        out_ref[0, :, j * cols : (j + 1) * cols] = final[...].astype(out_ref.dtype)
    sent(y_x.at[0 : roles - 1], yz_s.at[0])


def fused(
    query_rows,
    encoded_key_rows,
    value_matrix_rows,
    output_weight,
    residual,
    norm_gain,
    route_experts,
    route_gates,
    gate_weight,
    up_weight,
    down_weight,
):
    seqs, roles = lax.axis_size("seq"), lax.axis_size("role")
    batch, rows, width = query_rows.shape
    depth, cols = residual.shape[2], output_weight.shape[1]
    hidden_width = gate_weight.shape[2]
    full = rows * seqs
    bf16, f32 = jnp.bfloat16, jnp.float32
    gain = norm_gain.reshape(1, depth)
    route_experts = route_experts.transpose(0, 2, 1)
    route_gates = route_gates.transpose(0, 2, 1)
    vmem = [
        pltpu.VMEM(query_rows.shape, bf16),
        pltpu.VMEM((2, batch, full, HEAD_WIDTH), bf16),
        pltpu.VMEM((seqs, width, cols), bf16),
        pltpu.VMEM(residual.shape, bf16),
        pltpu.VMEM(gain.shape, f32),
        pltpu.VMEM(route_experts.shape, jnp.int32),
        pltpu.VMEM(route_gates.shape, f32),
        pltpu.VMEM(gate_weight.shape, bf16),
        pltpu.VMEM(up_weight.shape, bf16),
        pltpu.VMEM(down_weight.shape, bf16),
        pltpu.VMEM((batch * rows, width), bf16),
        pltpu.VMEM((2, seqs, 1, cols), f32),
        pltpu.VMEM((seqs, batch * rows, cols), bf16),
        pltpu.VMEM((seqs, batch * rows, cols), bf16),
        pltpu.VMEM((seqs, batch, rows, cols), bf16),
        pltpu.VMEM((seqs, batch, rows, cols), bf16),
        pltpu.VMEM((2 * (full + rows * LANES // cols), cols), bf16),
        pltpu.VMEM((roles, seqs, full, cols), bf16),
        pltpu.VMEM((roles, full, LANES), bf16),
        pltpu.VMEM((full, hidden_width), bf16),
        pltpu.VMEM((roles, seqs, full, cols), bf16),
        pltpu.VMEM((roles, seqs, 2, rows, cols), bf16),
        pltpu.VMEM((roles, seqs, rows, cols), bf16),
        pltpu.VMEM((roles + 1, seqs, rows, cols), bf16),
        pltpu.VMEM((rows, cols), f32),
    ]
    dma = pltpu.SemaphoreType.DMA
    steps = seqs * roles
    chunks = WO_CHUNKS
    counts = [(1,)] * 3 + [(3, batch)] + [(2,)] * 2 + [(1,), (chunks,)] * 2 + [(1,)] * 2
    counts += [(1,), (steps,)] * 2 + [(2,), (seqs, roles), (2,), (roles,)]
    counts += [(1,), (roles, seqs + 1), (1,), (roles, seqs), (1,), (roles + 1, seqs)]
    return pl.pallas_call(
        partial(layer_kernel, roles, seqs),
        out_shape=pltpu.VMEM(residual.shape, bf16),
        in_specs=[pl.BlockSpec(memory_space=pl.ANY)] * 11,
        out_specs=pl.BlockSpec(memory_space=pltpu.VMEM),
        scratch_shapes=vmem + [dma((9,)), dma((2,))] + [dma(count) for count in counts],
        compiler_params=pltpu.CompilerParams(
            collective_id=0, has_side_effects=True, vmem_limit_bytes=60 * 1024 * 1024
        ),
    )(
        query_rows,
        encoded_key_rows,
        value_matrix_rows,
        output_weight,
        residual,
        gain,
        route_experts,
        route_gates,
        gate_weight,
        up_weight,
        down_weight,
    )


def solution(mesh):
    square = mesh.shape["seq"] == 4 and mesh.shape["role"] == 4 and mesh.shape["groups"] == 2
    body = fused if square else shards
    placed = (
        P("groups", "seq", "role"),
        P("groups", ("seq", "role"), None),
        P("groups", ("seq", "role"), None),
        P("role", "seq"),
        P(("groups", "role"), "seq", None),
        P(),
        P(("groups", "role"), "seq", None),
        P(("groups", "role"), "seq", None),
        P(("seq", "role"), None, None),
        P(("seq", "role"), None, None),
        P(("seq", "role"), None, None),
    )
    return jax.shard_map(
        body,
        mesh=mesh,
        in_specs=placed,
        out_specs=P(("groups", "role"), "seq", None),
        check_vma=False,
    )
```

```python
from functools import partial

import jax
import jax.numpy as jnp
from jax import lax
from jax.experimental import pallas as pl
from jax.experimental.pallas import tpu as pltpu
from jax.sharding import PartitionSpec as P

D = 2048
QUERY_HEADS = 32
KEY_VALUE_HEADS = 4
HEAD_WIDTH = 128
TOPK = 8


epsilon = 1e-06
masked_score = -1e30


def score_block(queries, every_key, query_position, block_start, block_width, score_scale):
    keys_part = lax.slice_in_dim(every_key, block_start, block_start + block_width, axis=0)
    raw_scores = (
        jnp.einsum("qhd,kd->hqk", queries, keys_part, preferred_element_type=jnp.float32)
        * score_scale
    )
    key_position = block_start + jnp.arange(block_width, dtype=jnp.int32)
    return jnp.where(
        key_position[None, None, :] <= query_position[None, :, None], raw_scores, masked_score
    )


def value_block(rounded, every_value, block_start, block_width):
    prob_block = lax.slice_in_dim(rounded, block_start, block_start + block_width, axis=2)
    values_part = lax.slice_in_dim(every_value, block_start, block_start + block_width, axis=0)
    return jnp.einsum("hqk,kd->qhd", prob_block, values_part, preferred_element_type=jnp.float32)


def shards(
    query_rows,
    encoded_key_rows,
    value_matrix_rows,
    output_weight,
    residual,
    norm_gain,
    route_experts,
    route_gates,
    gate_weight,
    up_weight,
    down_weight,
):
    seq_count = lax.axis_size("seq")
    role_count = lax.axis_size("role")
    seq_index = lax.axis_index("seq")
    role_index = lax.axis_index("role")
    batch_count = query_rows.shape[0]
    local_length = query_rows.shape[1]
    local_heads = query_rows.shape[2] // HEAD_WIDTH
    full_length = local_length * seq_count
    query_group_width = QUERY_HEADS // KEY_VALUE_HEADS
    head_pick = role_index * local_heads // query_group_width
    role_keys, role_values = (
        lax.all_gather(encoded_key_rows, "role", axis=1, tiled=True),
        lax.all_gather(value_matrix_rows, "role", axis=1, tiled=True),
    )
    head_keys = lax.dynamic_slice_in_dim(role_keys, head_pick * HEAD_WIDTH, HEAD_WIDTH, 2)
    head_values = lax.dynamic_slice_in_dim(role_values, head_pick * HEAD_WIDTH, HEAD_WIDTH, 2)
    whole_keys, whole_values, whole_proj = (
        lax.all_gather(head_keys, "seq", axis=1, tiled=True),
        lax.all_gather(head_values, "seq", axis=1, tiled=True),
        lax.all_gather(output_weight, "seq", axis=1, tiled=True),
    )
    key_width = full_length // 8
    score_scale = HEAD_WIDTH ** (-0.5)
    query_position = seq_index * local_length + jnp.arange(local_length, dtype=jnp.int32)
    last_needed = (seq_index + 1) * local_length

    def one_sequence(operands):
        own_queries, every_key, every_value = operands
        queries = own_queries.reshape(local_length, local_heads, HEAD_WIDTH)
        pieces = []
        for number in range(8):
            block_start = number * key_width
            compute = partial(
                score_block, queries, every_key, query_position, block_start, key_width, score_scale
            )
            skipped = partial(
                jnp.full, (local_heads, local_length, key_width), masked_score, jnp.float32
            )
            pieces.append(lax.cond(block_start < last_needed, compute, skipped))
        scores = jnp.concatenate(pieces, axis=2)
        row_peak = jnp.max(scores, axis=2, keepdims=True)
        weights = jnp.exp(scores - row_peak)
        totals = jnp.sum(weights, axis=2, keepdims=True)
        rounded = weights.astype(jnp.bfloat16)
        mixed_rows = jnp.zeros((local_length, local_heads, HEAD_WIDTH), jnp.float32)
        for number in range(8):
            block_start = number * key_width
            product = partial(value_block, rounded, every_value, block_start, key_width)
            nothing = partial(jnp.zeros, (local_length, local_heads, HEAD_WIDTH), jnp.float32)
            mixed_rows = mixed_rows + lax.cond(block_start < last_needed, product, nothing)
        attended = (mixed_rows / totals.transpose(1, 0, 2)).astype(jnp.bfloat16)
        return attended.reshape(local_length, local_heads * HEAD_WIDTH)

    attended = lax.map(one_sequence, (query_rows, whole_keys, whole_values))
    flat_attended = attended.reshape(batch_count * local_length, local_heads * HEAD_WIDTH)
    projected = lax.psum_scatter(
        jnp.dot(flat_attended, whole_proj, preferred_element_type=jnp.float32).astype(jnp.bfloat16),
        "role",
        scatter_dimension=0,
        tiled=True,
    ).astype(jnp.float32)
    hidden = residual[0].astype(jnp.float32) + projected
    variance = jnp.mean(hidden * hidden, axis=-1, keepdims=True)
    normed = (hidden * lax.rsqrt(variance + epsilon) * norm_gain).astype(jnp.bfloat16)
    expert_ids = route_experts.reshape(-1)
    gate_values = route_gates.reshape(-1)
    experts_local = gate_weight.shape[0]
    device_count = seq_count * role_count
    expert_count = experts_local * device_count
    assign = expert_ids.shape[0]
    capacity = assign // expert_count + 1
    onehot = (expert_ids[:, None] == jnp.arange(expert_count, dtype=jnp.int32)[None, :]).astype(
        jnp.int32
    )
    before = jnp.tri(assign, k=-1, dtype=jnp.bfloat16)
    earlier = jnp.dot(
        before, onehot.astype(jnp.bfloat16), preferred_element_type=jnp.float32
    ).astype(jnp.int32)
    slot_rank = jnp.sum(earlier * onehot, axis=1)
    slot_index = expert_ids * capacity + slot_rank
    source_token = jnp.arange(assign, dtype=jnp.int32) // TOPK
    slot_token = jnp.zeros((expert_count * capacity,), jnp.int32).at[slot_index].set(source_token)
    slot_used = jnp.zeros((expert_count * capacity,), jnp.bfloat16).at[slot_index].set(1.0)
    outgoing = (normed[slot_token] * slot_used[:, None]).reshape(
        device_count, experts_local, capacity, D
    )
    incoming = lax.all_to_all(outgoing, ("seq", "role"), split_axis=0, concat_axis=0, tiled=True)
    gate_hidden = jnp.einsum(
        "sjcd,jdf->sjcf", incoming, gate_weight, preferred_element_type=jnp.float32
    )
    up_hidden = jnp.einsum(
        "sjcd,jdf->sjcf", incoming, up_weight, preferred_element_type=jnp.float32
    )
    activated = (jax.nn.silu(gate_hidden) * up_hidden).astype(jnp.bfloat16)
    returned = lax.all_to_all(
        jnp.einsum(
            "sjcf,jfd->sjcd", activated, down_weight, preferred_element_type=jnp.float32
        ).astype(jnp.bfloat16),
        ("seq", "role"),
        split_axis=0,
        concat_axis=0,
        tiled=True,
    )
    gathered = returned.reshape(expert_count * capacity, D)[slot_index]
    weighted = gathered.astype(jnp.float32) * gate_values[:, None]
    expert_sum = jnp.sum(weighted.reshape(-1, TOPK, D), axis=1)
    return (hidden + expert_sum).astype(jnp.bfloat16).reshape(residual.shape)


MESH = pl.DeviceIdType.MESH
LANES = 128
LAGS = (3, 3)
WO_CHUNKS = 8
WO_FIRST = 4
WO_ATTEND = ((2, 4),)
WO_END = ((1, 0), (1, 1), (1, 2), (0, 5), (0, 6), (1, 3), (0, 7), (1, 4), (1, 5), (1, 6), (1, 7))
WO_MIDDLE = {
    0: ((1, 0), (1, 1), (1, 2), (0, 5)),
    1: ((0, 6), (1, 3)),
    2: ((0, 7), (1, 4)),
    3: ((1, 5),),
    4: ((1, 6),),
    5: ((1, 7),),
}


def aligned(index, size):
    return pl.ds(pl.multiple_of(index * size, size), size)


SCALE_LANE = 32


def layer_kernel(
    roles,
    seqs,
    q_hbm,
    k_hbm,
    v_hbm,
    wo_hbm,
    res_hbm,
    gain_hbm,
    ids_hbm,
    gates_hbm,
    gw_hbm,
    uw_hbm,
    dw_hbm,
    out_ref,
    q,
    kv,
    wo,
    res,
    gain,
    ids,
    gates,
    gw,
    uw,
    dw,
    att,
    gains,
    base,
    part,
    from_end,
    from_mid,
    from_mate,
    tok,
    tab,
    act,
    y,
    y_core,
    y_x,
    y_line,
    final,
    load_sem,
    own_sem,
    kv1_s,
    kv1_r,
    kv2_s,
    kv2_r,
    wm_s,
    wm_r,
    wx_s,
    wx_r,
    wy_s,
    wy_r,
    tb_s,
    tb_r,
    ln_s,
    ln_r,
    mm_s,
    mm_r,
    tx_s,
    tx_r,
    tc_s,
    tc_r,
    yc_s,
    yc_r,
    yx_s,
    yx_r,
    yz_s,
    yz_r,
):
    s = lax.axis_index("seq")
    r = lax.axis_index("role")
    g = lax.axis_index("groups")
    mate = s + 1 - 2 * (s % 2)
    side = (s + 2) % 4
    far = mate + 2 - 4 * (mate // 2)
    batch, rows, width = q.shape
    heads = width // HEAD_WIDTH
    own_keys = k_hbm.shape[1]
    full = rows * seqs
    cols = wo.shape[2]
    depth = cols * seqs
    offs = (1, 2, 3)
    chunks = WO_CHUNKS
    chunk_rows = width // (2 * chunks)
    middle = (r + 1) // 2 % 2
    inner = r + 1 - 2 * (r // 2)
    outer = r - 1 + 2 * (r // 2)
    other = 3 - r

    def role_of(i):
        return (r // 2 + i // 2) % 2 * 2 + (r + i) % 2

    def turn(i):
        return (i + roles - 1) % roles

    def order(i):
        swap = (1 - r // (roles - 1)) * (1 - (i % 3 + 1) // 2)
        return middle * turn(i) + (1 - middle) * (i + swap * (3 - 2 * i))

    def column(n):
        return (s // 2 + n // 2) % 2 * 2 + (s + n) % 2

    def remote(src, dst, ssem, rsem, device):
        return pltpu.make_async_remote_copy(
            src_ref=src,
            dst_ref=dst,
            send_sem=ssem,
            recv_sem=rsem,
            device_id=device,
            device_id_type=MESH,
        )

    def to_role(off):
        return {"role": role_of(off)}

    barrier = pltpu.get_barrier_semaphore()
    for off in offs:
        pl.semaphore_signal(barrier, inc=1, device_id=to_role(off), device_id_type=MESH)
    for peer in ({"seq": mate}, {"seq": side}, {"groups": 1 - g}):
        pl.semaphore_signal(barrier, inc=1, device_id=peer, device_id_type=MESH)

    loads = [
        pltpu.make_async_copy(a, b, load_sem.at[i])
        for i, (a, b) in enumerate(
            (
                (q_hbm, q),
                (res_hbm, res),
                (gain_hbm, gain),
                (ids_hbm, ids),
                (gates_hbm, gates),
                (wo_hbm, wo.at[s]),
                (gw_hbm, gw),
                (uw_hbm, uw),
                (dw_hbm, dw),
            )
        )
    ]
    pair = (k_hbm, v_hbm)

    def kv_spot(t, seq, role):
        return kv.at[t, :, aligned(seq * roles + role, own_keys), :]

    owns = [
        pltpu.make_async_copy(
            pair[t].at[:, :, aligned(r, HEAD_WIDTH)], kv_spot(t, s, r), own_sem.at[t]
        )
        for t in range(2)
    ]
    for copy in owns + loads[:6]:
        copy.start()

    for copy in loads[1:5]:
        copy.wait()
    half_lanes = LANES // 2
    place = lax.broadcasted_iota(jnp.int32, (LANES, rows), 0)
    table = jnp.zeros((LANES, rows), jnp.float32)
    for k in range(ids.shape[1]):
        chosen = place % half_lanes == ids[0, k : k + 1, :]
        table = table + jnp.where(chosen, gates[0, k : k + 1, :], 0.0)
    high = table.astype(jnp.bfloat16).astype(jnp.float32)
    parts = jnp.where(place < half_lanes, high, table - high).astype(jnp.bfloat16)
    unit = (
        lax.broadcasted_iota(jnp.int32, (rows, rows), 0)
        == lax.broadcasted_iota(jnp.int32, (rows, rows), 1)
    )
    tab[r, aligned(s, rows), :] = lax.dot_general(
        jnp.where(unit, 1.0, 0.0).astype(jnp.bfloat16),
        parts,
        (((1,), (1,)), ((), ())),
        preferred_element_type=jnp.float32,
    ).astype(jnp.bfloat16)
    base[...] = jnp.zeros_like(base)
    for j in range(seqs):
        block = pl.ds(j * cols, cols)
        gains[0, j] = gain[:, block]
        gains[1, j] = 1.0 / gain[:, block]
        base[j, aligned(r, rows), :] = res[0, :, block]

    pl.semaphore_wait(barrier, roles - 1 + 3)

    def kv1(t, off):
        return remote(
            pair[t].at[:, :, aligned(role_of(off), HEAD_WIDTH)],
            kv_spot(t, s, r),
            kv1_s.at[0],
            kv1_r.at[0],
            to_role(off),
        )

    def tb(off):
        spot = tab.at[r, aligned(s, rows), :]
        return remote(spot, spot, tb_s.at[0], tb_r.at[0], to_role(off))

    def sent(ref, sem):
        remote(ref, ref, sem, sem, {"seq": mate}).wait_send()

    def landed(ref, sem):
        remote(ref, ref, sem, sem, {"seq": mate}).wait_recv()

    for off in offs:
        for t in range(2):
            kv1(t, off).start()

    def kv2(path, seq, target, b):
        spot = kv.at[:, b, aligned(seq, rows), :]
        return remote(spot, spot, kv2_s.at[0], kv2_r.at[path, b], {"seq": target})

    def wo_part(seq, n):
        return wo.at[seq, aligned(n, chunk_rows), :]

    def wo_own(seq):
        return remote(wo.at[seq], wo.at[seq], wm_s.at[0], wm_r.at[0], {"seq": mate})

    def wo_x(seq, c):
        spot = wo_part(seq, g * chunks + c)
        return remote(spot, spot, wx_s.at[0], wx_r.at[c], {"seq": side})

    def wo_y(half, c):
        spot = wo_part(side, half * chunks + c)
        return remote(spot, spot, wy_s.at[0], wy_r.at[c], {"groups": 1 - g})

    def wo_mate(seq, half, c):
        spot = wo_part(seq, half * chunks + c)
        return remote(spot, spot, wm_s.at[1], wm_r.at[1], {"seq": mate})

    def wo_pass(c):
        wo_x(side, c).wait_recv()
        wo_y(g, c).start()
        wo_mate(side, g, c).start()

    def wo_turn(c):
        wo_y(1 - g, c).wait_recv()
        wo_mate(side, 1 - g, c).start()

    loads[5].wait()
    for c in range(WO_FIRST):
        wo_x(s, c).start()
    wo_own(s).start()
    for off in offs:
        tb(off).start()
    for copy in loads[6:]:
        copy.start()
    for copy in owns:
        copy.wait()
    landed(kv.at[:, :, 0 : own_keys * (roles - 1)], kv1_r.at[0])
    for path, target in ((1, side), (0, mate)):
        for i in range(batch):
            kv2(path, s, target, turn(i)).start()
    for c in range(WO_FIRST, chunks):
        wo_x(s, c).start()
    loads[0].wait()
    for c in range(WO_FIRST):
        wo_pass(c)

    def kv_relay(i):
        kv2(1, side, side, turn(i)).wait_recv()
        kv2(2, side, mate, turn(i)).start()

    kv_relay(0)

    half_steps = 2 * roles
    steps = 2 * half_steps

    def spot_of(k):
        late = k // half_steps
        m = k % half_steps
        early_col, early_turn = m // roles, m % roles
        late_col, late_turn = 2 + m % 2, m // 2
        n = (1 - late) * early_col + late * late_col
        return column(n), turn((1 - late) * early_turn + late * late_turn)

    def part_of(k):
        j, b = spot_of(k)
        return part.at[j, aligned(b, rows), :]

    def em(k):
        j, b = spot_of(k)
        return remote(part_of(k), from_end.at[j, b], ln_s.at[0], ln_r.at[k], {"role": inner})

    def em_in(k):
        j, b = spot_of(k)
        return remote(part_of(k), from_end.at[j, b], ln_s.at[0], ln_r.at[k], {"role": outer})

    def mm(k):
        j, b = spot_of(k)
        return remote(part_of(k), from_mid.at[j, b], mm_s.at[0], mm_r.at[k], {"role": other})

    def piece(j, b, seq):
        return tok.at[b, j, aligned(seq, rows), :]

    def me(k):
        j, b = spot_of(k)
        return remote(piece(j, b, s), piece(j, b, s), ln_s.at[0], ln_r.at[k], {"role": outer})

    def me_in(k):
        j, b = spot_of(k)
        return remote(piece(j, b, s), piece(j, b, s), ln_s.at[0], ln_r.at[k], {"role": inner})

    def table_of(b, seq):
        return tab.at[b, aligned(seq, rows), :]

    def tx(j, b, seq):
        return remote(
            piece(j, b, seq), piece(j, b, seq), tx_s.at[0], tx_r.at[j, b], {"seq": side}
        )

    def tx_table(j, b, seq):
        spot = table_of(b, seq)
        return remote(spot, spot, tx_s.at[1], tx_r.at[j, b], {"seq": side})

    def tc(j, b, seq):
        spot = piece(j, b, seq)
        return remote(spot, spot, tc_s.at[0], tc_r.at[b], {"seq": mate})

    def tc_table(b, seq):
        spot = table_of(b, seq)
        return remote(spot, spot, tc_s.at[1], tc_r.at[b], {"seq": mate})

    table_rows = rows * LANES // cols
    with_table_bytes = from_mate.at[0 : rows + table_rows]
    sequence_bytes = from_mate.at[...]

    def when(condition, body):
        if isinstance(condition, bool):
            if condition:
                body()
        else:
            pl.when(condition)(body)

    def is_last(k):
        if isinstance(k, int):
            return k >= half_steps and k % 2 == 1
        return jnp.logical_and(k >= half_steps, k % 2 == 1)

    lane = lax.broadcasted_iota(jnp.int32, (rows, LANES), 1)

    def spread(k):
        j, b = spot_of(k)
        tx(j, b, s).start()
        tc(j, b, s).start()

        def with_table():
            square = jnp.zeros((rows, 1), jnp.float32)
            for c in range(seqs):
                value = tok[b, c, aligned(s, rows), :].astype(jnp.float32) * gains[1, c]
                square = square + jnp.sum(value * value, axis=1, keepdims=True)
            scale = lax.rsqrt(square / depth + epsilon)
            top = scale.astype(jnp.bfloat16).astype(jnp.float32)
            old = tab[b, aligned(s, rows), :].astype(jnp.float32)
            fresh = jnp.where(
                lane == SCALE_LANE,
                top,
                jnp.where(lane == SCALE_LANE + half_lanes, scale - top, old),
            )
            tab[b, aligned(s, rows), :] = fresh.astype(jnp.bfloat16)
            tx_table(j, b, s).start()
            tc_table(b, s).start()

        when(is_last(k), with_table)

    def relay(k):
        j, b = column_from(side, k), spot_of(k)[1]

        def plain():
            tx(j, b, side).wait_recv()
            tc(j, b, side).start()

        def with_table():
            landed(with_table_bytes, tx_r.at[j, b])
            tc(j, b, side).start()
            tc_table(b, side).start()

        if isinstance(k, int):
            (with_table if is_last(k) else plain)()
        else:
            pl.when(is_last(k))(with_table)
            pl.when(jnp.logical_not(is_last(k)))(plain)

    def column_from(seq, k):
        late = k // half_steps
        m = k % half_steps
        n = (1 - late) * (m // roles) + late * (2 + m % 2)
        return (seq // 2 + n // 2) % 2 * 2 + (seq + n) % 2

    def pair_up(k):
        em_in(k).wait_recv()
        j, b = spot_of(k)
        spot = aligned(b, rows)
        part[j, spot, :] = (
            part[j, spot, :].astype(jnp.float32) + from_end[j, b].astype(jnp.float32)
        ).astype(jnp.bfloat16)
        mm(k).start()

    def complete(k):
        mm(k).wait_recv()
        j, b = spot_of(k)
        total = part[j, aligned(b, rows), :].astype(jnp.float32) + from_mid[j, b].astype(
            jnp.float32
        )
        tok[b, j, aligned(s, rows), :] = (total * gains[0, j]).astype(jnp.bfloat16)
        me(k).start()
        spread(k)

    query_row = s * rows + lax.broadcasted_iota(jnp.int32, (rows, full), 0)
    allowed = lax.broadcasted_iota(jnp.int32, (rows, full), 1) <= query_row
    allowed = jnp.concatenate([allowed] * heads, axis=0)

    def attend(i, carry):
        b = turn(i)

        @pl.when(i < batch - 1)
        def _():
            kv_relay(i + 1)

        kv2(0, mate, mate, b).wait_recv()
        kv2(2, far, mate, b).wait_recv()
        stacked = jnp.concatenate(
            [q[b, :, h * HEAD_WIDTH : (h + 1) * HEAD_WIDTH] for h in range(heads)], axis=0
        )
        scores = lax.dot_general(
            stacked, kv[0, b], (((1,), (1,)), ((), ())), preferred_element_type=jnp.float32
        ) * (HEAD_WIDTH**-0.5)
        scores = jnp.where(allowed, scores, masked_score)
        weights = jnp.exp(scores - jnp.max(scores, axis=1, keepdims=True))
        totals = jnp.sum(weights, axis=1, keepdims=True)
        mixed = jnp.dot(
            weights.astype(jnp.bfloat16), kv[1, b], preferred_element_type=jnp.float32
        )
        mixed = (mixed / totals).astype(jnp.bfloat16)
        spot = aligned(b, rows)
        for h in range(heads):
            att[spot, h * HEAD_WIDTH : (h + 1) * HEAD_WIDTH] = mixed[h * rows : (h + 1) * rows]
        product = jnp.dot(att[spot, :], wo[s], preferred_element_type=jnp.float32)
        part[s, spot, :] = (product + base[s, spot, :].astype(jnp.float32)).astype(jnp.bfloat16)

        @pl.when(middle == 0)
        def _():
            em(i).start()

        for at, c in WO_ATTEND:

            @pl.when(i == at)
            def _():
                wo_pass(c)

        return carry

    def project(j):
        product = jnp.dot(att[...], wo[j], preferred_element_type=jnp.float32)
        part[j] = (product + base[j].astype(jnp.float32)).astype(jnp.bfloat16)

    lax.fori_loop(0, batch, attend, 0)
    wo_own(mate).wait_recv()
    project(mate)
    others = tab.at[0 : roles - 1, 0:rows]
    landed(others, tb_r.at[0])
    sent(others, tb_s.at[0])

    lag, relay_lag = LAGS

    def wo_finish():
        project(side)

        @pl.when(middle == 0)
        def _():
            em(half_steps).start()

        landed(wo.at[far], wm_r.at[1])
        project(far)

    held = steps - lag
    @pl.when(middle == 0)
    def _():
        for k in range(roles, half_steps):
            em(k).start()
        for relay_wo, c in WO_END:
            (wo_turn if relay_wo else wo_pass)(c)
        wo_finish()
        for k in range(half_steps + 1, steps):
            em(k).start()

        def step(k, carry):
            me_in(k).wait_recv()
            spread(k)

            @pl.when(k >= relay_lag)
            def _():
                relay(k - relay_lag)

            return carry

        lax.fori_loop(0, steps - lag, step, 0)

        @pl.when(r > 0)
        def _():
            for k in range(steps - lag - relay_lag, steps - lag - relay_lag + 2):
                relay(k)

    @pl.when(middle == 1)
    def _():
        def step(k):
            if isinstance(k, int):
                pair_up(k)
            else:
                when(k < steps, lambda: pair_up(k))
            when(k >= lag, lambda: complete(k - lag))
            when(k >= lag + relay_lag, lambda: relay(k - lag - relay_lag))

        for k in range(half_steps):
            for relay_wo, c in WO_MIDDLE.get(k, ()):
                (wo_turn if relay_wo else wo_pass)(c)
            step(k)
        wo_finish()

        def late_step(k, carry):
            step(k)
            return carry

        lax.fori_loop(half_steps, steps, late_step, 0)

    for copy in loads[6:]:
        copy.wait()

    expert = s * roles + r
    hidden_width = act.shape[1]
    step_f = hidden_width // 3 if hidden_width % 3 == 0 else hidden_width
    table_lane = lax.broadcasted_iota(jnp.int32, (full, LANES), 1) % half_lanes

    def yc(b, j, path):
        seq = far if path else mate
        return remote(
            y.at[b, j, aligned(seq, rows), :],
            y_core.at[b, j, path],
            yc_s.at[0],
            yc_r.at[b, j * path + seqs * (1 - path)],
            {"seq": mate},
        )

    def yx(b, j):
        return remote(
            y.at[b, j, aligned(side, rows), :],
            y_x.at[b, j],
            yx_s.at[0],
            yx_r.at[b, j],
            {"seq": side},
        )

    def slot(way, b, at):
        own = way * (1 - ((at - b) * way + roles - 2) // (roles - 1))
        return b * (1 - own) + roles * own

    def yz(way, b, j, to):
        place_there = slot(way, b, to)
        return remote(
            y.at[b, j, aligned(s, rows), :],
            y_line.at[place_there, j],
            yz_s.at[0],
            yz_r.at[place_there, j],
            {"role": to},
        )

    def yz_in(way, b, j):
        here = slot(way, b, r)
        landed(y_line.at[here, j], yz_r.at[here, j])
        return y_line[here, j].astype(jnp.float32)

    def pass_core(b, j):
        yc(b, j, 1).wait_recv()
        spot = aligned(side, rows)
        y[b, j, spot, :] = (
            y[b, j, spot, :].astype(jnp.float32) + y_core[b, j, 1].astype(jnp.float32)
        ).astype(jnp.bfloat16)
        yx(b, j).start()

    def summed(b, j):
        if j == 0:
            landed(y_core.at[b, :, 0], yc_r.at[b, seqs])
        yx(b, j).wait_recv()
        return (
            y[b, j, aligned(s, rows), :].astype(jnp.float32)
            + y_core[b, j, 0].astype(jnp.float32)
            + y_x[b, j].astype(jnp.float32)
        )

    def hop(b, j):
        for way in range(2):

            @pl.when(b > r if way == 0 else b < r)
            def _():
                final[...] = summed(b, j)

                @pl.when(r > 0 if way == 0 else r < roles - 1)
                def _():
                    final[...] = final[...] + yz_in(way, b, j)

                y[b, j, aligned(s, rows), :] = final[...].astype(jnp.bfloat16)
                yz(way, b, j, r + 1 - 2 * way).start()

    def relay_first(k):
        @pl.when(r == 0)
        def _():
            relay(k)

    def early_hop(n):
        hop(order(n // seqs), n % seqs)

    def arrive_end(k):
        me_in(k).wait_recv()
        spread(k)

    late_middle = {
        (0, 0): ((complete, 13), (relay, 10)),
        (0, 2): ((complete, 14), (relay, 11)),
        (0, 11): ((complete, 15),),
        (0, 3): ((relay, 12),),
        (1, 2): ((relay, 13),),
        (1, 3): ((relay, 14),),
        (2, 0): ((relay, 15),),
    }
    late_end = {
        (0, 0): ((arrive_end, 13), (relay_first, 10)),
        (0, 2): ((arrive_end, 14), (relay_first, 11)),
        (0, 11): ((arrive_end, 15),),
        (0, 3): ((relay, 12),),
        (0, 4): ((relay, 13),),
        (1, 2): ((relay, 14), (relay, 15)),
        (1, 3): ((early_hop, 0), (early_hop, 1)),
        (2, 0): ((early_hop, 2),),
        (2, 2): ((early_hop, 3),),
        (2, 3): ((early_hop, 4),),
        (3, 0): ((early_hop, 5),),
        (3, 2): ((early_hop, 6),),
        (3, 3): ((early_hop, 7),),
    }

    def late(i, at):
        for here, plan in ((1, late_middle), (0, late_end)):
            for (block, place_in), jobs in plan.items():
                if place_in == at:

                    @pl.when(jnp.logical_and(i == block, middle == here))
                    def _():
                        for job, k in jobs:
                            job(k)

    def one_block(i, carry):
        b = order(i)
        landed(sequence_bytes, tc_r.at[b])
        shares = tab[b].astype(jnp.float32)
        share = jnp.sum(jnp.where(table_lane == expert, shares, 0.0), axis=1, keepdims=True)
        scale = jnp.sum(jnp.where(table_lane == SCALE_LANE, shares, 0.0), axis=1, keepdims=True)
        inputs = jnp.concatenate([tok[b, j] for j in range(seqs)], axis=1)
        for start in range(0, hidden_width, step_f):
            block = pl.ds(start, step_f)
            gate = jnp.dot(inputs, gw[0, :, block], preferred_element_type=jnp.float32) * scale
            up = jnp.dot(inputs, uw[0, :, block], preferred_element_type=jnp.float32) * scale
            act[:, block] = (gate / (1.0 + jnp.exp(-gate)) * up).astype(jnp.bfloat16)
            if start == 0:

                @pl.when(i > 1)
                def _():
                    for j in range(seqs):
                        pass_core(order(i - 1), j)

                late(i, 0)

        late(i, 2)
        for j in range(seqs):
            block = pl.ds(j * cols, cols)
            product = jnp.dot(act[...], dw[0, :, block], preferred_element_type=jnp.float32)
            y[b, j] = (product * share).astype(jnp.bfloat16)
            yc(b, j, 1).start()
            yc(b, j, 0).start()
            if j > 1:

                @pl.when(i == 0)
                def _():
                    pass_core(b, j - 2)

            late(i, 10 + j)
        late(i, 3)

        @pl.when(i == 0)
        def _():
            for j in range(2, seqs):
                pass_core(b, j)

        late(i, 4)
        return carry

    lax.fori_loop(0, roles, one_block, 0)
    for j in range(seqs):
        pass_core(order(roles - 1), j)

    sent(tok.at[0], wm_s.at[1])
    sent(wo.at[0], wm_s.at[0])
    half_wo = wo.at[0, 0 : width // 2]
    sent(half_wo, wx_s.at[0])
    sent(half_wo, wy_s.at[0])
    sent(from_end, tx_s.at[0])
    sent(y_core, tc_s.at[0])
    sent(tab.at[:, 0:rows], tx_s.at[1])
    sent(tab.at[:, 0 : 2 * rows], tc_s.at[1])
    sent(kv.at[:, :, 0 : own_keys * (roles - 1)], kv1_s.at[0])
    sent(kv.at[:, :, 0 : 3 * rows], kv2_s.at[0])

    @pl.when(middle == 0)
    def _():
        sent(from_end, ln_s.at[0])

        for j in range(seqs):
            hop(order(roles - 2), j)

    @pl.when(middle == 1)
    def _():
        sent(from_end, mm_s.at[0])
        sent(from_end, ln_s.at[0])
        for b in ((2 - r) * (roles - 1), (r - 1) * (roles - 1), other):
            for j in range(seqs):
                hop(b, j)

    sent(y_core, yc_s.at[0])
    sent(y_x, yx_s.at[0])
    for j in range(seqs):
        final[...] = summed(r, j) + tok[r, j, aligned(s, rows), :].astype(jnp.float32) * gains[1, j]
        for way in range(2):

            @pl.when(r > 0 if way == 0 else r < roles - 1)
            def _():
                final[...] = final[...] + yz_in(way, r, j)

        out_ref[0, :, j * cols : (j + 1) * cols] = final[...].astype(out_ref.dtype)
    sent(y_x.at[0 : roles - 1], yz_s.at[0])


def fused(
    query_rows,
    encoded_key_rows,
    value_matrix_rows,
    output_weight,
    residual,
    norm_gain,
    route_experts,
    route_gates,
    gate_weight,
    up_weight,
    down_weight,
):
    seqs, roles = lax.axis_size("seq"), lax.axis_size("role")
    batch, rows, width = query_rows.shape
    depth, cols = residual.shape[2], output_weight.shape[1]
    hidden_width = gate_weight.shape[2]
    full = rows * seqs
    bf16, f32 = jnp.bfloat16, jnp.float32
    gain = norm_gain.reshape(1, depth)
    route_experts = route_experts.transpose(0, 2, 1)
    route_gates = route_gates.transpose(0, 2, 1)
    vmem = [
        pltpu.VMEM(query_rows.shape, bf16),
        pltpu.VMEM((2, batch, full, HEAD_WIDTH), bf16),
        pltpu.VMEM((seqs, width, cols), bf16),
        pltpu.VMEM(residual.shape, bf16),
        pltpu.VMEM(gain.shape, f32),
        pltpu.VMEM(route_experts.shape, jnp.int32),
        pltpu.VMEM(route_gates.shape, f32),
        pltpu.VMEM(gate_weight.shape, bf16),
        pltpu.VMEM(up_weight.shape, bf16),
        pltpu.VMEM(down_weight.shape, bf16),
        pltpu.VMEM((batch * rows, width), bf16),
        pltpu.VMEM((2, seqs, 1, cols), f32),
        pltpu.VMEM((seqs, batch * rows, cols), bf16),
        pltpu.VMEM((seqs, batch * rows, cols), bf16),
        pltpu.VMEM((seqs, batch, rows, cols), bf16),
        pltpu.VMEM((seqs, batch, rows, cols), bf16),
        pltpu.VMEM((2 * (full + rows * LANES // cols), cols), bf16),
        pltpu.VMEM((roles, seqs, full, cols), bf16),
        pltpu.VMEM((roles, full, LANES), bf16),
        pltpu.VMEM((full, hidden_width), bf16),
        pltpu.VMEM((roles, seqs, full, cols), bf16),
        pltpu.VMEM((roles, seqs, 2, rows, cols), bf16),
        pltpu.VMEM((roles, seqs, rows, cols), bf16),
        pltpu.VMEM((roles + 1, seqs, rows, cols), bf16),
        pltpu.VMEM((rows, cols), f32),
    ]
    dma = pltpu.SemaphoreType.DMA
    steps = seqs * roles
    chunks = WO_CHUNKS
    counts = [(1,)] * 3 + [(3, batch)] + [(2,)] * 2 + [(1,), (chunks,)] * 2 + [(1,)] * 2
    counts += [(1,), (steps,)] * 2 + [(2,), (seqs, roles), (2,), (roles,)]
    counts += [(1,), (roles, seqs + 1), (1,), (roles, seqs), (1,), (roles + 1, seqs)]
    return pl.pallas_call(
        partial(layer_kernel, roles, seqs),
        out_shape=pltpu.VMEM(residual.shape, bf16),
        in_specs=[pl.BlockSpec(memory_space=pl.ANY)] * 11,
        out_specs=pl.BlockSpec(memory_space=pltpu.VMEM),
        scratch_shapes=vmem + [dma((9,)), dma((2,))] + [dma(count) for count in counts],
        compiler_params=pltpu.CompilerParams(
            collective_id=0, has_side_effects=True, vmem_limit_bytes=60 * 1024 * 1024
        ),
    )(
        query_rows,
        encoded_key_rows,
        value_matrix_rows,
        output_weight,
        residual,
        gain,
        route_experts,
        route_gates,
        gate_weight,
        up_weight,
        down_weight,
    )


def solution(mesh):
    square = mesh.shape["seq"] == 4 and mesh.shape["role"] == 4 and mesh.shape["groups"] == 2
    body = fused if square else shards
    placed = (
        P("groups", "seq", "role"),
        P("groups", ("seq", "role"), None),
        P("groups", ("seq", "role"), None),
        P("role", "seq"),
        P(("groups", "role"), "seq", None),
        P(),
        P(("groups", "role"), "seq", None),
        P(("groups", "role"), "seq", None),
        P(("seq", "role"), None, None),
        P(("seq", "role"), None, None),
        P(("seq", "role"), None, None),
    )
    return jax.shard_map(
        body,
        mesh=mesh,
        in_specs=placed,
        out_specs=P(("groups", "role"), "seq", None),
        check_vma=False,
    )
```

```python
from functools import partial

import jax
import jax.numpy as jnp
from jax import lax
from jax.experimental import pallas as pl
from jax.experimental.pallas import tpu as pltpu
from jax.sharding import PartitionSpec as P

D = 2048
QUERY_HEADS = 32
KEY_VALUE_HEADS = 4
HEAD_WIDTH = 128
TOPK = 8


epsilon = 1e-06
masked_score = -1e30


def score_block(queries, every_key, query_position, block_start, block_width, score_scale):
    keys_part = lax.slice_in_dim(every_key, block_start, block_start + block_width, axis=0)
    raw_scores = (
        jnp.einsum("qhd,kd->hqk", queries, keys_part, preferred_element_type=jnp.float32)
        * score_scale
    )
    key_position = block_start + jnp.arange(block_width, dtype=jnp.int32)
    return jnp.where(
        key_position[None, None, :] <= query_position[None, :, None], raw_scores, masked_score
    )


def value_block(rounded, every_value, block_start, block_width):
    prob_block = lax.slice_in_dim(rounded, block_start, block_start + block_width, axis=2)
    values_part = lax.slice_in_dim(every_value, block_start, block_start + block_width, axis=0)
    return jnp.einsum("hqk,kd->qhd", prob_block, values_part, preferred_element_type=jnp.float32)


def shards(
    query_rows,
    encoded_key_rows,
    value_matrix_rows,
    output_weight,
    residual,
    norm_gain,
    route_experts,
    route_gates,
    gate_weight,
    up_weight,
    down_weight,
):
    seq_count = lax.axis_size("seq")
    role_count = lax.axis_size("role")
    seq_index = lax.axis_index("seq")
    role_index = lax.axis_index("role")
    batch_count = query_rows.shape[0]
    local_length = query_rows.shape[1]
    local_heads = query_rows.shape[2] // HEAD_WIDTH
    full_length = local_length * seq_count
    query_group_width = QUERY_HEADS // KEY_VALUE_HEADS
    head_pick = role_index * local_heads // query_group_width
    role_keys, role_values = (
        lax.all_gather(encoded_key_rows, "role", axis=1, tiled=True),
        lax.all_gather(value_matrix_rows, "role", axis=1, tiled=True),
    )
    head_keys = lax.dynamic_slice_in_dim(role_keys, head_pick * HEAD_WIDTH, HEAD_WIDTH, 2)
    head_values = lax.dynamic_slice_in_dim(role_values, head_pick * HEAD_WIDTH, HEAD_WIDTH, 2)
    whole_keys, whole_values, whole_proj = (
        lax.all_gather(head_keys, "seq", axis=1, tiled=True),
        lax.all_gather(head_values, "seq", axis=1, tiled=True),
        lax.all_gather(output_weight, "seq", axis=1, tiled=True),
    )
    key_width = full_length // 8
    score_scale = HEAD_WIDTH ** (-0.5)
    query_position = seq_index * local_length + jnp.arange(local_length, dtype=jnp.int32)
    last_needed = (seq_index + 1) * local_length

    def one_sequence(operands):
        own_queries, every_key, every_value = operands
        queries = own_queries.reshape(local_length, local_heads, HEAD_WIDTH)
        pieces = []
        for number in range(8):
            block_start = number * key_width
            compute = partial(
                score_block, queries, every_key, query_position, block_start, key_width, score_scale
            )
            skipped = partial(
                jnp.full, (local_heads, local_length, key_width), masked_score, jnp.float32
            )
            pieces.append(lax.cond(block_start < last_needed, compute, skipped))
        scores = jnp.concatenate(pieces, axis=2)
        row_peak = jnp.max(scores, axis=2, keepdims=True)
        weights = jnp.exp(scores - row_peak)
        totals = jnp.sum(weights, axis=2, keepdims=True)
        rounded = weights.astype(jnp.bfloat16)
        mixed_rows = jnp.zeros((local_length, local_heads, HEAD_WIDTH), jnp.float32)
        for number in range(8):
            block_start = number * key_width
            product = partial(value_block, rounded, every_value, block_start, key_width)
            nothing = partial(jnp.zeros, (local_length, local_heads, HEAD_WIDTH), jnp.float32)
            mixed_rows = mixed_rows + lax.cond(block_start < last_needed, product, nothing)
        attended = (mixed_rows / totals.transpose(1, 0, 2)).astype(jnp.bfloat16)
        return attended.reshape(local_length, local_heads * HEAD_WIDTH)

    attended = lax.map(one_sequence, (query_rows, whole_keys, whole_values))
    flat_attended = attended.reshape(batch_count * local_length, local_heads * HEAD_WIDTH)
    projected = lax.psum_scatter(
        jnp.dot(flat_attended, whole_proj, preferred_element_type=jnp.float32).astype(jnp.bfloat16),
        "role",
        scatter_dimension=0,
        tiled=True,
    ).astype(jnp.float32)
    hidden = residual[0].astype(jnp.float32) + projected
    variance = jnp.mean(hidden * hidden, axis=-1, keepdims=True)
    normed = (hidden * lax.rsqrt(variance + epsilon) * norm_gain).astype(jnp.bfloat16)
    expert_ids = route_experts.reshape(-1)
    gate_values = route_gates.reshape(-1)
    experts_local = gate_weight.shape[0]
    device_count = seq_count * role_count
    expert_count = experts_local * device_count
    assign = expert_ids.shape[0]
    capacity = assign // expert_count + 1
    onehot = (expert_ids[:, None] == jnp.arange(expert_count, dtype=jnp.int32)[None, :]).astype(
        jnp.int32
    )
    before = jnp.tri(assign, k=-1, dtype=jnp.bfloat16)
    earlier = jnp.dot(
        before, onehot.astype(jnp.bfloat16), preferred_element_type=jnp.float32
    ).astype(jnp.int32)
    slot_rank = jnp.sum(earlier * onehot, axis=1)
    slot_index = expert_ids * capacity + slot_rank
    source_token = jnp.arange(assign, dtype=jnp.int32) // TOPK
    slot_token = jnp.zeros((expert_count * capacity,), jnp.int32).at[slot_index].set(source_token)
    slot_used = jnp.zeros((expert_count * capacity,), jnp.bfloat16).at[slot_index].set(1.0)
    outgoing = (normed[slot_token] * slot_used[:, None]).reshape(
        device_count, experts_local, capacity, D
    )
    incoming = lax.all_to_all(outgoing, ("seq", "role"), split_axis=0, concat_axis=0, tiled=True)
    gate_hidden = jnp.einsum(
        "sjcd,jdf->sjcf", incoming, gate_weight, preferred_element_type=jnp.float32
    )
    up_hidden = jnp.einsum(
        "sjcd,jdf->sjcf", incoming, up_weight, preferred_element_type=jnp.float32
    )
    activated = (jax.nn.silu(gate_hidden) * up_hidden).astype(jnp.bfloat16)
    returned = lax.all_to_all(
        jnp.einsum(
            "sjcf,jfd->sjcd", activated, down_weight, preferred_element_type=jnp.float32
        ).astype(jnp.bfloat16),
        ("seq", "role"),
        split_axis=0,
        concat_axis=0,
        tiled=True,
    )
    gathered = returned.reshape(expert_count * capacity, D)[slot_index]
    weighted = gathered.astype(jnp.float32) * gate_values[:, None]
    expert_sum = jnp.sum(weighted.reshape(-1, TOPK, D), axis=1)
    return (hidden + expert_sum).astype(jnp.bfloat16).reshape(residual.shape)


MESH = pl.DeviceIdType.MESH
LANES = 128
LAGS = (3, 3)
WO_CHUNKS = 8
WO_FIRST = 4
WO_ATTEND = ((2, 4),)
WO_END = ((1, 0), (1, 1), (1, 2), (0, 5), (0, 6), (1, 3), (0, 7), (1, 4), (1, 5), (1, 6), (1, 7))
WO_MIDDLE = {
    0: ((1, 0), (1, 1), (1, 2), (0, 5)),
    1: ((0, 6), (1, 3)),
    2: ((0, 7), (1, 4)),
    3: ((1, 5),),
    4: ((1, 6),),
    5: ((1, 7),),
}


def aligned(index, size):
    return pl.ds(pl.multiple_of(index * size, size), size)


SCALE_LANE = 32


def layer_kernel(
    roles,
    seqs,
    q_hbm,
    k_hbm,
    v_hbm,
    wo_hbm,
    res_hbm,
    gain_hbm,
    ids_hbm,
    gates_hbm,
    gw_hbm,
    uw_hbm,
    dw_hbm,
    out_ref,
    q,
    kv,
    wo,
    res,
    gain,
    ids,
    gates,
    gw,
    uw,
    dw,
    att,
    gains,
    base,
    part,
    from_end,
    from_mid,
    from_mate,
    tok,
    tab,
    act,
    y,
    y_core,
    y_x,
    y_line,
    final,
    load_sem,
    own_sem,
    kv1_s,
    kv1_r,
    kv2_s,
    kv2_r,
    wm_s,
    wm_r,
    wx_s,
    wx_r,
    wy_s,
    wy_r,
    tb_s,
    tb_r,
    ln_s,
    ln_r,
    mm_s,
    mm_r,
    tx_s,
    tx_r,
    tc_s,
    tc_r,
    yc_s,
    yc_r,
    yx_s,
    yx_r,
    yz_s,
    yz_r,
):
    s = lax.axis_index("seq")
    r = lax.axis_index("role")
    g = lax.axis_index("groups")
    mate = s + 1 - 2 * (s % 2)
    side = (s + 2) % 4
    far = mate + 2 - 4 * (mate // 2)
    batch, rows, width = q.shape
    heads = width // HEAD_WIDTH
    own_keys = k_hbm.shape[1]
    full = rows * seqs
    cols = wo.shape[2]
    depth = cols * seqs
    offs = (1, 2, 3)
    chunks = WO_CHUNKS
    chunk_rows = width // (2 * chunks)
    middle = (r + 1) // 2 % 2
    inner = r + 1 - 2 * (r // 2)
    outer = r - 1 + 2 * (r // 2)
    other = 3 - r

    def role_of(i):
        return (r // 2 + i // 2) % 2 * 2 + (r + i) % 2

    def turn(i):
        return (i + roles - 1) % roles

    def order(i):
        swap = (1 - r // (roles - 1)) * (1 - (i % 3 + 1) // 2)
        return middle * turn(i) + (1 - middle) * (i + swap * (3 - 2 * i))

    def column(n):
        return (s // 2 + n // 2) % 2 * 2 + (s + n) % 2

    def remote(src, dst, ssem, rsem, device):
        return pltpu.make_async_remote_copy(
            src_ref=src,
            dst_ref=dst,
            send_sem=ssem,
            recv_sem=rsem,
            device_id=device,
            device_id_type=MESH,
        )

    def to_role(off):
        return {"role": role_of(off)}

    barrier = pltpu.get_barrier_semaphore()
    for off in offs:
        pl.semaphore_signal(barrier, inc=1, device_id=to_role(off), device_id_type=MESH)
    for peer in ({"seq": mate}, {"seq": side}, {"groups": 1 - g}):
        pl.semaphore_signal(barrier, inc=1, device_id=peer, device_id_type=MESH)

    loads = [
        pltpu.make_async_copy(a, b, load_sem.at[i])
        for i, (a, b) in enumerate(
            (
                (q_hbm, q),
                (res_hbm, res),
                (gain_hbm, gain),
                (ids_hbm, ids),
                (gates_hbm, gates),
                (wo_hbm, wo.at[s]),
                (gw_hbm, gw),
                (uw_hbm, uw),
                (dw_hbm, dw),
            )
        )
    ]
    pair = (k_hbm, v_hbm)

    def kv_spot(t, seq, role):
        return kv.at[t, :, aligned(seq * roles + role, own_keys), :]

    owns = [
        pltpu.make_async_copy(
            pair[t].at[:, :, aligned(r, HEAD_WIDTH)], kv_spot(t, s, r), own_sem.at[t]
        )
        for t in range(2)
    ]
    for copy in owns + loads[:6]:
        copy.start()

    for copy in loads[1:5]:
        copy.wait()
    half_lanes = LANES // 2
    place = lax.broadcasted_iota(jnp.int32, (LANES, rows), 0)
    table = jnp.zeros((LANES, rows), jnp.float32)
    for k in range(ids.shape[1]):
        chosen = place % half_lanes == ids[0, k : k + 1, :]
        table = table + jnp.where(chosen, gates[0, k : k + 1, :], 0.0)
    high = table.astype(jnp.bfloat16).astype(jnp.float32)
    parts = jnp.where(place < half_lanes, high, table - high).astype(jnp.bfloat16)
    unit = (
        lax.broadcasted_iota(jnp.int32, (rows, rows), 0)
        == lax.broadcasted_iota(jnp.int32, (rows, rows), 1)
    )
    tab[r, aligned(s, rows), :] = lax.dot_general(
        jnp.where(unit, 1.0, 0.0).astype(jnp.bfloat16),
        parts,
        (((1,), (1,)), ((), ())),
        preferred_element_type=jnp.float32,
    ).astype(jnp.bfloat16)
    base[...] = jnp.zeros_like(base)
    for j in range(seqs):
        block = pl.ds(j * cols, cols)
        gains[0, j] = gain[:, block]
        gains[1, j] = 1.0 / gain[:, block]
        base[j, aligned(r, rows), :] = res[0, :, block]

    pl.semaphore_wait(barrier, roles - 1 + 3)

    def kv1(t, off):
        return remote(
            pair[t].at[:, :, aligned(role_of(off), HEAD_WIDTH)],
            kv_spot(t, s, r),
            kv1_s.at[0],
            kv1_r.at[0],
            to_role(off),
        )

    def tb(off):
        spot = tab.at[r, aligned(s, rows), :]
        return remote(spot, spot, tb_s.at[0], tb_r.at[0], to_role(off))

    def sent(ref, sem):
        remote(ref, ref, sem, sem, {"seq": mate}).wait_send()

    def landed(ref, sem):
        remote(ref, ref, sem, sem, {"seq": mate}).wait_recv()

    for off in offs:
        for t in range(2):
            kv1(t, off).start()

    def kv2(path, seq, target, b):
        spot = kv.at[:, b, aligned(seq, rows), :]
        return remote(spot, spot, kv2_s.at[0], kv2_r.at[path, b], {"seq": target})

    def wo_part(seq, n):
        return wo.at[seq, aligned(n, chunk_rows), :]

    def wo_own(seq):
        return remote(wo.at[seq], wo.at[seq], wm_s.at[0], wm_r.at[0], {"seq": mate})

    def wo_x(seq, c):
        spot = wo_part(seq, g * chunks + c)
        return remote(spot, spot, wx_s.at[0], wx_r.at[c], {"seq": side})

    def wo_y(half, c):
        spot = wo_part(side, half * chunks + c)
        return remote(spot, spot, wy_s.at[0], wy_r.at[c], {"groups": 1 - g})

    def wo_mate(seq, half, c):
        spot = wo_part(seq, half * chunks + c)
        return remote(spot, spot, wm_s.at[1], wm_r.at[1], {"seq": mate})

    def wo_pass(c):
        wo_x(side, c).wait_recv()
        wo_y(g, c).start()
        wo_mate(side, g, c).start()

    def wo_turn(c):
        wo_y(1 - g, c).wait_recv()
        wo_mate(side, 1 - g, c).start()

    loads[5].wait()
    for c in range(WO_FIRST):
        wo_x(s, c).start()
    wo_own(s).start()
    for off in offs:
        tb(off).start()
    for copy in owns:
        copy.wait()
    landed(kv.at[:, :, 0 : own_keys * (roles - 1)], kv1_r.at[0])
    for path, target in ((1, side), (0, mate)):
        for i in range(batch):
            kv2(path, s, target, turn(i)).start()
    for c in range(WO_FIRST, chunks):
        wo_x(s, c).start()
    loads[0].wait()
    for c in range(WO_FIRST):
        wo_pass(c)

    def kv_relay(i):
        kv2(1, side, side, turn(i)).wait_recv()
        kv2(2, side, mate, turn(i)).start()

    kv_relay(0)

    half_steps = 2 * roles
    steps = 2 * half_steps

    def spot_of(k):
        late = k // half_steps
        m = k % half_steps
        early_col, early_turn = m // roles, m % roles
        late_col, late_turn = 2 + m % 2, m // 2
        n = (1 - late) * early_col + late * late_col
        return column(n), turn((1 - late) * early_turn + late * late_turn)

    def part_of(k):
        j, b = spot_of(k)
        return part.at[j, aligned(b, rows), :]

    def em(k):
        j, b = spot_of(k)
        return remote(part_of(k), from_end.at[j, b], ln_s.at[0], ln_r.at[k], {"role": inner})

    def em_in(k):
        j, b = spot_of(k)
        return remote(part_of(k), from_end.at[j, b], ln_s.at[0], ln_r.at[k], {"role": outer})

    def mm(k):
        j, b = spot_of(k)
        return remote(part_of(k), from_mid.at[j, b], mm_s.at[0], mm_r.at[k], {"role": other})

    def piece(j, b, seq):
        return tok.at[b, j, aligned(seq, rows), :]

    def me(k):
        j, b = spot_of(k)
        return remote(piece(j, b, s), piece(j, b, s), ln_s.at[0], ln_r.at[k], {"role": outer})

    def me_in(k):
        j, b = spot_of(k)
        return remote(piece(j, b, s), piece(j, b, s), ln_s.at[0], ln_r.at[k], {"role": inner})

    def table_of(b, seq):
        return tab.at[b, aligned(seq, rows), :]

    def tx(j, b, seq):
        return remote(
            piece(j, b, seq), piece(j, b, seq), tx_s.at[0], tx_r.at[j, b], {"seq": side}
        )

    def tx_table(j, b, seq):
        spot = table_of(b, seq)
        return remote(spot, spot, tx_s.at[1], tx_r.at[j, b], {"seq": side})

    def tc(j, b, seq):
        spot = piece(j, b, seq)
        return remote(spot, spot, tc_s.at[0], tc_r.at[b], {"seq": mate})

    def tc_table(b, seq):
        spot = table_of(b, seq)
        return remote(spot, spot, tc_s.at[1], tc_r.at[b], {"seq": mate})

    table_rows = rows * LANES // cols
    with_table_bytes = from_mate.at[0 : rows + table_rows]
    sequence_bytes = from_mate.at[...]

    def when(condition, body):
        if isinstance(condition, bool):
            if condition:
                body()
        else:
            pl.when(condition)(body)

    def is_last(k):
        if isinstance(k, int):
            return k >= half_steps and k % 2 == 1
        return jnp.logical_and(k >= half_steps, k % 2 == 1)

    lane = lax.broadcasted_iota(jnp.int32, (rows, LANES), 1)

    def spread(k):
        j, b = spot_of(k)
        tx(j, b, s).start()
        tc(j, b, s).start()

        def with_table():
            square = jnp.zeros((rows, 1), jnp.float32)
            for c in range(seqs):
                value = tok[b, c, aligned(s, rows), :].astype(jnp.float32) * gains[1, c]
                square = square + jnp.sum(value * value, axis=1, keepdims=True)
            scale = lax.rsqrt(square / depth + epsilon)
            top = scale.astype(jnp.bfloat16).astype(jnp.float32)
            old = tab[b, aligned(s, rows), :].astype(jnp.float32)
            fresh = jnp.where(
                lane == SCALE_LANE,
                top,
                jnp.where(lane == SCALE_LANE + half_lanes, scale - top, old),
            )
            tab[b, aligned(s, rows), :] = fresh.astype(jnp.bfloat16)
            tx_table(j, b, s).start()
            tc_table(b, s).start()

        when(is_last(k), with_table)

    def relay(k):
        j, b = column_from(side, k), spot_of(k)[1]

        def plain():
            tx(j, b, side).wait_recv()
            tc(j, b, side).start()

        def with_table():
            landed(with_table_bytes, tx_r.at[j, b])
            tc(j, b, side).start()
            tc_table(b, side).start()

        if isinstance(k, int):
            (with_table if is_last(k) else plain)()
        else:
            pl.when(is_last(k))(with_table)
            pl.when(jnp.logical_not(is_last(k)))(plain)

    def column_from(seq, k):
        late = k // half_steps
        m = k % half_steps
        n = (1 - late) * (m // roles) + late * (2 + m % 2)
        return (seq // 2 + n // 2) % 2 * 2 + (seq + n) % 2

    def pair_up(k):
        em_in(k).wait_recv()
        j, b = spot_of(k)
        spot = aligned(b, rows)
        part[j, spot, :] = (
            part[j, spot, :].astype(jnp.float32) + from_end[j, b].astype(jnp.float32)
        ).astype(jnp.bfloat16)
        mm(k).start()

    def complete(k):
        mm(k).wait_recv()
        j, b = spot_of(k)
        total = part[j, aligned(b, rows), :].astype(jnp.float32) + from_mid[j, b].astype(
            jnp.float32
        )
        tok[b, j, aligned(s, rows), :] = (total * gains[0, j]).astype(jnp.bfloat16)
        me(k).start()
        spread(k)

    query_row = s * rows + lax.broadcasted_iota(jnp.int32, (rows, full), 0)
    allowed = lax.broadcasted_iota(jnp.int32, (rows, full), 1) <= query_row
    allowed = jnp.concatenate([allowed] * heads, axis=0)

    def attend(i, carry):
        b = turn(i)

        @pl.when(i < batch - 1)
        def _():
            kv_relay(i + 1)

        kv2(0, mate, mate, b).wait_recv()
        kv2(2, far, mate, b).wait_recv()
        stacked = jnp.concatenate(
            [q[b, :, h * HEAD_WIDTH : (h + 1) * HEAD_WIDTH] for h in range(heads)], axis=0
        )
        scores = lax.dot_general(
            stacked, kv[0, b], (((1,), (1,)), ((), ())), preferred_element_type=jnp.float32
        ) * (HEAD_WIDTH**-0.5)
        scores = jnp.where(allowed, scores, masked_score)
        weights = jnp.exp(scores - jnp.max(scores, axis=1, keepdims=True))
        totals = jnp.sum(weights, axis=1, keepdims=True)
        mixed = jnp.dot(
            weights.astype(jnp.bfloat16), kv[1, b], preferred_element_type=jnp.float32
        )
        mixed = (mixed / totals).astype(jnp.bfloat16)
        spot = aligned(b, rows)
        for h in range(heads):
            att[spot, h * HEAD_WIDTH : (h + 1) * HEAD_WIDTH] = mixed[h * rows : (h + 1) * rows]
        product = jnp.dot(att[spot, :], wo[s], preferred_element_type=jnp.float32)
        part[s, spot, :] = (product + base[s, spot, :].astype(jnp.float32)).astype(jnp.bfloat16)

        @pl.when(middle == 0)
        def _():
            em(i).start()

        for at, c in WO_ATTEND:

            @pl.when(i == at)
            def _():
                wo_pass(c)

        return carry

    def project(j):
        product = jnp.dot(att[...], wo[j], preferred_element_type=jnp.float32)
        part[j] = (product + base[j].astype(jnp.float32)).astype(jnp.bfloat16)

    lax.fori_loop(0, batch, attend, 0)
    for copy in loads[6:]:
        copy.start()
    wo_own(mate).wait_recv()
    project(mate)
    others = tab.at[0 : roles - 1, 0:rows]
    landed(others, tb_r.at[0])
    sent(others, tb_s.at[0])

    lag, relay_lag = LAGS

    def wo_finish():
        project(side)

        @pl.when(middle == 0)
        def _():
            em(half_steps).start()

        landed(wo.at[far], wm_r.at[1])
        project(far)

    held = steps - lag
    @pl.when(middle == 0)
    def _():
        for k in range(roles, half_steps):
            em(k).start()
        for relay_wo, c in WO_END:
            (wo_turn if relay_wo else wo_pass)(c)
        wo_finish()
        for k in range(half_steps + 1, steps):
            em(k).start()

        def step(k, carry):
            me_in(k).wait_recv()
            spread(k)

            @pl.when(k >= relay_lag)
            def _():
                relay(k - relay_lag)

            return carry

        lax.fori_loop(0, steps - lag, step, 0)

        @pl.when(r > 0)
        def _():
            for k in range(steps - lag - relay_lag, steps - lag - relay_lag + 2):
                relay(k)

    @pl.when(middle == 1)
    def _():
        def step(k):
            if isinstance(k, int):
                pair_up(k)
            else:
                when(k < steps, lambda: pair_up(k))
            when(k >= lag, lambda: complete(k - lag))
            when(k >= lag + relay_lag, lambda: relay(k - lag - relay_lag))

        for k in range(half_steps):
            for relay_wo, c in WO_MIDDLE.get(k, ()):
                (wo_turn if relay_wo else wo_pass)(c)
            step(k)
        wo_finish()

        def late_step(k, carry):
            step(k)
            return carry

        lax.fori_loop(half_steps, steps, late_step, 0)

    for copy in loads[6:]:
        copy.wait()

    expert = s * roles + r
    hidden_width = act.shape[1]
    step_f = hidden_width // 3 if hidden_width % 3 == 0 else hidden_width
    table_lane = lax.broadcasted_iota(jnp.int32, (full, LANES), 1) % half_lanes

    def yc(b, j, path):
        seq = far if path else mate
        return remote(
            y.at[b, j, aligned(seq, rows), :],
            y_core.at[b, j, path],
            yc_s.at[0],
            yc_r.at[b, j * path + seqs * (1 - path)],
            {"seq": mate},
        )

    def yx(b, j):
        return remote(
            y.at[b, j, aligned(side, rows), :],
            y_x.at[b, j],
            yx_s.at[0],
            yx_r.at[b, j],
            {"seq": side},
        )

    def slot(way, b, at):
        own = way * (1 - ((at - b) * way + roles - 2) // (roles - 1))
        return b * (1 - own) + roles * own

    def yz(way, b, j, to):
        place_there = slot(way, b, to)
        return remote(
            y.at[b, j, aligned(s, rows), :],
            y_line.at[place_there, j],
            yz_s.at[0],
            yz_r.at[place_there, j],
            {"role": to},
        )

    def yz_in(way, b, j):
        here = slot(way, b, r)
        landed(y_line.at[here, j], yz_r.at[here, j])
        return y_line[here, j].astype(jnp.float32)

    def pass_core(b, j):
        yc(b, j, 1).wait_recv()
        spot = aligned(side, rows)
        y[b, j, spot, :] = (
            y[b, j, spot, :].astype(jnp.float32) + y_core[b, j, 1].astype(jnp.float32)
        ).astype(jnp.bfloat16)
        yx(b, j).start()

    def summed(b, j):
        if j == 0:
            landed(y_core.at[b, :, 0], yc_r.at[b, seqs])
        yx(b, j).wait_recv()
        return (
            y[b, j, aligned(s, rows), :].astype(jnp.float32)
            + y_core[b, j, 0].astype(jnp.float32)
            + y_x[b, j].astype(jnp.float32)
        )

    def hop(b, j):
        for way in range(2):

            @pl.when(b > r if way == 0 else b < r)
            def _():
                final[...] = summed(b, j)

                @pl.when(r > 0 if way == 0 else r < roles - 1)
                def _():
                    final[...] = final[...] + yz_in(way, b, j)

                y[b, j, aligned(s, rows), :] = final[...].astype(jnp.bfloat16)
                yz(way, b, j, r + 1 - 2 * way).start()

    def relay_first(k):
        @pl.when(r == 0)
        def _():
            relay(k)

    def early_hop(n):
        hop(order(n // seqs), n % seqs)

    def arrive_end(k):
        me_in(k).wait_recv()
        spread(k)

    late_middle = {
        (0, 0): ((complete, 13), (relay, 10)),
        (0, 2): ((complete, 14), (relay, 11)),
        (0, 11): ((complete, 15),),
        (0, 3): ((relay, 12),),
        (1, 2): ((relay, 13),),
        (1, 3): ((relay, 14),),
        (2, 0): ((relay, 15),),
    }
    late_end = {
        (0, 0): ((arrive_end, 13), (relay_first, 10)),
        (0, 2): ((arrive_end, 14), (relay_first, 11)),
        (0, 11): ((arrive_end, 15),),
        (0, 3): ((relay, 12),),
        (0, 4): ((relay, 13),),
        (1, 2): ((relay, 14), (relay, 15)),
        (1, 3): ((early_hop, 0),),
        (2, 0): ((early_hop, 1),),
        (2, 2): ((early_hop, 2),),
        (2, 3): ((early_hop, 3),),
        (3, 0): ((early_hop, 4),),
        (3, 2): ((early_hop, 5),),
        (3, 3): ((early_hop, 6), (early_hop, 7),),
    }

    def late(i, at):
        for here, plan in ((1, late_middle), (0, late_end)):
            for (block, place_in), jobs in plan.items():
                if place_in == at:

                    @pl.when(jnp.logical_and(i == block, middle == here))
                    def _():
                        for job, k in jobs:
                            job(k)

    def one_block(i, carry):
        b = order(i)
        landed(sequence_bytes, tc_r.at[b])
        shares = tab[b].astype(jnp.float32)
        share = jnp.sum(jnp.where(table_lane == expert, shares, 0.0), axis=1, keepdims=True)
        scale = jnp.sum(jnp.where(table_lane == SCALE_LANE, shares, 0.0), axis=1, keepdims=True)
        inputs = jnp.concatenate([tok[b, j] for j in range(seqs)], axis=1)
        for start in range(0, hidden_width, step_f):
            block = pl.ds(start, step_f)
            gate = jnp.dot(inputs, gw[0, :, block], preferred_element_type=jnp.float32) * scale
            up = jnp.dot(inputs, uw[0, :, block], preferred_element_type=jnp.float32) * scale
            act[:, block] = (gate / (1.0 + jnp.exp(-gate)) * up).astype(jnp.bfloat16)
            if start == 0:

                @pl.when(i > 1)
                def _():
                    for j in range(seqs):
                        pass_core(order(i - 1), j)

                late(i, 0)

        late(i, 2)
        for j in range(seqs):
            block = pl.ds(j * cols, cols)
            product = jnp.dot(act[...], dw[0, :, block], preferred_element_type=jnp.float32)
            y[b, j] = (product * share).astype(jnp.bfloat16)
            yc(b, j, 1).start()
            yc(b, j, 0).start()
            if j > 1:

                @pl.when(i == 0)
                def _():
                    pass_core(b, j - 2)

            late(i, 10 + j)
        late(i, 3)

        @pl.when(i == 0)
        def _():
            for j in range(2, seqs):
                pass_core(b, j)

        late(i, 4)
        return carry

    lax.fori_loop(0, roles, one_block, 0)
    for j in range(seqs):
        pass_core(order(roles - 1), j)

    sent(tok.at[0], wm_s.at[1])
    sent(wo.at[0], wm_s.at[0])
    half_wo = wo.at[0, 0 : width // 2]
    sent(half_wo, wx_s.at[0])
    sent(half_wo, wy_s.at[0])
    sent(from_end, tx_s.at[0])
    sent(y_core, tc_s.at[0])
    sent(tab.at[:, 0:rows], tx_s.at[1])
    sent(tab.at[:, 0 : 2 * rows], tc_s.at[1])
    sent(kv.at[:, :, 0 : own_keys * (roles - 1)], kv1_s.at[0])
    sent(kv.at[:, :, 0 : 3 * rows], kv2_s.at[0])

    @pl.when(middle == 0)
    def _():
        sent(from_end, ln_s.at[0])

        for j in range(seqs):
            hop(order(roles - 2), j)

    @pl.when(middle == 1)
    def _():
        sent(from_end, mm_s.at[0])
        sent(from_end, ln_s.at[0])
        for b in ((2 - r) * (roles - 1), (r - 1) * (roles - 1), other):
            for j in range(seqs):
                hop(b, j)

    sent(y_core, yc_s.at[0])
    sent(y_x, yx_s.at[0])
    for j in range(seqs):
        final[...] = summed(r, j) + tok[r, j, aligned(s, rows), :].astype(jnp.float32) * gains[1, j]
        for way in range(2):

            @pl.when(r > 0 if way == 0 else r < roles - 1)
            def _():
                final[...] = final[...] + yz_in(way, r, j)

        out_ref[0, :, j * cols : (j + 1) * cols] = final[...].astype(out_ref.dtype)
    sent(y_x.at[0 : roles - 1], yz_s.at[0])


def fused(
    query_rows,
    encoded_key_rows,
    value_matrix_rows,
    output_weight,
    residual,
    norm_gain,
    route_experts,
    route_gates,
    gate_weight,
    up_weight,
    down_weight,
):
    seqs, roles = lax.axis_size("seq"), lax.axis_size("role")
    batch, rows, width = query_rows.shape
    depth, cols = residual.shape[2], output_weight.shape[1]
    hidden_width = gate_weight.shape[2]
    full = rows * seqs
    bf16, f32 = jnp.bfloat16, jnp.float32
    gain = norm_gain.reshape(1, depth)
    route_experts = route_experts.transpose(0, 2, 1)
    route_gates = route_gates.transpose(0, 2, 1)
    vmem = [
        pltpu.VMEM(query_rows.shape, bf16),
        pltpu.VMEM((2, batch, full, HEAD_WIDTH), bf16),
        pltpu.VMEM((seqs, width, cols), bf16),
        pltpu.VMEM(residual.shape, bf16),
        pltpu.VMEM(gain.shape, f32),
        pltpu.VMEM(route_experts.shape, jnp.int32),
        pltpu.VMEM(route_gates.shape, f32),
        pltpu.VMEM(gate_weight.shape, bf16),
        pltpu.VMEM(up_weight.shape, bf16),
        pltpu.VMEM(down_weight.shape, bf16),
        pltpu.VMEM((batch * rows, width), bf16),
        pltpu.VMEM((2, seqs, 1, cols), f32),
        pltpu.VMEM((seqs, batch * rows, cols), bf16),
        pltpu.VMEM((seqs, batch * rows, cols), bf16),
        pltpu.VMEM((seqs, batch, rows, cols), bf16),
        pltpu.VMEM((seqs, batch, rows, cols), bf16),
        pltpu.VMEM((2 * (full + rows * LANES // cols), cols), bf16),
        pltpu.VMEM((roles, seqs, full, cols), bf16),
        pltpu.VMEM((roles, full, LANES), bf16),
        pltpu.VMEM((full, hidden_width), bf16),
        pltpu.VMEM((roles, seqs, full, cols), bf16),
        pltpu.VMEM((roles, seqs, 2, rows, cols), bf16),
        pltpu.VMEM((roles, seqs, rows, cols), bf16),
        pltpu.VMEM((roles + 1, seqs, rows, cols), bf16),
        pltpu.VMEM((rows, cols), f32),
    ]
    dma = pltpu.SemaphoreType.DMA
    steps = seqs * roles
    chunks = WO_CHUNKS
    counts = [(1,)] * 3 + [(3, batch)] + [(2,)] * 2 + [(1,), (chunks,)] * 2 + [(1,)] * 2
    counts += [(1,), (steps,)] * 2 + [(2,), (seqs, roles), (2,), (roles,)]
    counts += [(1,), (roles, seqs + 1), (1,), (roles, seqs), (1,), (roles + 1, seqs)]
    return pl.pallas_call(
        partial(layer_kernel, roles, seqs),
        out_shape=pltpu.VMEM(residual.shape, bf16),
        in_specs=[pl.BlockSpec(memory_space=pl.ANY)] * 11,
        out_specs=pl.BlockSpec(memory_space=pltpu.VMEM),
        scratch_shapes=vmem + [dma((9,)), dma((2,))] + [dma(count) for count in counts],
        compiler_params=pltpu.CompilerParams(
            collective_id=0, has_side_effects=True, vmem_limit_bytes=60 * 1024 * 1024
        ),
    )(
        query_rows,
        encoded_key_rows,
        value_matrix_rows,
        output_weight,
        residual,
        gain,
        route_experts,
        route_gates,
        gate_weight,
        up_weight,
        down_weight,
    )


def solution(mesh):
    square = mesh.shape["seq"] == 4 and mesh.shape["role"] == 4 and mesh.shape["groups"] == 2
    body = fused if square else shards
    placed = (
        P("groups", "seq", "role"),
        P("groups", ("seq", "role"), None),
        P("groups", ("seq", "role"), None),
        P("role", "seq"),
        P(("groups", "role"), "seq", None),
        P(),
        P(("groups", "role"), "seq", None),
        P(("groups", "role"), "seq", None),
        P(("seq", "role"), None, None),
        P(("seq", "role"), None, None),
        P(("seq", "role"), None, None),
    )
    return jax.shard_map(
        body,
        mesh=mesh,
        in_specs=placed,
        out_specs=P(("groups", "role"), "seq", None),
        check_vma=False,
    )
```
